32 devices in a mesh: dp: 16 (over z, y, core), tensor: 2 (over x).
Axes of the slice: x: 2, y: 2, z: 4, core: 2. Of those that a mesh axis runs over, the one named last changes fastest.
Arguments:
- tokens: bfloat16 [32768, 768], P('dp'), may hold values from -6 to 6
- qkv_weight: bfloat16 [768, 3, 768], P(None, None, 'tensor'), may hold values from -0.21875 to 0.21875
- qv_bias: float32 [2, 768], P(None, 'tensor'), may hold values from -1.5 to 1.5
- proj_weight: bfloat16 [768, 768], P('tensor'), may hold values from -1.75 to 1.75
- proj_bias: float32 [768], replicated, may hold values from -1.5 to 1.5
- first_gain: float32 [768], replicated, may hold values from 0.5 to 1.5
- first_shift: float32 [768], replicated, may hold values from -1.5 to 1.5
- up_weight: bfloat16 [768, 3072], P(None, 'tensor'), may hold values from -0.21875 to 0.21875
- up_bias: float32 [3072], P('tensor'), may hold values from -1.5 to 1.5
- down_weight: bfloat16 [3072, 768], P('tensor'), may hold values from -0.109375 to 0.109375
- down_bias: float32 [768], replicated, may hold values from -1.5 to 1.5
- second_gain: float32 [768], replicated, may hold values from 0.5 to 1.5
- second_shift: float32 [768], replicated, may hold values from -1.5 to 1.5
- cotangent: bfloat16 [32768, 768], P('dp'), may hold values from -6 to 6
- bucket: int32 [16], P('dp'), may hold values from 0 to 1, as said below
- lengths: int32 [256], P('dp'), may hold values from 0 to 512, as said below
- dropped: int32 [256], P('dp'), may hold values 0 or 1
Outputs:
- result: bfloat16 [32768, 768], P('dp')
- tokens_grad: float32 [32768, 768], P('dp')
- qkv_weight_grad: float32 [768, 3, 768], P(None, None, 'tensor')
- qv_bias_grad: float32 [2, 768], P(None, 'tensor')
- proj_weight_grad: float32 [768, 768], P('tensor')
- proj_bias_grad: float32 [768], replicated
- first_gain_grad: float32 [768], replicated
- first_shift_grad: float32 [768], replicated
- up_weight_grad: float32 [768, 3072], P(None, 'tensor')
- up_bias_grad: float32 [3072], P('tensor')
- down_weight_grad: float32 [3072, 768], P('tensor')
- down_bias_grad: float32 [768], replicated
- second_gain_grad: float32 [768], replicated
- second_shift_grad: float32 [768], replicated
The draws below stay inside these ranges and needn't reach their ends.
Inputs may be any that keep to these rules, and one draw needn't show every extreme that they name: Exactly a third of the token blocks, rounded down, have bucket 1. Slot k of block r (lengths[r * 16 + k]): in a block of bucket 1 every slot holds 32 to 128; in a block of bucket 0 slots k < 4 hold 128 to 512 and the other slots 0; in every block one used slot holds its whole span.
All inputs are finite; a program needn't handle non-finite values. No bound on the sum of `dropped` on one device may be relied on, other than what follows from the above.
Results may differ from the reference program's by a relative error of at most 0.015.
The reference program's roundings to bfloat16 on the way count: a program that leaves them out, or rounds other values in their place, can miss the bound.
Values may be sent and summed in bfloat16 or wider, within the bound.
No kernel may reach another device: no remote copies, remote signals or barrier semaphores. Data moves between devices by JAX's collectives and lax.ppermute only.
A program may use at most 192 MiB of HBM per device.

```python
import math
import jax
import jax.numpy as jnp
from jax import lax

D = 768
HEADS = 12
HEAD = 64
FF = 3072
LONG = 512
SHORT = 128
TOK_DEV = 2048
SLOTS = 16
BLOCKS = 16
TOKENS = 32768
SEQS = 256


def layout_bucket(key):
    shuffled = jax.random.permutation(jax.random.fold_in(key, 11), BLOCKS)
    return (shuffled < BLOCKS // 3).astype(jnp.int32)


def draw_bucket(key, part):
    return layout_bucket(key)


def draw_lengths(key, part):
    bucket_col = layout_bucket(key)[:, None]
    slot_ids = jnp.arange(SLOTS, dtype=jnp.int32)[None, :]
    seq_span = jnp.where(bucket_col == 1, SHORT, LONG).astype(jnp.int32)
    used_count = jnp.where(bucket_col == 1, SLOTS, TOK_DEV // LONG).astype(jnp.int32)
    low_end = seq_span // 4
    raw_draw = jax.random.randint(jax.random.fold_in(key, 12), (BLOCKS, SLOTS), 0, 1 << 20)
    length = low_end + raw_draw % (seq_span - low_end + 1)
    full_slot = jax.random.randint(jax.random.fold_in(key, 13), (BLOCKS, 1), 0, 1 << 20) % used_count
    length = jnp.where(slot_ids == full_slot, seq_span, length)
    length = jnp.where(slot_ids < used_count, length, 0)
    return length.reshape(-1).astype(jnp.int32)


def set_ends(array, rng, low, largest):
    dims = array.shape
    place = [jax.random.randint(jax.random.fold_in(rng, axis), (), 0, dims[axis]) for axis in range(len(dims))]
    array = array.at[tuple(place)].set(low)
    longest = dims.index(max(dims))
    place[longest] = (place[longest] + 1) % dims[longest]
    return array.at[tuple(place)].set(largest)


def block_levels(key, dims, shards, low, top_value):
    def one(axis_at, parts):
        draws = jax.random.uniform(jax.random.fold_in(jax.random.fold_in(key, 6), axis_at), (parts,), jnp.float32, low / len(shards), top_value / len(shards))
        return jnp.repeat(jnp.exp(draws), dims[axis_at] // parts).reshape((-1,) + (1,) * (len(dims) - axis_at - 1))

    level = one(*shards[0])
    for cut in shards[1:]:
        level = level * one(*cut)
    return level


def gaussian(rng, shape, deviation, most, pieces=(), kind=jnp.bfloat16):
    entries = deviation * jax.random.normal(rng, shape, jnp.float32)
    if pieces:
        entries = entries * block_levels(rng, shape, pieces, -0.22, 0.18)
    return jnp.clip(entries, -most, most).astype(kind)


def setup_inputs(seed: int = 0) -> dict:
    keys = jax.random.split(jax.random.key(seed), 18)
    return {
        "tokens": gaussian(keys[0], (TOKENS, D), 1.0, 6.0, ((0, 16),)),
        "qkv_weight": gaussian(keys[1], (D, 3, D), D ** -0.5, 0.21875, ((2, 2),)),
        "qv_bias": gaussian(keys[2], (2, D), 0.3, 1.5, ((1, 2),), jnp.float32),
        "proj_weight": gaussian(keys[3], (D, D), (max(D // 64, 1)) ** -0.5, 1.75, ((0, 2),)),
        "proj_bias": gaussian(keys[4], (D,), 0.3, 1.5, (), jnp.float32),
        "first_gain": jnp.clip(1.0 + 0.1 * jax.random.normal(keys[5], (D,), jnp.float32), 0.5, 1.5),
        "first_shift": gaussian(keys[6], (D,), 0.3, 1.5, (), jnp.float32),
        "up_weight": gaussian(keys[7], (D, FF), D ** -0.5, 0.21875, ((1, 2),)),
        "up_bias": gaussian(keys[8], (FF,), 0.3, 1.5, ((0, 2),), jnp.float32),
        "down_weight": gaussian(keys[9], (FF, D), FF ** -0.5, 0.109375, ((0, 2),)),
        "down_bias": gaussian(keys[10], (D,), 0.3, 1.5, (), jnp.float32),
        "second_gain": jnp.clip(1.0 + 0.1 * jax.random.normal(keys[11], (D,), jnp.float32), 0.5, 1.5),
        "second_shift": gaussian(keys[12], (D,), 0.3, 1.5, (), jnp.float32),
        "cotangent": gaussian(keys[13], (TOKENS, D), 1.0, 6.0, ((0, 16),)),
        "bucket": draw_bucket(jax.random.fold_in(keys[17], 71), 0),
        "lengths": draw_lengths(jax.random.fold_in(keys[17], 71), 0),
        "dropped": set_ends((jax.random.randint(keys[16], (SEQS,), 0, 5) < 1).astype(jnp.int32), jax.random.fold_in(keys[16], 1), 0, 1),
    }


@jax.custom_vjp
def low(v):
    return lax.optimization_barrier(v.astype(jnp.bfloat16)).astype(jnp.float32)

@jax.custom_vjp
def low_back(v):
    return v

def low_keep(v):
    return (low(v), None)

def low_pass(kept, grad):
    return (grad,)

def back_keep(v):
    return (v, None)

def back_low(kept, grad):
    return (low(grad),)
low.defvjp(low_keep, low_pass)
low_back.defvjp(back_keep, back_low)

def matmul(left, right):
    return jnp.dot(left, right, precision=lax.Precision.HIGHEST)

def layer_norm(values, gain_vec, shift_vec):
    centered = values - lax.optimization_barrier(jnp.mean(values, axis=-1, keepdims=True))
    variance = lax.optimization_barrier(jnp.mean(centered * centered, axis=-1, keepdims=True))
    return centered * lax.rsqrt(variance + 1e-05) * gain_vec + shift_vec

def token_layout(bucket_one, length_row, dropped_row):
    position = jnp.arange(TOK_DEV, dtype=jnp.int32)
    seq_span = jnp.where(bucket_one[0] == 1, SHORT, LONG).astype(jnp.int32)
    slot_index = position // seq_span
    offset = position % seq_span
    picker = slot_index[:, None] == jnp.arange(SLOTS, dtype=jnp.int32)[None, :]
    token_length = lax.optimization_barrier(jnp.sum(jnp.where(picker, length_row[None, :], 0), axis=1))
    token_drop = lax.optimization_barrier(jnp.sum(jnp.where(picker, dropped_row[None, :], 0), axis=1))
    is_valid = offset < token_length
    keep_rows = is_valid & (token_drop == 0)
    block_count = TOK_DEV // LONG
    block_slot = slot_index.reshape(block_count, LONG)
    block_valid = is_valid.reshape(block_count, LONG)
    allowed = (block_slot[:, :, None] == block_slot[:, None, :]) & block_valid[:, None, :]
    return (keep_rows, allowed)

def forward(inputs, params, allowed, keep_rows):
    weight_query, weight_key, weight_value, bias_query, bias_value, weight_proj, bias_proj, gain_one, shift_one, weight_up, bias_up, weight_down, bias_down, gain_two, shift_two = params
    scale_factor = 1.0 / math.sqrt(HEAD)
    queries = low_back(low(matmul(inputs, weight_query) + bias_query))
    key_rows = low_back(low(matmul(inputs, weight_key)))
    value_rows = low_back(low(matmul(inputs, weight_value) + bias_value))
    block_shape = (TOK_DEV // LONG, LONG, HEADS, HEAD)
    scores = jnp.einsum('bqhd,bkhd->bhqk', queries.reshape(block_shape), key_rows.reshape(block_shape), precision=lax.Precision.HIGHEST) * scale_factor
    scores = low_back(scores)
    scores = jnp.where(allowed[:, None], scores, -1e+30)
    row_max = lax.optimization_barrier(jnp.max(scores, axis=-1, keepdims=True))
    exp_scores = jnp.exp(scores - row_max)
    prob_rows = exp_scores / lax.optimization_barrier(jnp.sum(exp_scores, axis=-1, keepdims=True))
    prob_low = low(prob_rows)
    context = jnp.einsum('bhqk,bkhd->bqhd', prob_low, value_rows.reshape(block_shape), precision=lax.Precision.HIGHEST).reshape(TOK_DEV, D)
    context = low_back(low(context))
    attended = low_back(matmul(context, weight_proj))
    first_sum = inputs + attended + bias_proj
    hidden = layer_norm(first_sum, gain_one, shift_one)
    pre_act = low_back(matmul(low(hidden), weight_up) + bias_up)
    activated = low(jax.nn.gelu(pre_act, approximate=False))
    branch = low_back(matmul(activated, weight_down))
    second_sum = hidden + branch + bias_down
    normed = layer_norm(second_sum, gain_two, shift_two)
    return jnp.where(keep_rows[:, None], normed, inputs)

def reference(tokens, qkv_weight, qv_bias, proj_weight, proj_bias, first_gain, first_shift, up_weight, up_bias, down_weight, down_bias, second_gain, second_shift, cotangent, bucket, lengths, dropped):
    qkv_full = qkv_weight.astype(jnp.float32)
    bias_full = qv_bias.astype(jnp.float32)
    params = (qkv_full[:, 0, :], qkv_full[:, 1, :], qkv_full[:, 2, :], bias_full[0], bias_full[1], proj_weight.astype(jnp.float32), proj_bias.astype(jnp.float32), first_gain.astype(jnp.float32), first_shift.astype(jnp.float32), up_weight.astype(jnp.float32), up_bias.astype(jnp.float32), down_weight.astype(jnp.float32), down_bias.astype(jnp.float32), second_gain.astype(jnp.float32), second_shift.astype(jnp.float32))
    zero_grads = jax.tree.map(jnp.zeros_like, params)
    device_items = (tokens.reshape(BLOCKS, TOK_DEV, D), cotangent.reshape(BLOCKS, TOK_DEV, D), bucket.reshape(BLOCKS, 1), lengths.reshape(BLOCKS, SLOTS), dropped.reshape(BLOCKS, SLOTS))

    def device_step(running, items_now):
        tok_block, cot_block, bucket_one, length_row, dropped_row = items_now
        keep_rows, allowed = token_layout(bucket_one, length_row, dropped_row)

        def run_layer(inputs, layer_params):
            return forward(inputs, layer_params, allowed, keep_rows)
        outputs, pullback = jax.vjp(run_layer, tok_block.astype(jnp.float32), params)
        input_grad, param_grad = pullback(cot_block.astype(jnp.float32))
        running = jax.tree.map(lambda summed, addend: summed + addend, running, param_grad)
        return (running, (outputs.astype(jnp.bfloat16), input_grad))
    totals, (result_rows, grad_rows) = lax.scan(device_step, zero_grads, device_items)
    grad_query, grad_key, grad_value, grad_bias_query, grad_bias_value, grad_proj, grad_proj_bias, grad_gain_one, grad_shift_one, grad_up, grad_up_bias, grad_down, grad_down_bias, grad_gain_two, grad_shift_two = totals
    return (result_rows.reshape(TOKENS, D), grad_rows.reshape(TOKENS, D), jnp.stack([grad_query, grad_key, grad_value], axis=1), jnp.stack([grad_bias_query, grad_bias_value]), grad_proj, grad_proj_bias, grad_gain_one, grad_shift_one, grad_up, grad_up_bias, grad_down, grad_down_bias, grad_gain_two, grad_shift_two)
```

```python
import functools
import math

import jax
import jax.numpy as jnp
from jax import lax
from jax.experimental import pallas as pl
from jax.experimental.pallas import tpu as pltpu
from jax.sharding import PartitionSpec as P

HEAD = 64
LONG = 512
SHORT = 128
PAIR = 128
NEG = -1e30
BF = jnp.bfloat16
F32 = jnp.float32


def dot_nn(left, right):
    return lax.dot_general(left, right, (((1,), (0,)), ((), ())), preferred_element_type=F32)


def dot_nt(left, right):
    return lax.dot_general(left, right, (((1,), (1,)), ((), ())), preferred_element_type=F32)


def dot_tn(left, right):
    return lax.dot_general(left, right, (((0,), (0,)), ((), ())), preferred_element_type=F32)


def head_masks():
    lane = lax.broadcasted_iota(jnp.int32, (1, PAIR), 1)
    return (lane < HEAD, lane >= HEAD)


def only(mask, values):
    return jnp.where(mask, values, jnp.zeros_like(values))


def attend_tile(q, k, v, length):
    size = q.shape[0]
    valid = lax.broadcasted_iota(jnp.int32, (size, size), 0) < length
    total = None
    rows = []
    for mask in head_masks():
        scores = jnp.where(valid, dot_nt(k, only(mask, q)), NEG)
        top = jnp.max(scores, axis=0, keepdims=True)
        powers = jnp.exp(scores - top)
        summed = jnp.sum(powers, axis=0, keepdims=True)
        probs = (powers * (1.0 / summed)).astype(BF)
        part = dot_tn(probs, only(mask, v))
        total = part if total is None else total + part
        rows.append(top + jnp.log(summed))
    return total.astype(BF), jnp.concatenate(rows, axis=0)


def attend_kernel(info, q_ref, k_ref, v_ref, c_ref, lse_ref):
    block = pl.program_id(0)
    short = info[0] == 1

    @pl.when(jnp.logical_not(short))
    def _():
        c, rows = attend_tile(q_ref[...], k_ref[...], v_ref[...], info[1 + block])
        c_ref[...] = c
        lse_ref[0, 0] = rows

    @pl.when(short)
    def _():
        for sub in range(LONG // SHORT):
            at = slice(sub * SHORT, (sub + 1) * SHORT)
            length = info[1 + block * (LONG // SHORT) + sub]
            c, rows = attend_tile(q_ref[at, :], k_ref[at, :], v_ref[at, :], length)
            c_ref[at, :] = c
            lse_ref[0, 0, :, at] = rows


def attend_back_tile(q, k, v, grad_c, lse, length):
    size = q.shape[0]
    valid = lax.broadcasted_iota(jnp.int32, (size, size), 0) < length
    dq = dk = dv = None
    for index, mask in enumerate(head_masks()):
        q_own, c_own, k_own = only(mask, q), only(mask, grad_c), only(mask, k)
        scores = dot_nt(k, q_own)
        probs = jnp.where(valid, jnp.exp(scores - lse[index : index + 1, :]), 0.0)
        grad_probs = dot_nt(v, c_own)
        row_dot = jnp.sum(probs * grad_probs, axis=0, keepdims=True)
        grad_scores = (probs * (grad_probs - row_dot)).astype(BF)
        parts = (
            dot_tn(grad_scores, k_own),
            dot_nn(grad_scores, q_own),
            dot_nn(probs.astype(BF), c_own),
        )
        if dq is None:
            dq, dk, dv = parts
        else:
            dq, dk, dv = dq + parts[0], dk + parts[1], dv + parts[2]
    return (dq * (1.0 / math.sqrt(HEAD))).astype(BF), dk.astype(BF), dv.astype(BF)


def attend_back_kernel(info, q_ref, k_ref, v_ref, gc_ref, lse_ref, dq_ref, dk_ref, dv_ref):
    block = pl.program_id(0)
    short = info[0] == 1

    @pl.when(jnp.logical_not(short))
    def _():
        dq, dk, dv = attend_back_tile(
            q_ref[...], k_ref[...], v_ref[...], gc_ref[...], lse_ref[0, 0], info[1 + block]
        )
        dq_ref[...], dk_ref[...], dv_ref[...] = dq, dk, dv

    @pl.when(short)
    def _():
        for sub in range(LONG // SHORT):
            at = slice(sub * SHORT, (sub + 1) * SHORT)
            length = info[1 + block * (LONG // SHORT) + sub]
            dq, dk, dv = attend_back_tile(
                q_ref[at, :], k_ref[at, :], v_ref[at, :], gc_ref[at, :], lse_ref[0, 0, :, at], length
            )
            dq_ref[at, :], dk_ref[at, :], dv_ref[at, :] = dq, dk, dv


def attend_specs(width):
    pairs = width // PAIR
    return [
        pl.BlockSpec((LONG, PAIR), lambda b, p, info, k=k: (b, p + k * pairs)) for k in range(3)
    ]


def attend(info, qkv):
    rows, width = qkv.shape[0], qkv.shape[1] // 3
    blocks, pairs = rows // LONG, width // PAIR
    tile = pl.BlockSpec((LONG, PAIR), lambda b, p, info: (b, p))
    lse_tile = pl.BlockSpec((1, 1, 2, LONG), lambda b, p, info: (b, p, 0, 0))
    return pl.pallas_call(
        attend_kernel,
        grid_spec=pltpu.PrefetchScalarGridSpec(
            num_scalar_prefetch=1,
            grid=(blocks, pairs),
            in_specs=attend_specs(width),
            out_specs=[tile, lse_tile],
        ),
        out_shape=[
            jax.ShapeDtypeStruct((rows, width), BF),
            jax.ShapeDtypeStruct((blocks, pairs, 2, LONG), F32),
        ],
        compiler_params=pltpu.CompilerParams(vmem_limit_bytes=32 * 1024 * 1024),
        cost_estimate=pl.CostEstimate(
            flops=4 * rows * LONG * width, bytes_accessed=8 * rows * width, transcendentals=rows * LONG * width // HEAD
        ),
        name="attend",
    )(info, qkv, qkv, qkv)


def attend_back(info, qkv, grad_c, lse):
    rows, width = grad_c.shape
    blocks, pairs = rows // LONG, width // PAIR
    tile = pl.BlockSpec((LONG, PAIR), lambda b, p, info: (b, p))
    lse_tile = pl.BlockSpec((1, 1, 2, LONG), lambda b, p, info: (b, p, 0, 0))
    return pl.pallas_call(
        attend_back_kernel,
        grid_spec=pltpu.PrefetchScalarGridSpec(
            num_scalar_prefetch=1,
            grid=(blocks, pairs),
            in_specs=attend_specs(width) + [tile, lse_tile],
            out_specs=[tile] * 3,
        ),
        out_shape=[jax.ShapeDtypeStruct((rows, width), BF)] * 3,
        compiler_params=pltpu.CompilerParams(vmem_limit_bytes=48 * 1024 * 1024),
        cost_estimate=pl.CostEstimate(
            flops=10 * rows * LONG * width, bytes_accessed=14 * rows * width, transcendentals=rows * LONG * width // HEAD
        ),
        name="attend_back",
    )(info, qkv, qkv, qkv, grad_c, lse)


def swap_tensor(values):
    count = lax.axis_size("tensor")
    return lax.ppermute(values, "tensor", [(i, (i + 1) % count) for i in range(count)])


def swap_bit(values, bit):
    count = lax.axis_size("dp")
    return lax.ppermute(values, "dp", [(i, i ^ (1 << bit)) for i in range(count)])


def coordinate(bit):
    return (lax.axis_index("dp") >> bit) & 1


def half_of(values, which):
    rows = values.shape[0] // 2
    return lax.dynamic_slice_in_dim(values, which * rows, rows, 0)


def join(mine, other, bit):
    at = coordinate(bit)
    rows = mine.shape[0]
    whole = jnp.zeros((2 * rows,) + mine.shape[1:], mine.dtype)
    whole = lax.dynamic_update_slice_in_dim(whole, mine, at * rows, 0)
    return lax.dynamic_update_slice_in_dim(whole, other, (1 - at) * rows, 0)


def fetch(weight):
    mine = swap_tensor(half_of(weight, coordinate(0)))
    return join(mine, swap_bit(mine, 0), 0)


def scatter_step(values, bit):
    at = coordinate(bit)
    got = swap_bit(half_of(values, 1 - at).astype(BF), bit)
    return half_of(values, at).astype(F32) + got.astype(F32)


def dp_bits():
    return lax.axis_size("dp").bit_length() - 1


def sum_all(own, other):
    own, other = scatter_step(own, 0), scatter_step(other, 0)
    own = own + swap_tensor(other.astype(BF)).astype(F32)
    for bit in range(1, dp_bits()):
        own = scatter_step(own, bit)
    own = own.astype(BF)
    for bit in reversed(range(dp_bits())):
        own = join(own, swap_bit(own, bit), bit)
    return own.astype(F32)


def norm_forward(values, gain_vec, shift_vec):
    centered = values - jnp.mean(values, axis=-1, keepdims=True)
    variance = jnp.mean(centered * centered, axis=-1, keepdims=True)
    inverse = lax.rsqrt(variance + 1e-05)
    scaled = centered * inverse
    return (scaled * gain_vec + shift_vec, scaled, inverse)


def norm_backward(upstream, scaled, inverse, gain_vec):
    gain_grad = jnp.sum(upstream * scaled, axis=0)
    shift_grad = jnp.sum(upstream, axis=0)
    through = upstream * gain_vec
    inner_part = (
        through
        - jnp.mean(through, axis=-1, keepdims=True)
        - scaled * jnp.mean(through * scaled, axis=-1, keepdims=True)
    )
    return (inner_part * inverse, gain_grad, shift_grad)


def gelu_slope(values):
    cumulative = 0.5 * (1.0 + lax.erf(values * (1.0 / math.sqrt(2.0))))
    density = jnp.exp(-0.5 * values * values) * (1.0 / math.sqrt(2.0 * math.pi))
    return cumulative + values * density


def kept_rows(bucket, lengths, dropped, start, count):
    position = start + jnp.arange(count, dtype=jnp.int32)
    span = jnp.where(bucket[0] == 1, SHORT, LONG).astype(jnp.int32)
    slot, offset = position // span, position % span
    picker = slot[:, None] == jnp.arange(lengths.shape[0], dtype=jnp.int32)[None, :]
    limit = jnp.where(dropped == 0, lengths, 0)
    return offset < jnp.sum(jnp.where(picker, limit[None, :], 0), axis=1)


def body(
    tokens,
    qkv_weight,
    qv_bias,
    proj_weight,
    proj_bias,
    first_gain,
    first_shift,
    up_weight,
    up_bias,
    down_weight,
    down_bias,
    second_gain,
    second_shift,
    cotangent,
    bucket,
    lengths,
    dropped,
):
    token_count, width = tokens.shape
    parts = lax.axis_size("tensor")
    rows = token_count // parts
    place = lax.axis_index("tensor")
    row_start = place * rows
    local = qkv_weight.shape[2]
    keep = kept_rows(bucket, lengths, dropped, row_start, rows)[:, None]
    slots = rows // SHORT
    first_slot = jnp.where(bucket[0] == 1, place * slots, place * (rows // LONG))
    info = jnp.concatenate([bucket, lax.dynamic_slice_in_dim(lengths, first_slot, slots, 0)])
    x_low = lax.dynamic_slice_in_dim(tokens, row_start, rows, 0)
    x = x_low.astype(F32)
    upstream = lax.dynamic_slice_in_dim(cotangent, row_start, rows, 0).astype(F32)

    qkv_own = qkv_weight.reshape(width, 3 * local)
    qkv_oth = fetch(qkv_own)
    proj_oth = fetch(proj_weight)
    up_oth = fetch(up_weight)
    down_oth = fetch(down_weight)
    qv_bias_oth = swap_tensor(qv_bias)
    up_bias_oth = swap_tensor(up_bias)
    halves = range(2)
    qkv_w, proj_w = (qkv_own, qkv_oth), (proj_weight, proj_oth)
    up_w, down_w = (up_weight, up_oth), (down_weight, down_oth)
    qv_b, up_b = (qv_bias, qv_bias_oth), (up_bias, up_bias_oth)

    scale = 1.0 / math.sqrt(HEAD)
    qkv, context, lse = [], [], []
    for h in halves:
        bias_row = jnp.concatenate([qv_b[h][0], jnp.zeros_like(qv_b[h][0]), qv_b[h][1]])
        factor = jnp.concatenate([jnp.full((local,), scale, F32), jnp.ones((2 * local,), F32)])
        qkv.append(((dot_nn(x_low, qkv_w[h]) + bias_row) * factor).astype(BF))
        c, rows_lse = attend(info, qkv[h])
        context.append(c)
        lse.append(rows_lse)
    first_sum = x + proj_bias + (dot_nn(context[0], proj_w[0]) + dot_nn(context[1], proj_w[1]))
    hidden, scaled_one, inverse_one = norm_forward(first_sum, first_gain, first_shift)
    hidden_low = hidden.astype(BF)
    pre_act = [dot_nn(hidden_low, up_w[h]) + up_b[h] for h in halves]
    activated = [jax.nn.gelu(pre_act[h], approximate=False).astype(BF) for h in halves]
    second_sum = hidden + down_bias + (dot_nn(activated[0], down_w[0]) + dot_nn(activated[1], down_w[1]))
    normed, scaled_two, inverse_two = norm_forward(second_sum, second_gain, second_shift)
    result_own = jnp.where(keep, normed, x).astype(BF)

    def both_rows(mine):
        other = swap_tensor(mine)
        whole = jnp.zeros((token_count, width), mine.dtype)
        whole = lax.dynamic_update_slice_in_dim(whole, mine, row_start, 0)
        return lax.dynamic_update_slice_in_dim(whole, other, rows - row_start, 0)

    result = both_rows(result_own)

    grad_normed = jnp.where(keep, upstream, 0.0)
    grad_skip = jnp.where(keep, 0.0, upstream)
    grad_second, gain_two_grad, shift_two_grad = norm_backward(
        grad_normed, scaled_two, inverse_two, second_gain
    )
    down_bias_grad = jnp.sum(grad_second, axis=0)
    branch_grad = grad_second.astype(BF)
    down_grad = [dot_tn(activated[h], branch_grad) for h in halves]
    down_total = sum_all(*down_grad)
    grad_pre = [
        (dot_nt(branch_grad, down_w[h]) * gelu_slope(pre_act[h])).astype(BF) for h in halves
    ]
    up_grad = [dot_tn(hidden_low, grad_pre[h]) for h in halves]
    up_bias_grad = [jnp.sum(grad_pre[h], axis=0, dtype=F32) for h in halves]
    up_total = sum_all(*up_grad)
    grad_hidden = grad_second + (dot_nt(grad_pre[0], up_w[0]) + dot_nt(grad_pre[1], up_w[1]))
    grad_first, gain_one_grad, shift_one_grad = norm_backward(
        grad_hidden, scaled_one, inverse_one, first_gain
    )
    proj_bias_grad = jnp.sum(grad_first, axis=0)
    attn_grad = grad_first.astype(BF)
    proj_grad = [dot_tn(context[h], attn_grad) for h in halves]
    qkv_grad, qv_sums, input_grad = [], [], grad_skip + grad_first
    for h in halves:
        grad_ctx = dot_nt(attn_grad, proj_w[h]).astype(BF)
        dq, dk, dv = attend_back(info, qkv[h], grad_ctx, lse[h])
        grads = jnp.concatenate([dq, dk, dv], axis=1)
        qkv_grad.append(dot_tn(x_low, grads))
        qv_sums.append(jnp.stack([jnp.sum(dq, axis=0, dtype=F32), jnp.sum(dv, axis=0, dtype=F32)]))
        input_grad = input_grad + dot_nt(grads, qkv_w[h])
    qkv_total = sum_all(*qkv_grad)
    proj_total = sum_all(*proj_grad)
    tokens_grad = both_rows(input_grad.astype(BF)).astype(F32)

    norm_sums = lax.psum(
        jnp.stack(
            [proj_bias_grad, gain_one_grad, shift_one_grad, down_bias_grad, gain_two_grad, shift_two_grad]
        ),
        ("dp", "tensor"),
    )
    bias_own = jnp.concatenate([qv_sums[0].reshape(-1), up_bias_grad[0]])
    bias_oth = jnp.concatenate([qv_sums[1].reshape(-1), up_bias_grad[1]])
    bias_sum = lax.psum(bias_own + swap_tensor(bias_oth), "dp")
    return (
        result,
        tokens_grad,
        qkv_total.reshape(width, 3, local),
        bias_sum[: 2 * local].reshape(2, local),
        proj_total,
        norm_sums[0],
        norm_sums[1],
        norm_sums[2],
        up_total,
        bias_sum[2 * local :],
        down_total,
        norm_sums[3],
        norm_sums[4],
        norm_sums[5],
    )


def solution(mesh):
    rows, columns, whole = P("dp", None), P(None, "tensor"), P()
    return jax.shard_map(
        body,
        mesh=mesh,
        in_specs=(
            rows,
            P(None, None, "tensor"),
            columns,
            P("tensor", None),
            whole,
            whole,
            whole,
            columns,
            P("tensor"),
            P("tensor", None),
            whole,
            whole,
            whole,
            rows,
            P("dp"),
            P("dp"),
            P("dp"),
        ),
        out_specs=(
            rows,
            rows,
            P(None, None, "tensor"),
            columns,
            P("tensor", None),
            whole,
            whole,
            whole,
            columns,
            P("tensor"),
            P("tensor", None),
            whole,
            whole,
            whole,
        ),
        check_vma=False,
    )
```

```python
import functools
import math

import jax
import jax.numpy as jnp
from jax import lax
from jax.experimental import pallas as pl
from jax.experimental.pallas import tpu as pltpu
from jax.sharding import PartitionSpec as P

HEAD = 64
LONG = 512
SHORT = 128
PAIR = 128
NEG = -1e30
BF = jnp.bfloat16
F32 = jnp.float32
MIB = 1024 * 1024


def dot_nn(left, right):
    return lax.dot_general(left, right, (((1,), (0,)), ((), ())), preferred_element_type=F32)


def dot_nt(left, right):
    return lax.dot_general(left, right, (((1,), (1,)), ((), ())), preferred_element_type=F32)


def dot_tn(left, right):
    return lax.dot_general(left, right, (((0,), (0,)), ((), ())), preferred_element_type=F32)


def shaped(shape, dtype):
    return jax.ShapeDtypeStruct(shape, dtype)


def whole_block(shape):
    return pl.BlockSpec(shape, lambda *_: (0,) * len(shape), pipeline_mode=pl.Buffered(1))


def call(kernel, name, place, grid, ins, in_specs, outs, out_specs, flops=0, moved=0, limit=20, aliases=None, exps=0, deps=()):
    moved = moved or sum(math.prod(a.shape) * a.dtype.itemsize for a in (*ins, *outs))
    count, extra = len(ins) + 1, len(deps)

    def inner(*refs):
        kernel(*refs[:count], *refs[count + extra :])

    return pl.pallas_call(
        inner,
        grid_spec=pltpu.PrefetchScalarGridSpec(
            num_scalar_prefetch=1,
            grid=grid,
            in_specs=[*in_specs, *[pl.BlockSpec(memory_space=pl.ANY)] * extra],
            out_specs=out_specs,
        ),
        out_shape=outs,
        compiler_params=pltpu.CompilerParams(vmem_limit_bytes=limit * MIB),
        cost_estimate=pl.CostEstimate(flops=flops, bytes_accessed=moved, transcendentals=exps),
        input_output_aliases=aliases or {},
        name=name,
    )(place, *ins, *deps)


def head_masks():
    lane = lax.broadcasted_iota(jnp.int32, (1, PAIR), 1)
    return (lane < HEAD, lane >= HEAD)


def only(mask, values):
    return jnp.where(mask, values, jnp.zeros_like(values))


def attend_tile(q, k, v, length):
    size = q.shape[0]
    hide = jnp.where(lax.broadcasted_iota(jnp.int32, (size, 1), 0) < length, 0.0, NEG)
    total = None
    rows = []
    for mask in head_masks():
        scores = dot_nt(k, only(mask, q)) + hide
        top = jnp.max(scores, axis=0, keepdims=True)
        powers = jnp.exp(scores - top)
        summed = jnp.sum(powers, axis=0, keepdims=True)
        probs = (powers * (1.0 / summed)).astype(BF)
        part = dot_tn(only(mask, v), probs)
        total = part if total is None else total + part
        rows.append(top + jnp.log(summed))
    return jnp.transpose(total).astype(BF), jnp.concatenate(rows, axis=0)


def attend_kernel(info, q_ref, k_ref, v_ref, c_ref, lse_ref):
    block = pl.program_id(0)
    short = info[4] == 1

    @pl.when(jnp.logical_not(short))
    def _():
        c, rows = attend_tile(q_ref[...], k_ref[...], v_ref[...], info[5 + block])
        c_ref[...] = c
        lse_ref[0, 0] = rows

    @pl.when(short)
    def _():
        for sub in range(LONG // SHORT):
            at = slice(sub * SHORT, (sub + 1) * SHORT)
            length = info[5 + block * (LONG // SHORT) + sub]
            c, rows = attend_tile(q_ref[at, :], k_ref[at, :], v_ref[at, :], length)
            c_ref[at, :] = c
            lse_ref[0, 0, :, at] = rows


def attend_back_tile(q, k, v, grad_c, lse, length):
    size = q.shape[0]
    hide = jnp.where(lax.broadcasted_iota(jnp.int32, (size, 1), 0) < length, 0.0, NEG)
    dq = dk = dv = None
    for index, mask in enumerate(head_masks()):
        q_own, c_own, k_own = only(mask, q), only(mask, grad_c), only(mask, k)
        scores = dot_nt(k, q_own) + hide
        probs = jnp.exp(scores - lse[index : index + 1, :])
        grad_probs = dot_nt(v, c_own)
        row_dot = jnp.sum(probs * grad_probs, axis=0, keepdims=True)
        grad_scores = (probs * (grad_probs - row_dot)).astype(BF)
        parts = (
            dot_tn(k_own, grad_scores),
            dot_nn(grad_scores, q_own),
            dot_nn(probs.astype(BF), c_own),
        )
        if dq is None:
            dq, dk, dv = parts
        else:
            dq, dk, dv = dq + parts[0], dk + parts[1], dv + parts[2]
    return (jnp.transpose(dq) * (1.0 / math.sqrt(HEAD))).astype(BF), dk.astype(BF), dv.astype(BF)


def attend_back_kernel(pairs, info, q_ref, k_ref, v_ref, gc_ref, lse_ref, out_ref, sum_ref):
    block, pair = pl.program_id(0), pl.program_id(1)
    short = info[4] == 1

    def put(rows, parts, add):
        for which, part in enumerate(parts):
            lanes = pl.ds(pl.multiple_of((which * pairs + pair) * PAIR, PAIR), PAIR)
            out_ref[rows, lanes] = part
            summed = jnp.sum(part.astype(F32), axis=0, keepdims=True)
            if add:
                sum_ref[0, :, lanes] += summed
            else:
                sum_ref[0, :, lanes] = summed

    @pl.when(jnp.logical_not(short))
    def _():
        put(
            slice(None),
            attend_back_tile(
                q_ref[...], k_ref[...], v_ref[...], gc_ref[...], lse_ref[0, 0], info[5 + block]
            ),
            False,
        )

    @pl.when(short)
    def _():
        for sub in range(LONG // SHORT):
            at = slice(sub * SHORT, (sub + 1) * SHORT)
            length = info[5 + block * (LONG // SHORT) + sub]
            put(
                at,
                attend_back_tile(
                    q_ref[at, :], k_ref[at, :], v_ref[at, :], gc_ref[at, :], lse_ref[0, 0, :, at], length
                ),
                sub > 0,
            )


def attend_specs(width):
    pairs = width // PAIR
    return [
        pl.BlockSpec((LONG, PAIR), lambda b, p, info, k=k: (b, p + k * pairs)) for k in range(3)
    ]


def attend(info, qkv, deps=()):
    rows, width = qkv.shape[0], qkv.shape[1] // 3
    blocks, pairs = rows // LONG, width // PAIR
    tile = pl.BlockSpec((LONG, PAIR), lambda b, p, info: (b, p))
    lse_tile = pl.BlockSpec((1, 1, 2, LONG), lambda b, p, info: (b, p, 0, 0))
    return call(
        attend_kernel,
        "attend",
        info,
        (blocks, pairs),
        (qkv, qkv, qkv),
        attend_specs(width),
        [shaped((rows, width), BF), shaped((blocks, pairs, 2, LONG), F32)],
        [tile, lse_tile],
        flops=4 * rows * LONG * width,
        moved=8 * rows * width,
        exps=rows * LONG * width // HEAD,
        deps=deps,
    )


def attend_back(info, qkv, grad_c, lse, deps=()):
    rows, width = grad_c.shape
    blocks, pairs = rows // LONG, width // PAIR
    tile = pl.BlockSpec((LONG, PAIR), lambda b, p, info: (b, p))
    lse_tile = pl.BlockSpec((1, 1, 2, LONG), lambda b, p, info: (b, p, 0, 0))
    grads, sums = call(
        functools.partial(attend_back_kernel, pairs),
        "attend_back",
        info,
        (blocks, pairs),
        (qkv, qkv, qkv, grad_c, lse),
        attend_specs(width) + [tile, lse_tile],
        [shaped((rows, 3 * width), BF), shaped((blocks, 1, 3 * width), F32)],
        [
            pl.BlockSpec((LONG, 3 * width), lambda b, p, info: (b, 0)),
            pl.BlockSpec((1, 1, 3 * width), lambda b, p, info: (b, 0, 0)),
        ],
        flops=10 * rows * LONG * width,
        moved=14 * rows * width,
        exps=rows * LONG * width // HEAD,
        deps=deps,
    )
    return grads, jnp.sum(sums, axis=(0, 1))


def ffn_forward_kernel(chunk, place, h_ref, up_ref, bias_ref, down_ref, acc_in, *rest):
    act_ref, slope_ref, acc_ref = rest[-3:]

    @pl.when(pl.program_id(0) == 0)
    def _():
        acc_ref[...] = acc_in[...]

    for start in range(0, h_ref.shape[0], chunk):
        at = slice(start, start + chunk)
        pre = dot_nn(h_ref[at, :], up_ref[...]) + bias_ref[...]
        cumulative = 0.5 + 0.5 * lax.erf(pre * (1.0 / math.sqrt(2.0)))
        density = jnp.exp(-0.5 * pre * pre) * (1.0 / math.sqrt(2.0 * math.pi))
        act = (pre * cumulative).astype(BF)
        act_ref[0, at, :] = act
        slope_ref[0, at, :] = (cumulative + pre * density).astype(BF)
        acc_ref[at, :] += dot_nn(act, down_ref[...])


def ffn_forward(place, half, hidden_low, up, bias, down, acc, kept):
    rows, width = hidden_low.shape
    local = up.shape[1]
    tiles = 3
    size = local // tiles
    ins = [hidden_low, up, bias, down, acc]
    specs = [
        whole_block((rows, width)),
        pl.BlockSpec((width, size), lambda i, p: (0, i)),
        pl.BlockSpec((1, size), lambda i, p: (0, i)),
        pl.BlockSpec((size, width), lambda i, p: (i, 0)),
        whole_block((rows, width)),
    ]
    aliases = {}
    if kept:
        ins += kept
        specs += [pl.BlockSpec(memory_space=pl.ANY)] * 2
        aliases = {6: 0, 7: 1}
    piece = pl.BlockSpec((1, rows, size), lambda i, p: (half, 0, i))
    return call(
        functools.partial(ffn_forward_kernel, min(rows, 512)),
        "ffn_forward",
        place,
        (tiles,),
        ins,
        specs,
        [shaped((2, rows, local), BF), shaped((2, rows, local), BF), shaped((rows, width), F32)],
        [piece, piece, whole_block((rows, width))],
        flops=4 * rows * width * local,
        moved=20 * rows * width,
        exps=rows * local,
        limit=28,
        aliases=aliases,
    )


def ffn_backward_kernel(
    tiles, chunk, place, g_ref, slope_ref, up_own, up_oth, down_own, down_oth, acc_in, pre_ref, acc_ref, sum_ref
):
    step = pl.program_id(0)

    @pl.when(step == 0)
    def _():
        acc_ref[...] = acc_in[...]

    def work(up_ref, down_ref):
        total = None
        for start in range(0, g_ref.shape[0], chunk):
            at = slice(start, start + chunk)
            grad_act = dot_nt(g_ref[at, :], down_ref[...])
            low = (grad_act * slope_ref[0, at, :].astype(F32)).astype(BF)
            pre_ref[0, at, :] = low
            part = jnp.sum(low.astype(F32), axis=0, keepdims=True)
            total = part if total is None else total + part
            acc_ref[at, :] += dot_nt(low, up_ref[...])
        sum_ref[0] = total

    pl.when(step < tiles)(lambda: work(up_own, down_own))
    pl.when(step >= tiles)(lambda: work(up_oth, down_oth))


def ffn_backward(place, grad_low, slope, up, down, acc, deps=()):
    rows, width = grad_low.shape
    local = up[0].shape[1]
    tiles = 3
    size = local // tiles
    first = lambda i, p: (0, jnp.minimum(i, tiles - 1))
    second = lambda i, p: (0, jnp.maximum(i - tiles, 0))
    turned = lambda f: lambda i, p: f(i, p)[::-1]
    piece = pl.BlockSpec((1, rows, size), lambda i, p: (i // tiles, 0, i % tiles))
    return call(
        functools.partial(ffn_backward_kernel, tiles, min(rows, 512)),
        "ffn_backward",
        place,
        (2 * tiles,),
        (grad_low, slope, *up, *down, acc),
        [
            whole_block((rows, width)),
            piece,
            pl.BlockSpec((width, size), first),
            pl.BlockSpec((width, size), second),
            pl.BlockSpec((size, width), turned(first)),
            pl.BlockSpec((size, width), turned(second)),
            whole_block((rows, width)),
        ],
        [shaped((2, rows, local), BF), shaped((rows, width), F32), shaped((2 * tiles, 1, size), F32)],
        [piece, whole_block((rows, width)), pl.BlockSpec((1, 1, size), lambda i, p: (i, 0, 0))],
        flops=8 * rows * width * local,
        limit=28,
        deps=deps,
    )


def spread(value, got, place, put):
    count = 8
    size = value.shape[0] // count
    step = 16 if size % 16 == 0 else 8
    for k in range(count):
        at = pl.ds(pl.multiple_of((k ^ place[2]) * size, step), size)
        part = value[k * size : (k + 1) * size]
        if got is not None:
            part = part + got(at).astype(F32)
        put(at, part.astype(BF))


def spread_halves(value, got, place, puts):
    count = 8
    size = value.shape[0] // count
    step = 16 if size % 16 == 0 else 8
    for k in range(count):
        where = k ^ place[2]
        part = value[k * size : (k + 1) * size]
        if got is not None:
            part = part + got(pl.ds(pl.multiple_of(where * size, step), size)).astype(F32)
        part = part.astype(BF)
        at = pl.ds(pl.multiple_of((where & 3) * size, step), size)
        for high, put in enumerate(puts):
            pl.when((where >> 2) == high)(lambda: put(at, part))


def ffn_grad_kernel(has_got, form, place, left_ref, right_ref, *rest):
    half = pl.program_id(0)
    left = left_ref[0] if len(left_ref.shape) == 3 else left_ref[...]
    right = right_ref[0] if len(right_ref.shape) == 3 else right_ref[...]
    value = dot_tn(left, right)
    got = (lambda at: rest[0][0, at, :]) if has_got else None
    outs = rest[1:] if has_got else rest
    if form == "whole":

        def put(at, part):
            outs[0][0, at, :] = part

        spread(value, got, place, put)
    elif form == "sides":
        for which, out in enumerate(outs):

            @pl.when(half == which)
            def _():
                def put(at, part):
                    out[at, :] = part

                spread(value, got, place, put)
    else:
        spread_halves(value, got, place, [lambda at, part, out=out: put_first(out, at, part) for out in outs])


def put_first(out, at, part):
    out[0, at, :] = part


def ffn_grad(name, place, left, right, near, form, got=None, deps=()):
    rows = left.shape[-2]

    def spec(array):
        if array.ndim == 3:
            size = array.shape[2] // 2
            return pl.BlockSpec((1, rows, size), lambda h, p: (h, 0, p[0] if near else 1 - p[0])), size
        return whole_block(array.shape), array.shape[1]

    (left_spec, tall), (right_spec, wide) = spec(left), spec(right)
    piece = pl.BlockSpec((1, tall, wide), lambda h, p: (h, 0, 0))
    ins, specs = [left, right], [left_spec, right_spec]
    if got is not None:
        ins.append(got)
        specs.append(piece)
    outs, out_specs = {
        "whole": ([shaped((2, tall, wide), BF)], [piece]),
        "sides": ([shaped((tall, wide), BF)] * 2, [whole_block((tall, wide))] * 2),
        "rows": (
            [shaped((2, tall // 2, wide), BF)] * 2,
            [pl.BlockSpec((1, tall // 2, wide), lambda h, p: (h, 0, 0))] * 2,
        ),
    }[form]
    return call(
        functools.partial(ffn_grad_kernel, got is not None, form),
        name,
        place,
        (2,),
        ins,
        specs,
        outs,
        out_specs,
        flops=4 * rows * tall * wide,
        moved=2 * (4 * rows * tall + 4 * tall * wide),
        deps=deps,
    )


def attn_grad_kernel(near, place, x_ref, grads_ref, c_ref, a_ref, *rest):
    values = (dot_tn(x_ref[...], grads_ref[...]), dot_tn(c_ref[...], a_ref[...]))
    wide = values[0].shape[1]
    half = (wide + values[1].shape[1]) // 2
    if not near:
        out_ref = rest[0]
        for start, value in ((0, values[0]), (wide, values[1])):
            lanes = slice(start, start + value.shape[1])

            def put(at, part):
                out_ref[at, lanes] = part

            spread(value, None, place, put)
        return
    got_ref, left_ref, low_ref, high_ref = rest[0], *rest[-3:]

    def put_left(at, part):
        left_ref[at, :] = part

    spread(values[0][:, :half], lambda at: got_ref[at, :half], place, put_left)
    for start, value in ((half, values[0][:, half:]), (wide, values[1])):
        lanes = slice(start - half, start - half + value.shape[1])
        from_lanes = slice(start, start + value.shape[1])

        def put_in(out):
            def put(at, part):
                out[0, at, lanes] = part

            return put

        spread_halves(value, lambda at: got_ref[at, from_lanes], place, [put_in(low_ref), put_in(high_ref)])


def attn_grad(name, place, tokens, grads, context, out_grad, near, got=None, half=0, kept=(), deps=()):
    rows, width = out_grad.shape
    tall = width // 2
    side = pl.BlockSpec((rows, tall), lambda i, p: (0, p[0] if near else 1 - p[0]))
    tokens_side = pl.BlockSpec((rows, tall), lambda i, p: (p[3], p[0] if near else 1 - p[0]))
    wide = grads.shape[1] + tall
    ins = [tokens, grads, context, out_grad]
    specs = [tokens_side, whole_block(grads.shape), whole_block(context.shape), side]
    outs, out_specs, aliases = [shaped((tall, wide), BF)], [whole_block((tall, wide))], {}
    if near:
        ins.append(got)
        specs.append(whole_block(got.shape))
        outs = [shaped((tall, wide // 2), BF)] + [shaped((2, tall // 2, wide // 2), BF)] * 2
        piece = pl.BlockSpec((1, tall // 2, wide // 2), lambda i, p: (half, 0, 0))
        out_specs = [whole_block((tall, wide // 2)), piece, piece]
        if kept:
            ins += kept
            specs += [pl.BlockSpec(memory_space=pl.ANY)] * 2
            aliases = {6: 1, 7: 2}
    return call(
        functools.partial(attn_grad_kernel, near),
        name,
        place,
        (1,),
        ins,
        specs,
        outs,
        out_specs,
        flops=2 * rows * tall * wide,
        moved=2 * (rows * (wide + 2 * tall) + 2 * tall * wide),
        aliases=aliases,
        deps=deps,
    )


def pack_kernel(place, qkv_ref, proj_ref, up_ref, down_ref, attn_ref, *ffn_refs):
    wide = qkv_ref.shape[2]
    for k in range(3):
        attn_ref[:, k * wide : (k + 1) * wide] = qkv_ref[k]
    attn_ref[:, 3 * wide :] = proj_ref[...]
    tall = up_ref.shape[0] // 2
    for half, out in enumerate(ffn_refs):
        at = slice(half * tall, (half + 1) * tall)
        out[:tall, :] = up_ref[at, :]
        out[tall:, :] = down_ref[at, :]


def pack(place, qkv, proj, up, down):
    _, width, wide = qkv.shape
    heads, hidden = proj.shape[0], up.shape[1]
    quarter = lambda i, p: (2 * p[0] + p[1], 0)
    corner = lambda i, p: (p[1], p[0])
    rows = width // 4
    attn, ffn = (rows, 3 * wide + width // 2), (width // 4 + hidden // 8, width)
    qkv, proj, up, down = [pltpu.with_memory_space_constraint(a, pltpu.HBM) for a in (qkv, proj, up, down)]
    return call(
        pack_kernel,
        "pack",
        place,
        (1,),
        (qkv, proj, up, down),
        [
            pl.BlockSpec((3, rows, wide), lambda i, p: (0, 2 * p[0] + p[1], 0)),
            pl.BlockSpec((heads // 2, width // 2), corner),
            pl.BlockSpec((width // 2, hidden // 2), corner),
            pl.BlockSpec((hidden // 4, width), quarter),
        ],
        [shaped(attn, BF), shaped(ffn, BF), shaped(ffn, BF)],
        [whole_block(attn), whole_block(ffn), whole_block(ffn)],
        moved=8 * MIB,
    )


def join_attn_kernel(place, *refs):
    qkv_ref, proj_ref = refs[4:]
    wide = qkv_ref.shape[2]
    rows, side = refs[0].shape[0], refs[0].shape[1] - 3 * wide
    for r in range(4):
        c, y = (r >> 1) ^ place[0], (r & 1) ^ place[1]
        for k in range(3):
            qkv_ref[k, pl.ds(pl.multiple_of((2 * c + y) * rows, rows), rows), :] = refs[r][
                :, k * wide : (k + 1) * wide
            ]
        proj_ref[
            pl.ds(pl.multiple_of(y * rows, rows), rows), pl.ds(pl.multiple_of(c * side, side), side)
        ] = refs[r][:, 3 * wide :]


def join_attn(place, pieces, wide):
    rows, lanes = pieces[0].shape
    side = lanes - 3 * wide
    shapes = [(3, 4 * rows, wide), (2 * rows, 2 * side)]
    return call(
        join_attn_kernel,
        "join_attn",
        place,
        (1,),
        pieces,
        [whole_block(pieces[0].shape)] * 4,
        [shaped(s, BF) for s in shapes],
        [whole_block(s) for s in shapes],
    )


def join_ffn_kernel(place, *refs):
    up_ref, down_ref = refs[8:]
    rows, lanes = refs[0].shape
    tall = rows // 2
    for r in range(4):
        c, y = (r >> 1) ^ place[0], (r & 1) ^ place[1]
        for half in range(2):
            source = refs[4 * half + r]
            up_ref[
                pl.ds(pl.multiple_of((2 * y + half) * tall, tall), tall),
                pl.ds(pl.multiple_of(c * lanes, lanes), lanes),
            ] = source[:tall, :]
            down_ref[
                pl.ds(pl.multiple_of((4 * c + 2 * y + half) * tall, tall), tall), :
            ] = source[tall:, :]


def join_ffn(place, first, second):
    rows, lanes = first[0].shape
    shapes = [(2 * rows, 2 * lanes), (4 * rows, lanes)]
    return call(
        join_ffn_kernel,
        "join_ffn",
        place,
        (1,),
        [*first, *second],
        [whole_block(first[0].shape)] * 8,
        [shaped(s, BF) for s in shapes],
        [whole_block(s) for s in shapes],
    )


def rows_kernel(place, mine_ref, other_ref, out_ref):
    step = pl.program_id(0)

    @pl.when(step == 0)
    def _():
        out_ref[...] = mine_ref[...].astype(out_ref.dtype)

    @pl.when(step == 1)
    def _():
        out_ref[...] = other_ref[...].astype(out_ref.dtype)


def both_rows(name, place, mine, other, dtype, deps=()):
    rows, width = mine.shape
    return call(
        rows_kernel,
        name,
        place,
        (2,),
        (mine, other),
        [whole_block((rows, width))] * 2,
        [shaped((2 * rows, width), dtype)],
        [pl.BlockSpec((rows, width), lambda i, p: (i ^ p[3], 0))],
        deps=deps,
    )[0]


def tile_out_kernel(place, *refs):
    out_ref = refs[4]
    step = pl.program_id(0)
    size = refs[0].shape[0] // 4

    def work(low, high):
        for k in range(8):
            for h in range(2):

                @pl.when((k >> 2) ^ (place[2] >> 2) == h)
                def _():
                    at = pl.ds(pl.multiple_of(((k ^ place[2]) & 3) * size, size), size)
                    out_ref[k * size : (k + 1) * size, :] = (low, high)[h][at, :].astype(F32)

    pl.when(step == 0)(lambda: work(refs[0], refs[1]))
    pl.when(step == 1)(lambda: work(refs[2], refs[3]))


def tile_out(name, place, parts, across, deps=()):
    rows, width = parts[0].shape
    tall = 2 * rows
    shape = (tall, 2 * width) if across else (2 * tall, width)
    turn = (lambda i, p: (0, i ^ p[0])) if across else (lambda i, p: (i ^ p[0], 0))
    return call(
        tile_out_kernel,
        name,
        place,
        (2,),
        parts,
        [whole_block(parts[0].shape)] * 4,
        [shaped(shape, F32)],
        [pl.BlockSpec((tall, width), turn)],
        deps=deps,
    )[0]


def attn_out_kernel(place, *refs):
    qkv_ref, proj_ref = refs[4:]
    step = pl.program_id(0)
    size = refs[0].shape[0] // 4
    count, _, lanes = qkv_ref.shape

    def work(low, high):
        for k in range(8):
            for h in range(2):

                @pl.when((k >> 2) ^ (place[2] >> 2) == h)
                def _():
                    at = pl.ds(pl.multiple_of(((k ^ place[2]) & 3) * size, size), size)
                    source = (low, high)[h]
                    for n in range(count):
                        qkv_ref[n, k * size : (k + 1) * size, :] = source[
                            at, n * lanes : (n + 1) * lanes
                        ].astype(F32)
                    proj_ref[k * size : (k + 1) * size, :] = source[at, count * lanes :].astype(F32)

    pl.when(step == 0)(lambda: work(refs[0], refs[1]))
    pl.when(step == 1)(lambda: work(refs[2], refs[3]))


def attn_out(place, parts, count, lanes, deps=()):
    rows, wide = parts[0].shape
    tall = 2 * rows
    side = wide - count * lanes
    return call(
        attn_out_kernel,
        "attn_out",
        place,
        (2,),
        parts,
        [whole_block(parts[0].shape)] * 4,
        [shaped((count, 2 * tall, lanes), F32), shaped((tall, 2 * side), F32)],
        [
            pl.BlockSpec((count, tall, lanes), lambda i, p: (0, i ^ p[0], 0)),
            pl.BlockSpec((tall, side), lambda i, p: (0, i ^ p[0])),
        ],
        deps=deps,
    )


CORE, ROW, NEAR, FAR = range(4)


def swap_tensor(values):
    count = lax.axis_size("tensor")
    return lax.ppermute(values, "tensor", [(i, (i + 1) % count) for i in range(count)])


def swap(values, bit):
    count = lax.axis_size("dp")
    return lax.ppermute(values, "dp", [(i, i ^ (1 << bit)) for i in range(count)])


def dp_bits():
    return lax.axis_size("dp").bit_length() - 1


def after(values, *others):
    return lax.optimization_barrier((values, *others))[0]


def add(left, right):
    return (left.astype(F32) + right.astype(F32)).astype(BF)


def halves(left, right):
    rows = left.shape[0] // 2
    return add(left[:rows], right[:rows]), add(left[rows:], right[rows:])


def sum_along(keep, send):
    keep, send = halves(keep, swap(send, NEAR))
    keep = add(keep, swap(send, FAR))
    for bit in range(4, dp_bits()):
        keep = add(keep, swap(keep, bit))
    return keep


def spread_out(piece, axis):
    piece = jnp.concatenate([piece, swap(piece, FAR)], axis=axis)
    piece = jnp.concatenate([piece, swap(piece, NEAR)], axis=axis)
    high = swap(piece, ROW)
    return piece, high, swap(piece, CORE), swap(high, CORE)


BIAS_ONE, GAIN_ONE, SHIFT_ONE, BIAS_TWO, GAIN_TWO, SHIFT_TWO = range(6)


def vector(ref, which):
    return ref[which : which + 1, :]


def average(values):
    return jnp.sum(values, axis=-1, keepdims=True) * (1.0 / values.shape[-1])


def normed(values):
    centered = values - average(values)
    inverse = lax.rsqrt(average(centered * centered) + 1e-05)
    return centered * inverse, inverse


def norm_back(upstream, scaled, inverse, gain):
    through = upstream * gain
    return inverse * (through - average(through) - scaled * average(through * scaled))


def column_sums(ref, parts):
    summed = [jnp.sum(part, axis=0, keepdims=True) for part in parts]
    summed.append(jnp.zeros((ref.shape[0] - len(parts), ref.shape[1]), F32))
    summed = jnp.concatenate(summed, axis=0)

    @pl.when(pl.program_id(0) == 0)
    def _():
        ref[...] = summed

    @pl.when(pl.program_id(0) > 0)
    def _():
        ref[...] += summed


def kept_column(place, groups):
    row = lax.broadcasted_iota(jnp.int32, (SHORT, 1), 0)
    first = 13 + pl.program_id(0) * groups
    return jnp.concatenate([(row < place[first + g]).astype(F32) for g in range(groups)], axis=0) > 0.5


def qkv_kernel(place, x_ref, weight_ref, bias_ref, out_ref):
    factor = jnp.where(pl.program_id(0) == 0, 1.0 / math.sqrt(HEAD), 1.0)
    out_ref[...] = ((dot_nn(x_ref[...], weight_ref[0]) + bias_ref[0]) * factor).astype(BF)


def project_qkv(place, tokens, rows, weight, bias):
    count, width, local = weight.shape
    return call(
        qkv_kernel,
        "project_qkv",
        place,
        (count,),
        (tokens, weight, bias),
        [
            pl.BlockSpec((rows, width), lambda k, p: (p[3], 0)),
            pl.BlockSpec((1, width, local), lambda k, p: (k, 0, 0)),
            pl.BlockSpec((1, 1, local), lambda k, p: (k, 0, 0)),
        ],
        [shaped((rows, count * local), BF)],
        [pl.BlockSpec((rows, local), lambda k, p: (0, k))],
        flops=2 * rows * width * count * local,
    )[0]


def first_norm_kernel(place, x_ref, c_own, c_oth, w_own, w_oth, vec_ref, hidden_ref, low_ref, scaled_ref, inverse_ref):
    attended = dot_nn(c_own[...], w_own[...]) + dot_nn(c_oth[...], w_oth[...])
    scaled, inverse = normed(x_ref[...].astype(F32) + attended + vector(vec_ref, BIAS_ONE))
    hidden = scaled * vector(vec_ref, GAIN_ONE) + vector(vec_ref, SHIFT_ONE)
    hidden_ref[...] = hidden
    low_ref[...] = hidden.astype(BF)
    scaled_ref[...] = scaled
    inverse_ref[...] = inverse


def first_norm(place, tokens, context, proj, vec):
    rows, local = context[0].shape
    width = tokens.shape[1]
    steps = 4
    size = rows // steps
    tile = pl.BlockSpec((size, width), lambda i, p: (i, 0))
    part = pl.BlockSpec((size, local), lambda i, p: (i, 0))
    return call(
        first_norm_kernel,
        "first_norm",
        place,
        (steps,),
        (tokens, *context, *proj, vec),
        [
            pl.BlockSpec((size, width), lambda i, p: (steps * p[3] + i, 0)),
            part,
            part,
            whole_block((local, width)),
            whole_block((local, width)),
            whole_block(vec.shape),
        ],
        [
            shaped((rows, width), F32),
            shaped((rows, width), BF),
            shaped((rows, width), F32),
            shaped((rows, 1), F32),
        ],
        [tile, tile, tile, pl.BlockSpec((size, 1), lambda i, p: (i, 0))],
        flops=4 * rows * width * local,
        moved=14 * rows * width,
    )


def second_norm_kernel(place, acc_ref, x_ref, up_ref, vec_ref, result_ref, grad_ref, low_ref, sum_ref):
    keep = kept_column(place, acc_ref.shape[0] // SHORT)
    gain = vector(vec_ref, GAIN_TWO)
    scaled, inverse = normed(acc_ref[...] + vector(vec_ref, BIAS_TWO))
    result = scaled * gain + vector(vec_ref, SHIFT_TWO)
    result_ref[...] = jnp.where(keep, result, x_ref[...].astype(F32)).astype(BF)
    upstream = jnp.where(keep, up_ref[...].astype(F32), 0.0)
    grad = norm_back(upstream, scaled, inverse, gain)
    grad_ref[...] = grad
    low_ref[...] = grad.astype(BF)
    column_sums(sum_ref, (grad, upstream * scaled, upstream))


def second_norm(place, acc, tokens, cotangent, vec):
    rows, width = acc.shape
    steps = 4
    size = rows // steps
    tile = pl.BlockSpec((size, width), lambda i, p: (i, 0))
    far = pl.BlockSpec((size, width), lambda i, p: (steps * p[3] + i, 0))
    return call(
        second_norm_kernel,
        "second_norm",
        place,
        (steps,),
        (acc, tokens, cotangent, vec),
        [tile, far, far, whole_block(vec.shape)],
        [shaped((rows, width), BF), shaped((rows, width), F32), shaped((rows, width), BF), shaped((8, width), F32)],
        [tile, tile, tile, whole_block((8, width))],
        moved=16 * rows * width,
    )


def first_back_kernel(
    place, grad_in, scaled_ref, inverse_ref, up_ref, w_own, w_oth, vec_ref, base_ref, low_ref, c_own, c_oth, sum_ref
):
    keep = kept_column(place, grad_in.shape[0] // SHORT)
    upstream, scaled = grad_in[...], scaled_ref[...]
    grad = norm_back(upstream, scaled, inverse_ref[...], vector(vec_ref, GAIN_ONE))
    low = grad.astype(BF)
    base_ref[...] = grad + jnp.where(keep, 0.0, up_ref[...].astype(F32))
    low_ref[...] = low
    c_own[...] = dot_nt(low, w_own[...]).astype(BF)
    c_oth[...] = dot_nt(low, w_oth[...]).astype(BF)
    column_sums(sum_ref, (grad, upstream * scaled, upstream))


def first_back(place, grad, scaled, inverse, cotangent, proj, vec, deps=()):
    rows, width = grad.shape
    local = proj[0].shape[0]
    steps = 4
    size = rows // steps
    tile = pl.BlockSpec((size, width), lambda i, p: (i, 0))
    part = pl.BlockSpec((size, local), lambda i, p: (i, 0))
    return call(
        first_back_kernel,
        "first_back",
        place,
        (steps,),
        (grad, scaled, inverse, cotangent, *proj, vec),
        [
            tile,
            tile,
            pl.BlockSpec((size, 1), lambda i, p: (i, 0)),
            pl.BlockSpec((size, width), lambda i, p: (steps * p[3] + i, 0)),
            whole_block((local, width)),
            whole_block((local, width)),
            whole_block(vec.shape),
        ],
        [
            shaped((rows, width), F32),
            shaped((rows, width), BF),
            shaped((rows, local), BF),
            shaped((rows, local), BF),
            shaped((8, width), F32),
        ],
        [tile, tile, part, part, whole_block((8, width))],
        flops=4 * rows * width * local,
        moved=18 * rows * width,
        deps=deps,
    )


def input_grad_kernel(place, base_ref, g_own, g_oth, w_own, w_oth, out_ref):
    count, _, local = w_own.shape
    total = base_ref[...]
    for grads, weight in ((g_own, w_own), (g_oth, w_oth)):
        for k in range(count):
            total = total + dot_nt(grads[:, k * local : (k + 1) * local], weight[k])
    out_ref[...] = total.astype(BF)


def input_grad(place, base, grads, weights, deps=()):
    rows, width = base.shape
    wide = grads[0].shape[1]
    steps = 2
    size = rows // steps
    tile = pl.BlockSpec((size, width), lambda i, p: (i, 0))
    part = pl.BlockSpec((size, wide), lambda i, p: (i, 0))
    return call(
        input_grad_kernel,
        "input_grad",
        place,
        (steps,),
        (base, *grads, *weights),
        [tile, part, part, whole_block(weights[0].shape), whole_block(weights[0].shape)],
        [shaped((rows, width), BF)],
        [tile],
        flops=4 * rows * width * wide,
        deps=deps,
    )[0]


def body(
    tokens,
    qkv_weight,
    qv_bias,
    proj_weight,
    proj_bias,
    first_gain,
    first_shift,
    up_weight,
    up_bias,
    down_weight,
    down_bias,
    second_gain,
    second_shift,
    cotangent,
    bucket,
    lengths,
    dropped,
):
    token_count, width = tokens.shape
    rows = token_count // lax.axis_size("tensor")
    side = lax.axis_index("tensor")
    index = lax.axis_index("dp")
    core, row, near, far = [(index >> bit) & 1 for bit in range(4)]
    local = qkv_weight.shape[2]
    hidden_count = up_weight.shape[1]

    groups = rows // SHORT
    is_short = bucket[0] == 1
    first_slot = jnp.where(is_short, side * groups, side * (rows // LONG))
    slot_lengths = lax.dynamic_slice_in_dim(lengths, first_slot, groups, 0)
    slot_drops = lax.dynamic_slice_in_dim(dropped, first_slot, groups, 0)
    limits = jnp.where(slot_drops == 0, slot_lengths, 0)
    per = LONG // SHORT
    long_limits = jnp.repeat(limits[: groups // per], per) - SHORT * (jnp.arange(groups) % per)
    limits = jnp.where(is_short, limits, long_limits)
    place = jnp.concatenate(
        [
            jnp.stack([core, row, 4 * row + 2 * near + far, side, bucket[0]]),
            slot_lengths,
            limits,
        ]
    ).astype(jnp.int32)
    vec = jnp.stack([proj_bias, first_gain, first_shift, down_bias, second_gain, second_shift])

    qkv_own = jnp.transpose(qkv_weight, (1, 0, 2))
    attn_piece, ffn_one, ffn_two = pack(place, qkv_own, proj_weight, up_weight, down_weight)
    biases = jnp.concatenate([qv_bias.reshape(-1), up_bias])

    def qkv_bias(values):
        return jnp.stack([values[:local], jnp.zeros((local,), F32), values[local : 2 * local]])[:, None, :]

    def up_row(values):
        return values[2 * local :].reshape(1, hidden_count)

    attn_x = swap_tensor(attn_piece)
    qkv = [project_qkv(place, tokens, rows, qkv_own, qkv_bias(biases))]
    c_own, lse_own = attend(place, qkv[0])
    attn_x = after(attn_x, c_own)
    attn_y = swap(attn_x, ROW)
    ffn_x = [swap_tensor(after(ffn_one, c_own))]
    biases_oth = swap_tensor(after(biases, c_own))
    ffn_x.append(swap_tensor(after(ffn_two, attn_x)))
    attn_core = swap(attn_x, CORE)
    ffn_x[0] = after(ffn_x[0], attn_y)
    ffn_y = [swap(ffn_x[0], ROW)]
    qkv_oth, proj_oth = join_attn(place, [attn_x, attn_y, attn_core, swap(attn_y, CORE)], local)
    qkv_w, proj_w = (qkv_own, qkv_oth), (proj_weight, proj_oth)
    qkv.append(project_qkv(place, tokens, rows, qkv_oth, qkv_bias(biases_oth)))
    ffn_x[1] = after(ffn_x[1], qkv[1])
    c_oth, lse_oth = attend(place, qkv[1], deps=[ffn_x[1]])
    context, lse = (c_own, c_oth), (lse_own, lse_oth)
    ffn_y[0] = after(ffn_y[0], c_oth)
    ffn_y.append(swap(ffn_x[1], ROW))
    ffn_core = [swap(after(v, c_oth), CORE) for v in ffn_x]
    hidden, hidden_low, scaled, inverse = first_norm(place, tokens, context, proj_w, vec)
    act, slope, acc = ffn_forward(
        place, 0, hidden_low, up_weight, up_row(biases), down_weight, hidden, []
    )
    ffn_y[1] = after(ffn_y[1], act)
    first, second = [
        [ffn_x[k], ffn_y[k], ffn_core[k], swap(ffn_y[k], CORE)] for k in range(2)
    ]
    up_oth, down_oth = join_ffn(place, first, second)
    up_w, down_w = (up_weight, up_oth), (down_weight, down_oth)
    act, slope, acc = ffn_forward(
        place, 1, hidden_low, up_oth, up_row(biases_oth), down_oth, acc, [act, slope]
    )
    result_own, grad_second, branch_grad, sums_two = second_norm(place, acc, tokens, cotangent, vec)
    result_x = swap_tensor(result_own)

    (down_far,) = ffn_grad("down_far", place, act, branch_grad, False, "whole")
    down_got = swap(down_far, CORE)
    grad_pre, grad_hidden, up_sums = ffn_backward(
        place, branch_grad, slope, up_w, down_w, grad_second, deps=[down_far]
    )
    down_own, down_other = ffn_grad(
        "down_near", place, act, branch_grad, True, "sides", down_got, deps=[grad_hidden]
    )
    down_x = swap_tensor(down_other)
    (up_far,) = ffn_grad("up_far", place, hidden_low, grad_pre, False, "whole", deps=[down_own])
    up_got = swap(up_far, CORE)
    base, out_grad, gc_own, gc_oth, sums_one = first_back(
        place, grad_hidden, scaled, inverse, cotangent, proj_w, vec, deps=[up_far]
    )
    up_low, up_high = ffn_grad(
        "up_near", place, hidden_low, grad_pre, True, "rows", up_got, deps=[out_grad]
    )
    up_y = swap(up_high, ROW)

    grads_oth, bias_sums_oth = attend_back(place, qkv[1], gc_oth, lse[1], deps=[up_low])
    (far_oth,) = attn_grad("attn_far", place, tokens, grads_oth, context[1], out_grad, False)
    got_oth = swap(far_oth, CORE)
    down_keep, down_send = halves(down_own, after(down_x, far_oth))
    down_y = swap(down_send, ROW)
    grads_own, bias_sums_own = attend_back(place, qkv[0], gc_own, lse[0], deps=[far_oth, down_keep])
    up_y = after(up_y, grads_own)
    up_keep, up_send = add(up_low[0], up_y[0]), add(up_low[1], up_y[1])
    up_x = swap_tensor(up_send)
    (far_own,) = attn_grad(
        "attn_far", place, tokens, grads_own, context[0], out_grad, False, deps=[up_send]
    )
    got_own = swap(far_own, CORE)
    left_oth, *right = attn_grad(
        "attn_near", place, tokens, grads_oth, context[1], out_grad, True, got_oth, 1, deps=[far_own]
    )
    left_x = swap_tensor(left_oth)
    down_keep, down_send = halves(down_keep, after(down_y, left_oth))
    left_own, right_low, right_high = attn_grad(
        "attn_near", place, tokens, grads_own, context[0], out_grad, True, got_own, 0, right, deps=[down_keep]
    )
    right_y = swap(right_high, ROW)
    down_z = swap(down_send, NEAR)
    down_keep, down_send = halves(down_keep, after(down_z, left_own))
    down_f = swap(down_send, FAR)
    input_low = input_grad(place, base, (grads_own, grads_oth), qkv_w, deps=[left_own, down_keep])
    input_x = swap_tensor(input_low)

    token = [input_low]

    def then(values):
        values = after(values, *token)
        return values

    def done(*results):
        token[0] = results[-1]
        return results if len(results) > 1 else results[0]

    def grown(piece, other):
        return done(jnp.concatenate([piece, other], axis=0))

    up_sums = up_sums.reshape(2, hidden_count)
    mine = [
        jnp.concatenate([s[:local], s[2 * local :], up_sums[h]]).reshape(-1, width)
        for h, s in enumerate((bias_sums_own, bias_sums_oth))
    ]
    shared = jnp.concatenate([sums_one[:3], sums_two[:3]])
    small = jnp.concatenate([shared, mine[0]])
    small_x = swap_tensor(jnp.concatenate([shared, mine[1]]))

    def last_bits(values):
        for bit in range(4, dp_bits()):
            values = add(values, swap(values, bit))
        return values

    up_keep, up_send = done(*halves(up_keep, then(up_x)))
    up_z = swap(up_send, NEAR)
    down_sum = done(last_bits(add(down_keep, then(down_f))))
    down_a = swap(down_sum, FAR)
    left_keep, left_send = done(*halves(left_own, then(left_x)))
    left_y = swap(left_send, ROW)
    right_y = then(right_y)
    right_keep, right_send = done(add(right_low[0], right_y[0]), add(right_low[1], right_y[1]))
    right_x = swap_tensor(right_send)
    small = done(small + then(small_x))
    small_c = swap(small, CORE)
    up_keep, up_send = done(*halves(up_keep, then(up_z)))
    up_f = swap(up_send, FAR)
    down_sum = grown(down_sum, then(down_a))
    down_b = swap(down_sum, NEAR)
    small = done(small + then(small_c))
    small_y = swap(small, ROW)
    left_keep, left_send = done(*halves(left_keep, then(left_y)))
    left_z = swap(left_send, NEAR)
    up_sum = done(last_bits(add(up_keep, then(up_f))))
    up_a = swap(up_sum, FAR)
    right_keep, right_send = done(*halves(right_keep, then(right_x)))
    right_z = swap(right_send, NEAR)
    down_sum = grown(down_sum, then(down_b))
    down_y = swap(down_sum, ROW)
    down_core = swap(down_sum, CORE)
    left_keep, left_send = done(*halves(left_keep, then(left_z)))
    left_f = swap(left_send, FAR)
    right_keep, right_send = done(*halves(right_keep, then(right_z)))
    right_f = swap(right_send, FAR)
    up_sum = grown(up_sum, then(up_a))
    up_b = swap(up_sum, NEAR)
    small = done(small + then(small_y))
    small_z = swap(small, NEAR)
    left_sum = add(left_keep, then(left_f))
    attn_sum = jnp.concatenate([left_sum, add(right_keep, then(right_f))], axis=1)
    attn_sum = done(last_bits(attn_sum))
    attn_a = swap(attn_sum, FAR)
    result = done(both_rows("result_rows", place, result_own, result_x, BF, deps=token))
    up_sum = grown(up_sum, then(up_b))
    up_y = swap(up_sum, ROW)
    up_core = swap(up_sum, CORE)
    attn_sum = grown(attn_sum, then(attn_a))
    attn_b = swap(attn_sum, NEAR)
    small = done(small + then(small_z))
    for bit in range(FAR, dp_bits()):
        small = small + swap(small, bit)
    down_y = then(down_y)
    down_parts = [down_sum, down_y, down_core, swap(down_y, CORE)]
    attn_sum = grown(attn_sum, then(attn_b))
    attn_y = swap(attn_sum, ROW)
    attn_core = swap(attn_sum, CORE)
    down_total = done(tile_out("down_out", place, down_parts, False, deps=token))
    up_y = then(up_y)
    up_parts = [up_sum, up_y, up_core, swap(up_y, CORE)]
    tokens_grad = done(both_rows("grad_rows", place, input_low, input_x, F32, deps=token))
    up_total = done(tile_out("up_out", place, up_parts, True, deps=token))
    attn_y = then(attn_y)
    qkv_total, proj_total = attn_out(
        place, [attn_sum, attn_y, attn_core, swap(attn_y, CORE)], 3, local, deps=token
    )

    bias_total = small[6:].reshape(-1)
    return (
        result,
        tokens_grad,
        jnp.transpose(qkv_total, (1, 0, 2)),
        bias_total[: 2 * local].reshape(2, local),
        proj_total,
        small[0],
        small[1],
        small[2],
        up_total,
        bias_total[2 * local :],
        down_total,
        small[3],
        small[4],
        small[5],
    )


def solution(mesh):
    rows, columns, whole = P("dp", None), P(None, "tensor"), P()
    return jax.shard_map(
        body,
        mesh=mesh,
        in_specs=(
            rows,
            P(None, None, "tensor"),
            columns,
            P("tensor", None),
            whole,
            whole,
            whole,
            columns,
            P("tensor"),
            P("tensor", None),
            whole,
            whole,
            whole,
            rows,
            P("dp"),
            P("dp"),
            P("dp"),
        ),
        out_specs=(
            rows,
            rows,
            P(None, None, "tensor"),
            columns,
            P("tensor", None),
            whole,
            whole,
            whole,
            columns,
            P("tensor"),
            P("tensor", None),
            whole,
            whole,
            whole,
        ),
        check_vma=False,
    )
```

```python
import functools
import math

import jax
import jax.numpy as jnp
from jax import lax
from jax.experimental import pallas as pl
from jax.experimental.pallas import tpu as pltpu
from jax.sharding import PartitionSpec as P

HEAD = 64
LONG = 512
SHORT = 128
PAIR = 128
NEG = -1e30
BF = jnp.bfloat16
F32 = jnp.float32
MIB = 1024 * 1024
WEIGHT = 40
SUM_WEIGHT = 4


def dot_nn(left, right):
    return lax.dot_general(left, right, (((1,), (0,)), ((), ())), preferred_element_type=F32)


def dot_nt(left, right):
    return lax.dot_general(left, right, (((1,), (1,)), ((), ())), preferred_element_type=F32)


def dot_tn(left, right):
    return lax.dot_general(left, right, (((0,), (0,)), ((), ())), preferred_element_type=F32)


def shaped(shape, dtype):
    return jax.ShapeDtypeStruct(shape, dtype)


def whole_block(shape):
    return pl.BlockSpec(shape, lambda *_: (0,) * len(shape), pipeline_mode=pl.Buffered(1))


def call(kernel, name, place, grid, ins, in_specs, outs, out_specs, flops=0, moved=0, limit=20, aliases=None, exps=0, deps=(), weight=WEIGHT, final=False):
    moved = moved or sum(math.prod(a.shape) * a.dtype.itemsize for a in (*ins, *outs))
    count, extra = len(ins) + 1, len(deps)
    if final:
        outs = [pltpu.HBM(a.shape, a.dtype) for a in outs]

    def inner(*refs):
        kernel(*refs[:count], *refs[count + extra :])

    return pl.pallas_call(
        inner,
        grid_spec=pltpu.PrefetchScalarGridSpec(
            num_scalar_prefetch=1,
            grid=grid,
            in_specs=[*in_specs, *[pl.BlockSpec(memory_space=pl.ANY)] * extra],
            out_specs=out_specs,
        ),
        out_shape=outs,
        compiler_params=pltpu.CompilerParams(vmem_limit_bytes=limit * MIB),
        cost_estimate=pl.CostEstimate(
            flops=weight * flops, bytes_accessed=weight * moved, transcendentals=weight * exps
        ),
        input_output_aliases=aliases or {},
        name=name,
    )(place, *ins, *deps)


def head_masks():
    lane = lax.broadcasted_iota(jnp.int32, (1, PAIR), 1)
    return (lane < HEAD, lane >= HEAD)


def only(mask, values):
    return jnp.where(mask, values, jnp.zeros_like(values))


def attend_tile(q, k, v, length):
    size = q.shape[0]
    hide = jnp.where(lax.broadcasted_iota(jnp.int32, (size, 1), 0) < length, 0.0, NEG)
    total = None
    rows = []
    for mask in head_masks():
        scores = dot_nt(k, only(mask, q)) + hide
        top = jnp.max(scores, axis=0, keepdims=True)
        powers = jnp.exp(scores - top)
        summed = jnp.sum(powers, axis=0, keepdims=True)
        probs = (powers * (1.0 / summed)).astype(BF)
        part = dot_tn(only(mask, v), probs)
        total = part if total is None else total + part
        rows.append(top + jnp.log(summed))
    return jnp.transpose(total).astype(BF), jnp.concatenate(rows, axis=0)


def attend_kernel(info, q_ref, k_ref, v_ref, c_ref, lse_ref):
    block = pl.program_id(0)
    short = info[4] == 1

    @pl.when(jnp.logical_not(short))
    def _():
        c, rows = attend_tile(q_ref[...], k_ref[...], v_ref[...], info[5 + block])
        c_ref[...] = c
        lse_ref[0, 0] = rows

    @pl.when(short)
    def _():
        for sub in range(LONG // SHORT):
            at = slice(sub * SHORT, (sub + 1) * SHORT)
            length = info[5 + block * (LONG // SHORT) + sub]
            c, rows = attend_tile(q_ref[at, :], k_ref[at, :], v_ref[at, :], length)
            c_ref[at, :] = c
            lse_ref[0, 0, :, at] = rows


def attend_back_tile(q, k, v, grad_c, lse, length):
    size = q.shape[0]
    hide = jnp.where(lax.broadcasted_iota(jnp.int32, (size, 1), 0) < length, 0.0, NEG)
    dq = dk = dv = None
    for index, mask in enumerate(head_masks()):
        q_own, c_own, k_own = only(mask, q), only(mask, grad_c), only(mask, k)
        scores = dot_nt(k, q_own) + hide
        probs = jnp.exp(scores - lse[index : index + 1, :])
        grad_probs = dot_nt(v, c_own)
        row_dot = jnp.sum(probs * grad_probs, axis=0, keepdims=True)
        grad_scores = (probs * (grad_probs - row_dot)).astype(BF)
        parts = (
            dot_tn(k_own, grad_scores),
            dot_nn(grad_scores, q_own),
            dot_nn(probs.astype(BF), c_own),
        )
        if dq is None:
            dq, dk, dv = parts
        else:
            dq, dk, dv = dq + parts[0], dk + parts[1], dv + parts[2]
    return (jnp.transpose(dq) * (1.0 / math.sqrt(HEAD))).astype(BF), dk.astype(BF), dv.astype(BF)


def attend_back_kernel(pairs, info, q_ref, k_ref, v_ref, gc_ref, lse_ref, out_ref, sum_ref):
    block, pair = pl.program_id(0), pl.program_id(1)
    short = info[4] == 1

    def put(rows, parts, add):
        for which, part in enumerate(parts):
            lanes = pl.ds(pl.multiple_of((which * pairs + pair) * PAIR, PAIR), PAIR)
            out_ref[rows, lanes] = part
            summed = jnp.sum(part.astype(F32), axis=0, keepdims=True)
            if add:
                sum_ref[0, :, lanes] += summed
            else:
                sum_ref[0, :, lanes] = summed

    @pl.when(jnp.logical_not(short))
    def _():
        put(
            slice(None),
            attend_back_tile(
                q_ref[...], k_ref[...], v_ref[...], gc_ref[...], lse_ref[0, 0], info[5 + block]
            ),
            False,
        )

    @pl.when(short)
    def _():
        for sub in range(LONG // SHORT):
            at = slice(sub * SHORT, (sub + 1) * SHORT)
            length = info[5 + block * (LONG // SHORT) + sub]
            put(
                at,
                attend_back_tile(
                    q_ref[at, :], k_ref[at, :], v_ref[at, :], gc_ref[at, :], lse_ref[0, 0, :, at], length
                ),
                sub > 0,
            )


def attend_specs(width):
    pairs = width // PAIR
    return [
        pl.BlockSpec((LONG, PAIR), lambda b, p, info, k=k: (b, p + k * pairs)) for k in range(3)
    ]


def attend(info, qkv, deps=()):
    rows, width = qkv.shape[0], qkv.shape[1] // 3
    blocks, pairs = rows // LONG, width // PAIR
    tile = pl.BlockSpec((LONG, PAIR), lambda b, p, info: (b, p))
    lse_tile = pl.BlockSpec((1, 1, 2, LONG), lambda b, p, info: (b, p, 0, 0))
    return call(
        attend_kernel,
        "attend",
        info,
        (blocks, pairs),
        (qkv, qkv, qkv),
        attend_specs(width),
        [shaped((rows, width), BF), shaped((blocks, pairs, 2, LONG), F32)],
        [tile, lse_tile],
        flops=4 * rows * LONG * width,
        moved=8 * rows * width,
        limit=14,
        exps=rows * LONG * width // HEAD,
        deps=deps,
    )


def attend_back(info, qkv, grad_c, lse, deps=()):
    rows, width = grad_c.shape
    blocks, pairs = rows // LONG, width // PAIR
    tile = pl.BlockSpec((LONG, PAIR), lambda b, p, info: (b, p))
    lse_tile = pl.BlockSpec((1, 1, 2, LONG), lambda b, p, info: (b, p, 0, 0))
    grads, sums = call(
        functools.partial(attend_back_kernel, pairs),
        "attend_back",
        info,
        (blocks, pairs),
        (qkv, qkv, qkv, grad_c, lse),
        attend_specs(width) + [tile, lse_tile],
        [shaped((rows, 3 * width), BF), shaped((blocks, 1, 3 * width), F32)],
        [
            pl.BlockSpec((LONG, 3 * width), lambda b, p, info: (b, 0)),
            pl.BlockSpec((1, 1, 3 * width), lambda b, p, info: (b, 0, 0)),
        ],
        flops=10 * rows * LONG * width,
        moved=14 * rows * width,
        limit=18,
        exps=rows * LONG * width // HEAD,
        deps=deps,
    )
    return grads, sums


def ffn_forward_kernel(
    chunk, place, h_ref, up_ref, bias_ref, down_ref, acc_in, act_ref, slope_ref, acc_ref
):
    @pl.when(pl.program_id(0) == 0)
    def _():
        acc_ref[...] = acc_in[...]

    size = up_ref.shape[1]
    first = bias_ref.shape[1] - pl.num_programs(0) * size
    bias = bias_ref[:, pl.ds(pl.multiple_of(first + pl.program_id(0) * size, PAIR), size)]
    for start in range(0, h_ref.shape[0], chunk):
        at = slice(start, start + chunk)
        pre = dot_nn(h_ref[at, :], up_ref[...]) + bias
        cumulative = 0.5 + 0.5 * lax.erf(pre * (1.0 / math.sqrt(2.0)))
        density = jnp.exp(-0.5 * pre * pre) * (1.0 / math.sqrt(2.0 * math.pi))
        act = (pre * cumulative).astype(BF)
        act_ref[at, :] = act
        slope_ref[at, :] = (cumulative + pre * density).astype(BF)
        acc_ref[at, :] += dot_nn(act, down_ref[...])


def ffn_forward(place, hidden_low, up, bias, down, acc):
    rows, width = hidden_low.shape
    local = up.shape[1]
    tiles = 3
    size = local // tiles
    piece = pl.BlockSpec((rows, size), lambda i, p: (0, i))
    return call(
        functools.partial(ffn_forward_kernel, min(rows, 512)),
        "ffn_forward",
        place,
        (tiles,),
        (hidden_low, up, bias, down, acc),
        [
            whole_block((rows, width)),
            pl.BlockSpec((width, size), lambda i, p: (0, i)),
            whole_block(bias.shape),
            pl.BlockSpec((size, width), lambda i, p: (i, 0)),
            whole_block((rows, width)),
        ],
        [shaped((rows, local), BF), shaped((rows, local), BF), shaped((rows, width), F32)],
        [piece, piece, whole_block((rows, width))],
        flops=4 * rows * width * local,
        moved=20 * rows * width,
        exps=rows * local,
        limit=22,
    )


def ffn_backward_kernel(chunk, place, g_ref, slope_ref, up_ref, down_ref, acc_in, pre_ref, acc_ref, sum_ref):
    @pl.when(pl.program_id(0) == 0)
    def _():
        acc_ref[...] = acc_in[...]

    total = None
    for start in range(0, g_ref.shape[0], chunk):
        at = slice(start, start + chunk)
        grad_act = dot_nt(g_ref[at, :], down_ref[...])
        low = (grad_act * slope_ref[at, :].astype(F32)).astype(BF)
        pre_ref[at, :] = low
        part = jnp.sum(low.astype(F32), axis=0, keepdims=True)
        total = part if total is None else total + part
        acc_ref[at, :] += dot_nt(low, up_ref[...])
    size = pre_ref.shape[1]
    sum_ref[:, pl.ds(pl.multiple_of(pl.program_id(0) * size, size), size)] = total


def ffn_backward(place, grad_low, slope, up, down, acc, deps=()):
    rows, width = grad_low.shape
    local = up.shape[1]
    tiles = 3
    size = local // tiles
    piece = pl.BlockSpec((rows, size), lambda i, p: (0, i))
    return call(
        functools.partial(ffn_backward_kernel, min(rows, 512)),
        "ffn_backward",
        place,
        (tiles,),
        (grad_low, slope, up, down, acc),
        [
            whole_block((rows, width)),
            piece,
            pl.BlockSpec((width, size), lambda i, p: (0, i)),
            pl.BlockSpec((size, width), lambda i, p: (i, 0)),
            whole_block((rows, width)),
        ],
        [shaped((rows, local), BF), shaped((rows, width), F32), shaped((1, local), F32)],
        [piece, whole_block((rows, width)), whole_block((1, local))],
        flops=4 * rows * width * local,
        limit=22,
        deps=deps,
    )


def spread(value, place, put):
    count = 8
    size = value.shape[0] // count
    step = 16 if size % 16 == 0 else 8
    for k in range(count):
        at = pl.ds(pl.multiple_of((k ^ place[2]) * size, step), size)
        put(at, value[k * size : (k + 1) * size].astype(BF))


def ffn_grad_kernel(paired, place, *refs):
    left, right = (refs[:2], refs[2:3]) if paired == "left" else (refs[:1], refs[1:3])
    step = pl.program_id(0)
    for half in range(2):
        for far in range(2):

            @pl.when(step == 2 * (1 - far) + half)
            def _():
                out = refs[3 if far else 4]

                def put(at, part):
                    out[0, at, :] = part

                spread(dot_tn(left[half % len(left)][...], right[half % len(right)][...]), place, put)


def ffn_grad(name, place, pair, shared, paired, deps=()):
    rows, size = pair[0].shape[0], pair[0].shape[1] // 2
    width = shared.shape[1]
    own = pl.BlockSpec((rows, size), lambda i, p: (0, jnp.where(i < 2, 1 - p[0], p[0])))
    oth = pl.BlockSpec((rows, size), lambda i, p: (0, jnp.where(i < 3, 1 - p[0], p[0])))
    whole = whole_block(shared.shape)
    ins, specs = ((*pair, shared), [own, oth, whole]) if paired == "left" else ((shared, *pair), [whole, own, oth])
    shape = (2, size, width) if paired == "left" else (2, width, size)
    return call(
        functools.partial(ffn_grad_kernel, paired),
        name,
        place,
        (4,),
        ins,
        specs,
        [shaped(shape, BF)] * 2,
        [
            pl.BlockSpec((1, *shape[1:]), lambda i, p: (jnp.minimum(i, 1), 0, 0)),
            pl.BlockSpec((1, *shape[1:]), lambda i, p: (jnp.maximum(i - 2, 0), 0, 0)),
        ],
        flops=8 * rows * size * width,
        limit=24,
        deps=deps,
    )


def attn_grad_kernel(place, x_ref, grads_ref, c_ref, a_ref, far_ref, near_ref):
    wide = grads_ref.shape[1]
    for far, out in ((True, far_ref), (False, near_ref)):

        @pl.when(pl.program_id(0) == (0 if far else 1))
        def _():
            values = (dot_tn(x_ref[...], grads_ref[...]), dot_tn(c_ref[...], a_ref[...]))
            for start, value in zip((0, wide), values):
                lanes = slice(start, start + value.shape[1])

                def put(at, part):
                    out[at, lanes] = part

                spread(value, place, put)


def attn_grad(place, tokens, grads, context, out_grad, deps=()):
    rows, width = out_grad.shape
    tall = width // 2
    tile = lambda i, p: jnp.where(i == 0, 1 - p[0], p[0])
    wide = grads.shape[1] + tall
    return call(
        attn_grad_kernel,
        "attn_grad",
        place,
        (2,),
        (tokens, grads, context, out_grad),
        [
            pl.BlockSpec((rows, tall), lambda i, p: (p[3], tile(i, p))),
            whole_block(grads.shape),
            whole_block(context.shape),
            pl.BlockSpec((rows, tall), lambda i, p: (0, tile(i, p))),
        ],
        [shaped((tall, wide), BF)] * 2,
        [whole_block((tall, wide))] * 2,
        flops=4 * rows * tall * wide,
        moved=2 * (rows * (wide + 3 * tall) + 2 * tall * wide),
        limit=18,
        deps=deps,
    )


def pack_kernel(place, qkv_ref, proj_ref, up_ref, down_ref, attn_ref, *ffn_refs):
    wide = qkv_ref.shape[2]
    for k in range(3):
        attn_ref[:, k * wide : (k + 1) * wide] = qkv_ref[k]
    attn_ref[:, 3 * wide :] = proj_ref[...]
    tall = up_ref.shape[0] // 2
    for half, out in enumerate(ffn_refs):
        at = slice(half * tall, (half + 1) * tall)
        out[:tall, :] = up_ref[at, :]
        out[tall:, :] = down_ref[at, :]


def pack(place, qkv, proj, up, down):
    _, width, wide = qkv.shape
    heads, hidden = proj.shape[0], up.shape[1]
    quarter = lambda i, p: (2 * p[0] + p[1], 0)
    corner = lambda i, p: (p[1], p[0])
    rows = width // 4
    attn, ffn = (rows, 3 * wide + width // 2), (width // 4 + hidden // 8, width)
    qkv, proj, up, down = [pltpu.with_memory_space_constraint(a, pltpu.HBM) for a in (qkv, proj, up, down)]
    return call(
        pack_kernel,
        "pack",
        place,
        (1,),
        (qkv, proj, up, down),
        [
            pl.BlockSpec((3, rows, wide), lambda i, p: (0, 2 * p[0] + p[1], 0)),
            pl.BlockSpec((heads // 2, width // 2), corner),
            pl.BlockSpec((width // 2, hidden // 2), corner),
            pl.BlockSpec((hidden // 4, width), quarter),
        ],
        [shaped(attn, BF), shaped(ffn, BF), shaped(ffn, BF)],
        [whole_block(attn), whole_block(ffn), whole_block(ffn)],
        moved=8 * MIB,
    )


def join_attn_kernel(place, *refs):
    qkv_ref, proj_ref = refs[4:]
    wide = qkv_ref.shape[2]
    rows, side = refs[0].shape[0], refs[0].shape[1] - 3 * wide
    for r in range(4):
        c, y = (r >> 1) ^ place[0], (r & 1) ^ place[1]
        for k in range(3):
            qkv_ref[k, pl.ds(pl.multiple_of((2 * c + y) * rows, rows), rows), :] = refs[r][
                :, k * wide : (k + 1) * wide
            ]
        proj_ref[
            pl.ds(pl.multiple_of(y * rows, rows), rows), pl.ds(pl.multiple_of(c * side, side), side)
        ] = refs[r][:, 3 * wide :]


def join_attn(place, pieces, wide):
    rows, lanes = pieces[0].shape
    side = lanes - 3 * wide
    shapes = [(3, 4 * rows, wide), (2 * rows, 2 * side)]
    return call(
        join_attn_kernel,
        "join_attn",
        place,
        (1,),
        pieces,
        [whole_block(pieces[0].shape)] * 4,
        [shaped(s, BF) for s in shapes],
        [whole_block(s) for s in shapes],
    )


def join_ffn_kernel(place, *refs):
    up_ref, down_ref = refs[8:]
    rows, lanes = refs[0].shape
    tall = rows // 2
    for r in range(4):
        c, y = (r >> 1) ^ place[0], (r & 1) ^ place[1]
        for half in range(2):
            source = refs[4 * half + r]
            up_ref[
                pl.ds(pl.multiple_of((2 * y + half) * tall, tall), tall),
                pl.ds(pl.multiple_of(c * lanes, lanes), lanes),
            ] = source[:tall, :]
            down_ref[
                pl.ds(pl.multiple_of((4 * c + 2 * y + half) * tall, tall), tall), :
            ] = source[tall:, :]


def join_ffn(place, first, second):
    rows, lanes = first[0].shape
    shapes = [(2 * rows, 2 * lanes), (4 * rows, lanes)]
    return call(
        join_ffn_kernel,
        "join_ffn",
        place,
        (1,),
        [*first, *second],
        [whole_block(first[0].shape)] * 8,
        [shaped(s, BF) for s in shapes],
        [whole_block(s) for s in shapes],
    )


def rows_kernel(place, *refs):
    out_ref = refs[4]
    for step in range(4):

        @pl.when(pl.program_id(0) == step)
        def _():
            out_ref[...] = refs[step][...].astype(out_ref.dtype)


def both_rows(name, place, parts, dtype, deps=()):
    rows, width = parts[0].shape
    return call(
        rows_kernel,
        name,
        place,
        (4,),
        parts,
        [whole_block((rows, width))] * 4,
        [shaped((4 * rows, width), dtype)],
        [pl.BlockSpec((rows, width), lambda i, p: (i ^ (2 * p[3]), 0))],
        deps=deps,
        final=True,
    )[0]


def small_kernel(place, one_ref, two_ref, *refs):
    for half in range(2):
        attn_ref, up_ref, out_ref = refs[half], refs[2 + half], refs[4 + half]
        local, width = attn_ref.shape[2] // 3, one_ref.shape[1]
        attn = jnp.sum(attn_ref[...], axis=0)
        rows = [one_ref[:3, :], two_ref[:3, :], jnp.concatenate([attn[:, :local], attn[:, 2 * local :]], axis=1)]
        rows += [up_ref[:, k * width : (k + 1) * width] for k in range(up_ref.shape[1] // width)]
        used = sum(r.shape[0] for r in rows)
        out_ref[:used, :] = jnp.concatenate(rows, axis=0)
        out_ref[used:, :] = jnp.zeros((out_ref.shape[0] - used, width), F32)


def small_sums(place, one, two, attn, up, deps=()):
    ins = (one, two, *attn, *up)
    shape = (16, one.shape[1])
    return call(
        small_kernel,
        "small_sums",
        place,
        (1,),
        ins,
        [whole_block(a.shape) for a in ins],
        [shaped(shape, F32)] * 2,
        [whole_block(shape)] * 2,
        deps=deps,
    )


def sums_kernel(outs, count, place, *refs):
    for out_ref, pieces in zip(refs[count:], outs):
        for out_at, parts in pieces:
            total = refs[parts[0][0]][parts[0][1]].astype(F32)
            for which, at in parts[1:]:
                total = total + refs[which][at].astype(F32)
            out_ref[out_at] = total.astype(out_ref.dtype)


def sums(name, place, outs, deps=()):
    arrays = []

    def number(array):
        for k, other in enumerate(arrays):
            if other is array:
                return k
        arrays.append(array)
        return len(arrays) - 1

    plan = [
        [(out_at, [(number(array), at) for array, at in parts]) for out_at, parts in pieces]
        for _, pieces in outs
    ]
    kinds = [pieces[0][1][0][0].dtype for _, pieces in outs]
    return call(
        functools.partial(sums_kernel, plan, len(arrays)),
        name,
        place,
        (1,),
        arrays,
        [whole_block(a.shape) for a in arrays],
        [shaped(shape, kind) for (shape, _), kind in zip(outs, kinds)],
        [whole_block(shape) for shape, _ in outs],
        deps=deps,
        weight=SUM_WEIGHT,
    )


def tile_out_kernel(place, *refs):
    out_ref = refs[4]
    step = pl.program_id(0)
    size = refs[0].shape[0] // 4

    def work(low, high):
        for k in range(8):
            for h in range(2):

                @pl.when((k >> 2) ^ (place[2] >> 2) == h)
                def _():
                    at = pl.ds(pl.multiple_of(((k ^ place[2]) & 3) * size, size), size)
                    out_ref[k * size : (k + 1) * size, :] = (low, high)[h][at, :].astype(F32)

    pl.when(step == 0)(lambda: work(refs[0], refs[1]))
    pl.when(step == 1)(lambda: work(refs[2], refs[3]))


def tile_out(name, place, parts, across, deps=()):
    rows, width = parts[0].shape
    tall = 2 * rows
    shape = (tall, 2 * width) if across else (2 * tall, width)
    turn = (lambda i, p: (0, i ^ p[0])) if across else (lambda i, p: (i ^ p[0], 0))
    return call(
        tile_out_kernel,
        name,
        place,
        (2,),
        parts,
        [whole_block(parts[0].shape)] * 4,
        [shaped(shape, F32)],
        [pl.BlockSpec((tall, width), turn)],
        deps=deps,
        final=True,
    )[0]


def attn_out_kernel(place, *refs):
    qkv_ref, proj_ref = refs[4:]
    step = pl.program_id(0)
    size = refs[0].shape[0] // 4
    count, _, lanes = qkv_ref.shape

    def work(low, high):
        for k in range(8):
            for h in range(2):

                @pl.when((k >> 2) ^ (place[2] >> 2) == h)
                def _():
                    at = pl.ds(pl.multiple_of(((k ^ place[2]) & 3) * size, size), size)
                    source = (low, high)[h]
                    for n in range(count):
                        qkv_ref[n, k * size : (k + 1) * size, :] = source[
                            at, n * lanes : (n + 1) * lanes
                        ].astype(F32)
                    proj_ref[k * size : (k + 1) * size, :] = source[at, count * lanes :].astype(F32)

    pl.when(step == 0)(lambda: work(refs[0], refs[1]))
    pl.when(step == 1)(lambda: work(refs[2], refs[3]))


def attn_out(place, parts, count, lanes, deps=()):
    rows, wide = parts[0].shape
    tall = 2 * rows
    side = wide - count * lanes
    return call(
        attn_out_kernel,
        "attn_out",
        place,
        (2,),
        parts,
        [whole_block(parts[0].shape)] * 4,
        [shaped((count, 2 * tall, lanes), F32), shaped((tall, 2 * side), F32)],
        [
            pl.BlockSpec((count, tall, lanes), lambda i, p: (0, i ^ p[0], 0)),
            pl.BlockSpec((tall, side), lambda i, p: (0, i ^ p[0])),
        ],
        deps=deps,
        final=True,
    )


CORE, ROW, NEAR, FAR = range(4)


def swap_tensor(values):
    count = lax.axis_size("tensor")
    return lax.ppermute(values, "tensor", [(i, (i + 1) % count) for i in range(count)])


def swap(values, bit):
    count = lax.axis_size("dp")
    return lax.ppermute(values, "dp", [(i, i ^ (1 << bit)) for i in range(count)])


def dp_bits():
    return lax.axis_size("dp").bit_length() - 1


def after(values, *others):
    return lax.optimization_barrier((values, *others))[0]


def add(*parts):
    total = parts[0].astype(F32)
    for part in parts[1:]:
        total = total + part.astype(F32)
    return total.astype(BF)


def vector(ref):
    return ref[...].reshape(1, -1)


def average(values):
    return jnp.sum(values, axis=-1, keepdims=True) * (1.0 / values.shape[-1])


def normed(values):
    centered = values - average(values)
    inverse = lax.rsqrt(average(centered * centered) + 1e-05)
    return centered * inverse, inverse


def norm_back(upstream, scaled, inverse, gain):
    through = upstream * gain
    return inverse * (through - average(through) - scaled * average(through * scaled))


def column_sums(ref, parts):
    summed = [jnp.sum(part, axis=0, keepdims=True) for part in parts]
    summed.append(jnp.zeros((ref.shape[0] - len(parts), ref.shape[1]), F32))
    summed = jnp.concatenate(summed, axis=0)

    @pl.when(pl.program_id(0) == 0)
    def _():
        ref[...] = summed

    @pl.when(pl.program_id(0) > 0)
    def _():
        ref[...] += summed


def kept_column(place, groups):
    row = lax.broadcasted_iota(jnp.int32, (SHORT, 1), 0)
    first = 13 + pl.program_id(0) * groups
    return jnp.concatenate([(row < place[first + g]).astype(F32) for g in range(groups)], axis=0) > 0.5


def qkv_kernel(place, x_ref, weight_ref, bias_ref, out_ref):
    which, local = pl.program_id(0), weight_ref.shape[2]
    factor = jnp.where(which == 0, 1.0 / math.sqrt(HEAD), 1.0)
    value_bias = jnp.where(which == 2, bias_ref[:, local : 2 * local], 0.0)
    bias = jnp.where(which == 0, bias_ref[:, :local], value_bias)
    out_ref[...] = ((dot_nn(x_ref[...], weight_ref[0]) + bias) * factor).astype(BF)


def project_qkv(place, tokens, rows, weight, bias):
    count, width, local = weight.shape
    return call(
        qkv_kernel,
        "project_qkv",
        place,
        (count,),
        (tokens, weight, bias),
        [
            pl.BlockSpec((rows, width), lambda k, p: (p[3], 0)),
            pl.BlockSpec((1, width, local), lambda k, p: (k, 0, 0)),
            whole_block(bias.shape),
        ],
        [shaped((rows, count * local), BF)],
        [pl.BlockSpec((rows, local), lambda k, p: (0, k))],
        flops=2 * rows * width * count * local,
    )[0]


def first_norm_kernel(
    place, x_ref, c_own, c_oth, w_own, w_oth, bias, gain, shift, hidden_ref, low_ref, scaled_ref, inverse_ref
):
    attended = dot_nn(c_own[...], w_own[...]) + dot_nn(c_oth[...], w_oth[...])
    scaled, inverse = normed(x_ref[...].astype(F32) + attended + vector(bias))
    hidden = scaled * vector(gain) + vector(shift)
    hidden_ref[...] = hidden
    low_ref[...] = hidden.astype(BF)
    scaled_ref[...] = scaled
    inverse_ref[...] = inverse


def first_norm(place, tokens, context, proj, vectors):
    rows, local = context[0].shape
    width = tokens.shape[1]
    steps = 4
    size = rows // steps
    tile = pl.BlockSpec((size, width), lambda i, p: (i, 0))
    part = pl.BlockSpec((size, local), lambda i, p: (i, 0))
    return call(
        first_norm_kernel,
        "first_norm",
        place,
        (steps,),
        (tokens, *context, *proj, *vectors),
        [
            pl.BlockSpec((size, width), lambda i, p: (steps * p[3] + i, 0)),
            part,
            part,
            whole_block((local, width)),
            whole_block((local, width)),
            *[whole_block((width,))] * 3,
        ],
        [
            shaped((rows, width), F32),
            shaped((rows, width), BF),
            shaped((rows, width), F32),
            shaped((rows, 1), F32),
        ],
        [tile, tile, tile, pl.BlockSpec((size, 1), lambda i, p: (i, 0))],
        flops=4 * rows * width * local,
        moved=14 * rows * width,
    )


def put_rows(low_ref, high_ref, value):
    first = pl.program_id(0) < pl.num_programs(0) // 2

    @pl.when(first)
    def _():
        low_ref[...] = value

    @pl.when(jnp.logical_not(first))
    def _():
        high_ref[...] = value


def two_arrays(size, width, steps):
    half = steps // 2
    return [
        pl.BlockSpec((size, width), lambda i, p: (jnp.minimum(i, half - 1), 0)),
        pl.BlockSpec((size, width), lambda i, p: (jnp.maximum(i - half, 0), 0)),
    ]


def second_norm_kernel(
    place, acc_ref, x_ref, up_ref, bias, gain_ref, shift, result_low, result_high, grad_ref, low_ref, sum_ref
):
    keep = kept_column(place, acc_ref.shape[0] // SHORT)
    gain = vector(gain_ref)
    scaled, inverse = normed(acc_ref[...] + vector(bias))
    result = scaled * gain + vector(shift)
    put_rows(result_low, result_high, jnp.where(keep, result, x_ref[...].astype(F32)).astype(BF))
    upstream = jnp.where(keep, up_ref[...].astype(F32), 0.0)
    grad = norm_back(upstream, scaled, inverse, gain)
    grad_ref[...] = grad
    low_ref[...] = grad.astype(BF)
    column_sums(sum_ref, (grad, upstream * scaled, upstream))


def second_norm(place, acc, tokens, cotangent, vectors):
    rows, width = acc.shape
    steps = 4
    size = rows // steps
    tile = pl.BlockSpec((size, width), lambda i, p: (i, 0))
    far = pl.BlockSpec((size, width), lambda i, p: (steps * p[3] + i, 0))
    return call(
        second_norm_kernel,
        "second_norm",
        place,
        (steps,),
        (acc, tokens, cotangent, *vectors),
        [tile, far, far, *[whole_block((width,))] * 3],
        [shaped((rows // 2, width), BF)] * 2
        + [shaped((rows, width), F32), shaped((rows, width), BF), shaped((8, width), F32)],
        [*two_arrays(size, width, steps), tile, tile, whole_block((8, width))],
        moved=16 * rows * width,
    )


def first_back_kernel(
    place, grad_in, scaled_ref, inverse_ref, up_ref, w_own, w_oth, gain, base_ref, low_ref, c_own, c_oth, sum_ref
):
    keep = kept_column(place, grad_in.shape[0] // SHORT)
    upstream, scaled = grad_in[...], scaled_ref[...]
    grad = norm_back(upstream, scaled, inverse_ref[...], vector(gain))
    low = grad.astype(BF)
    base_ref[...] = grad + jnp.where(keep, 0.0, up_ref[...].astype(F32))
    low_ref[...] = low
    c_own[...] = dot_nt(low, w_own[...]).astype(BF)
    c_oth[...] = dot_nt(low, w_oth[...]).astype(BF)
    column_sums(sum_ref, (grad, upstream * scaled, upstream))


def first_back(place, grad, scaled, inverse, cotangent, proj, gain, deps=()):
    rows, width = grad.shape
    local = proj[0].shape[0]
    steps = 4
    size = rows // steps
    tile = pl.BlockSpec((size, width), lambda i, p: (i, 0))
    part = pl.BlockSpec((size, local), lambda i, p: (i, 0))
    return call(
        first_back_kernel,
        "first_back",
        place,
        (steps,),
        (grad, scaled, inverse, cotangent, *proj, gain),
        [
            tile,
            tile,
            pl.BlockSpec((size, 1), lambda i, p: (i, 0)),
            pl.BlockSpec((size, width), lambda i, p: (steps * p[3] + i, 0)),
            whole_block((local, width)),
            whole_block((local, width)),
            whole_block((width,)),
        ],
        [
            shaped((rows, width), F32),
            shaped((rows, width), BF),
            shaped((rows, local), BF),
            shaped((rows, local), BF),
            shaped((8, width), F32),
        ],
        [tile, tile, part, part, whole_block((8, width))],
        flops=4 * rows * width * local,
        moved=18 * rows * width,
        deps=deps,
    )


def input_grad_kernel(place, base_ref, g_own, g_oth, w_own, w_oth, low_ref, high_ref):
    count, _, local = w_own.shape
    total = base_ref[...]
    for grads, weight in ((g_own, w_own), (g_oth, w_oth)):
        for k in range(count):
            total = total + dot_nt(grads[:, k * local : (k + 1) * local], weight[k])
    put_rows(low_ref, high_ref, total.astype(BF))


def input_grad(place, base, grads, weights, deps=()):
    rows, width = base.shape
    wide = grads[0].shape[1]
    steps = 2
    size = rows // steps
    tile = pl.BlockSpec((size, width), lambda i, p: (i, 0))
    part = pl.BlockSpec((size, wide), lambda i, p: (i, 0))
    return call(
        input_grad_kernel,
        "input_grad",
        place,
        (steps,),
        (base, *grads, *weights),
        [tile, part, part, whole_block(weights[0].shape), whole_block(weights[0].shape)],
        [shaped((rows // 2, width), BF)] * 2,
        two_arrays(size, width, steps),
        flops=4 * rows * width * wide,
        deps=deps,
    )


def body(
    tokens,
    qkv_weight,
    qv_bias,
    proj_weight,
    proj_bias,
    first_gain,
    first_shift,
    up_weight,
    up_bias,
    down_weight,
    down_bias,
    second_gain,
    second_shift,
    cotangent,
    bucket,
    lengths,
    dropped,
):
    token_count, width = tokens.shape
    rows = token_count // lax.axis_size("tensor")
    side = lax.axis_index("tensor")
    index = lax.axis_index("dp")
    core, row, near, far = [(index >> bit) & 1 for bit in range(4)]
    local = qkv_weight.shape[2]
    hidden_count = up_weight.shape[1]

    groups = rows // SHORT
    is_short = bucket[0] == 1
    first_slot = jnp.where(is_short, side * groups, side * (rows // LONG))
    slot_lengths = lax.dynamic_slice_in_dim(lengths, first_slot, groups, 0)
    slot_drops = lax.dynamic_slice_in_dim(dropped, first_slot, groups, 0)
    limits = jnp.where(slot_drops == 0, slot_lengths, 0)
    per = LONG // SHORT
    long_limits = jnp.repeat(limits[: groups // per], per) - SHORT * (jnp.arange(groups) % per)
    limits = jnp.where(is_short, limits, long_limits)
    place = jnp.concatenate(
        [
            jnp.stack([core, row, 4 * row + 2 * near + far, side, bucket[0]]),
            slot_lengths,
            limits,
        ]
    ).astype(jnp.int32)
    qkv_own = jnp.transpose(qkv_weight, (1, 0, 2))
    attn_piece, ffn_one, ffn_two = pack(place, qkv_own, proj_weight, up_weight, down_weight)
    biases = jnp.concatenate([qv_bias.reshape(1, -1), up_bias.reshape(1, -1)], axis=1)
    attn_x = swap_tensor(attn_piece)
    qkv = [project_qkv(place, tokens, rows, qkv_own, biases)]
    c_own, lse_own = attend(place, qkv[0])
    attn_x = after(attn_x, c_own)
    attn_y = swap(attn_x, ROW)
    ffn_x = [swap_tensor(after(ffn_one, c_own))]
    biases_oth = swap_tensor(after(biases, c_own))
    ffn_x.append(swap_tensor(after(ffn_two, attn_x)))
    attn_core = swap(attn_x, CORE)
    ffn_x[0] = after(ffn_x[0], attn_y)
    ffn_y = [swap(ffn_x[0], ROW)]
    qkv_oth, proj_oth = join_attn(place, [attn_x, attn_y, attn_core, swap(attn_y, CORE)], local)
    qkv_w, proj_w = (qkv_own, qkv_oth), (proj_weight, proj_oth)
    qkv.append(project_qkv(place, tokens, rows, qkv_oth, biases_oth))
    c_oth, lse_oth = attend(place, qkv[1])
    ffn_x[1] = after(ffn_x[1], c_oth)
    context, lse = (c_own, c_oth), (lse_own, lse_oth)
    ffn_y[0] = after(ffn_y[0], c_oth)
    ffn_y.append(swap(ffn_x[1], ROW))
    ffn_core = [swap(after(v, c_oth), CORE) for v in ffn_x]
    hidden, hidden_low, scaled, inverse = first_norm(
        place, tokens, context, proj_w, (proj_bias, first_gain, first_shift)
    )
    act_own, slope_own, acc = ffn_forward(place, hidden_low, up_weight, biases, down_weight, hidden)
    ffn_y[1] = after(ffn_y[1], act_own)
    first, second = [
        [ffn_x[k], ffn_y[k], ffn_core[k], swap(ffn_y[k], CORE)] for k in range(2)
    ]
    up_oth, down_oth = join_ffn(place, first, second)
    act_oth, slope_oth, acc = ffn_forward(place, hidden_low, up_oth, biases_oth, down_oth, acc)
    *result_own, grad_second, branch_grad, sums_two = second_norm(
        place, acc, tokens, cotangent, (down_bias, second_gain, second_shift)
    )
    result_x = [swap_tensor(result_own[0])]

    def part(pair, half, low, high, first, last):
        at = (slice(low, high), slice(first, last))
        return (pair[half], at) if isinstance(pair, tuple) else (pair, (half, *at))

    def first_left(near, got, size, wide):
        pieces = [part(p, 1, 0, size, 0, wide) for p in (near, got)]
        return ((size, wide), [((slice(None), slice(None)), pieces)])

    def first_right(near, got, size, wide):
        return (
            (size // 2, 2 * wide),
            [
                (
                    (slice(None), slice(h * wide, (h + 1) * wide)),
                    [part(p, h, size // 2, size, wide, 2 * wide) for p in (near, got)],
                )
                for h in range(2)
            ],
        )

    def second_left(near, got, left, size, wide):
        return [
            (
                (size // 2, wide),
                [
                    (
                        (slice(None), slice(None)),
                        [part(p, 0, low, low + size // 2, 0, wide) for p in (near, got)]
                        + [(left, (slice(low, low + size // 2), slice(None)))],
                    )
                ],
            )
            for low in (0, size // 2)
        ]

    def second_right(near, got, right, size, wide):
        return [
            (
                (size // 2, wide),
                [
                    (
                        (slice(None), slice(None)),
                        [part(p, h, 0, size // 2, wide, 2 * wide) for p in (near, got)]
                        + [(right, (slice(None), slice(h * wide, (h + 1) * wide)))],
                    )
                ],
            )
            for h in range(2)
        ]

    def third(keeps, received):
        size, wide = keeps[0].shape
        return [
            (
                (size // 2, 2 * wide),
                [
                    (
                        (slice(None), slice(k * wide, (k + 1) * wide)),
                        [(a, (slice(low, low + size // 2), slice(None))) for a in (keeps[k], received[k])],
                    )
                    for k in range(2)
                ],
            )
            for low in (0, size // 2)
        ]

    def fourth(keep, received):
        size, wide = keep.shape
        return [
            (
                (size // 2, wide),
                [((slice(None), slice(None)), [(a, (slice(low, low + size // 2), slice(None))) for a in (keep, received)])],
            )
            for low in (0, size // 2)
        ]

    everything = (slice(None), slice(None))

    def plain(*arrays):
        return (arrays[0].shape, [(everything, [(a, everything) for a in arrays])])

    def grown(piece, other):
        size, wide = piece.shape
        return (
            (2 * size, wide),
            [
                ((slice(k * size, (k + 1) * size), slice(None)), [(a, everything)])
                for k, a in enumerate((piece, other))
            ],
        )

    def last_bits(values):
        for bit in range(4, dp_bits()):
            values = add(values, swap(values, bit))
        return values

    size, half = width, width // 2
    down_far, down_near = ffn_grad("down_grad", place, (act_own, act_oth), branch_grad, "left")
    down_got = swap(down_far, CORE)
    pre_own, acc, up_sums_own = ffn_backward(
        place, branch_grad, slope_own, up_weight, down_weight, grad_second, deps=[down_near]
    )
    left, right = sums(
        "sums_1",
        place,
        [first_left(down_near, down_got, size, half), first_right(down_near, down_got, size, half)],
        deps=[pre_own],
    )
    down_left, down_right = swap_tensor(left), swap(right, ROW)
    pre_oth, grad_hidden, up_sums_oth = ffn_backward(
        place, branch_grad, slope_oth, up_oth, down_oth, acc, deps=[left, result_x[0]]
    )
    up_far, up_near = ffn_grad("up_grad", place, (pre_own, pre_oth), hidden_low, "right")
    up_got = swap(up_far, CORE)
    down_keep = [None, None]
    down_keep[0], left, down_keep[1], right = sums(
        "sums_2",
        place,
        [
            *second_left(down_near, down_got, down_left, size, half),
            *second_right(down_near, down_got, down_right, size, half),
        ],
        deps=[up_near],
    )
    down_left, down_right = swap(left, ROW), swap_tensor(right)
    base, out_grad, gc_own, gc_oth, sums_one = first_back(
        place, grad_hidden, scaled, inverse, cotangent, proj_w, first_gain, deps=[left]
    )
    down_keep, down_send, left, right = sums(
        "sums_3",
        place,
        [
            *third(down_keep, (down_left, down_right)),
            first_left(up_near, up_got, size, half),
            first_right(up_near, up_got, size, half),
        ],
        deps=[out_grad],
    )
    down_z = swap(down_send, NEAR)
    up_left, up_right = swap_tensor(left), swap(right, ROW)
    grads_oth, attn_sums_oth = attend_back(place, qkv[1], gc_oth, lse[1], deps=[down_send])
    down_keep, down_send = sums("sums_4", place, fourth(down_keep, down_z), deps=[grads_oth])
    down_f = swap(down_send, FAR)
    far_oth, near_oth = attn_grad(place, tokens, grads_oth, context[1], out_grad, deps=[down_send])
    got_oth = swap(far_oth, CORE)
    up_keep = [None, None]
    up_keep[0], left, up_keep[1], right, down_sum = sums(
        "sums_5",
        place,
        [
            *second_left(up_near, up_got, up_left, size, half),
            *second_right(up_near, up_got, up_right, size, half),
            plain(down_keep, down_f),
        ],
        deps=[far_oth],
    )
    down_sum = last_bits(down_sum)
    up_left, up_right = swap(left, ROW), swap_tensor(right)
    down_a = swap(down_sum, FAR)
    grads_own, attn_sums_own = attend_back(place, qkv[0], gc_own, lse[0], deps=[down_sum])
    wide, tall = near_oth.shape[1] // 2, near_oth.shape[0]
    up_keep, up_send, down_sum, left = sums(
        "sums_6",
        place,
        [
            *third(up_keep, (up_left, up_right)),
            grown(down_sum, down_a),
            first_left((None, near_oth), (None, got_oth), tall, wide),
        ],
        deps=[grads_own],
    )
    up_z = swap(up_send, NEAR)
    down_b = swap(down_sum, NEAR)
    attn_left = swap_tensor(left)
    far_own, near_own = attn_grad(place, tokens, grads_own, context[0], out_grad, deps=[up_send])
    got_own = swap(far_own, CORE)
    small_own, small_oth = small_sums(
        place,
        sums_one,
        sums_two,
        (attn_sums_own, attn_sums_oth),
        (up_sums_own, up_sums_oth),
        deps=[far_own],
    )
    small_x = swap_tensor(small_oth)
    up_keep, up_send, down_sum = sums(
        "sums_7", place, [*fourth(up_keep, up_z), grown(down_sum, down_b)], deps=[small_own]
    )
    up_f = swap(up_send, FAR)
    down_core = swap(down_sum, CORE)
    input_own = input_grad(place, base, (grads_own, grads_oth), qkv_w, deps=[up_send])
    input_x = [swap_tensor(input_own[0])]
    near, got = (near_own, near_oth), (got_own, got_oth)
    right, keep_left, left, up_sum, small = sums(
        "sums_8",
        place,
        [
            first_right(near, got, tall, wide),
            *second_left(near, got, attn_left, tall, wide),
            plain(up_keep, up_f),
            plain(small_own, small_x),
        ],
        deps=[input_own[0]],
    )
    up_sum = last_bits(up_sum)
    attn_right, attn_left = swap(right, ROW), swap(left, ROW)
    up_a, small_r = swap(up_sum, FAR), swap(small, CORE)
    up_sum, small = sums("sums_9", place, [grown(up_sum, up_a), plain(small, small_r)])
    up_b, small_r = swap(up_sum, NEAR), swap(small, ROW)
    keep_right, right = sums(
        "sums_10", place, second_right(near, got, attn_right, tall, wide), deps=[up_sum]
    )
    attn_right = swap_tensor(right)
    down_y = swap(after(down_sum, right), ROW)
    up_sum, small = sums(
        "sums_11", place, [grown(up_sum, up_b), plain(small, small_r)], deps=[right, attn_left]
    )
    up_core, small_r = swap(up_sum, CORE), swap(small, NEAR)
    attn_keep, attn_send = sums(
        "sums_12",
        place,
        third((keep_left, keep_right), (attn_left, attn_right)),
        deps=[up_sum, input_x[0]],
    )
    attn_z = swap(attn_send, NEAR)
    input_x.append(swap_tensor(after(input_own[1], attn_send)))
    attn_keep, attn_send, small = sums(
        "sums_13", place, [*fourth(attn_keep, attn_z), plain(small, small_r)], deps=[down_y]
    )
    attn_f, small_r = swap(attn_send, FAR), swap(small, FAR)
    up_y = swap(after(up_sum, attn_send), ROW)
    down_last = swap(after(down_y, attn_send), CORE)
    (attn_sum,) = sums("sums_14", place, [plain(attn_keep, attn_f)], deps=[small])
    attn_sum = last_bits(attn_sum)
    attn_a = swap(attn_sum, FAR)
    result_x.append(swap_tensor(after(result_own[1], attn_sum)))
    attn_sum, small = sums(
        "sums_15", place, [grown(attn_sum, attn_a), plain(small, small_r)], deps=[input_x[1], up_y]
    )
    for bit in range(4, dp_bits()):
        small = small + swap(small, bit)
    attn_b = swap(attn_sum, NEAR)
    up_last = swap(after(up_y, attn_sum), CORE)
    (attn_sum,) = sums("sums_16", place, [grown(attn_sum, attn_b)])
    attn_y, attn_core = swap(attn_sum, ROW), swap(attn_sum, CORE)
    down_total = tile_out("down_out", place, [down_sum, down_y, down_core, down_last], False, deps=[attn_sum])
    up_total = tile_out("up_out", place, [up_sum, up_y, up_core, up_last], True, deps=[down_total])
    tokens_grad = both_rows("grad_rows", place, [*input_own, *input_x], F32, deps=[up_total])
    attn_y = after(attn_y, tokens_grad)
    attn_last = swap(attn_y, CORE)
    result = both_rows("result_rows", place, [*result_own, *result_x], BF, deps=[attn_y])
    qkv_total, proj_total = attn_out(place, [attn_sum, attn_y, attn_core, attn_last], 3, local, deps=[result])
    bias_total = small[6:9].reshape(-1)
    return (
        result,
        tokens_grad,
        jnp.transpose(qkv_total, (1, 0, 2)),
        bias_total[: 2 * local].reshape(2, local),
        proj_total,
        small[0],
        small[1],
        small[2],
        up_total,
        bias_total[2 * local :],
        down_total,
        small[3],
        small[4],
        small[5],
    )


def solution(mesh):
    rows, columns, whole = P("dp", None), P(None, "tensor"), P()
    return jax.shard_map(
        body,
        mesh=mesh,
        in_specs=(
            rows,
            P(None, None, "tensor"),
            columns,
            P("tensor", None),
            whole,
            whole,
            whole,
            columns,
            P("tensor"),
            P("tensor", None),
            whole,
            whole,
            whole,
            rows,
            P("dp"),
            P("dp"),
            P("dp"),
        ),
        out_specs=(
            rows,
            rows,
            P(None, None, "tensor"),
            columns,
            P("tensor", None),
            whole,
            whole,
            whole,
            columns,
            P("tensor"),
            P("tensor", None),
            whole,
            whole,
            whole,
        ),
        check_vma=False,
    )
```

```python
import functools
import math

import jax
import jax.numpy as jnp
from jax import lax
from jax.experimental import pallas as pl
from jax.experimental.pallas import tpu as pltpu
from jax.sharding import PartitionSpec as P

HEAD = 64
LONG = 512
SHORT = 128
PAIR = 128
NEG = -1e30
BF = jnp.bfloat16
F32 = jnp.float32
MIB = 1024 * 1024
WEIGHT = 40
SUM_WEIGHT = 1


def dot_nn(left, right):
    return lax.dot_general(left, right, (((1,), (0,)), ((), ())), preferred_element_type=F32)


def dot_nt(left, right):
    return lax.dot_general(left, right, (((1,), (1,)), ((), ())), preferred_element_type=F32)


def dot_tn(left, right):
    return lax.dot_general(left, right, (((0,), (0,)), ((), ())), preferred_element_type=F32)


def shaped(shape, dtype):
    return jax.ShapeDtypeStruct(shape, dtype)


def whole_block(shape):
    return pl.BlockSpec(shape, lambda *_: (0,) * len(shape), pipeline_mode=pl.Buffered(1))


def call(kernel, name, place, grid, ins, in_specs, outs, out_specs, flops=0, moved=0, limit=14, aliases=None, exps=0, deps=(), weight=WEIGHT):
    moved = moved or sum(math.prod(a.shape) * a.dtype.itemsize for a in (*ins, *outs))
    if deps:
        place = lax.optimization_barrier((place, *deps))[0]
    return pl.pallas_call(
        kernel,
        grid_spec=pltpu.PrefetchScalarGridSpec(
            num_scalar_prefetch=1, grid=grid, in_specs=in_specs, out_specs=out_specs
        ),
        out_shape=outs,
        compiler_params=pltpu.CompilerParams(vmem_limit_bytes=limit * MIB),
        cost_estimate=pl.CostEstimate(
            flops=weight * flops, bytes_accessed=weight * moved, transcendentals=weight * exps
        ),
        input_output_aliases=aliases or {},
        name=name,
    )(place, *ins)


def head_masks():
    lane = lax.broadcasted_iota(jnp.int32, (1, PAIR), 1)
    return (lane < HEAD, lane >= HEAD)


def only(mask, values):
    return jnp.where(mask, values, jnp.zeros_like(values))


def attend_tile(q, k, v, length):
    size = q.shape[0]
    hide = jnp.where(lax.broadcasted_iota(jnp.int32, (size, 1), 0) < length, 0.0, NEG)
    total = None
    rows = []
    for mask in head_masks():
        scores = dot_nt(k, only(mask, q)) + hide
        top = jnp.max(scores, axis=0, keepdims=True)
        powers = jnp.exp(scores - top)
        summed = jnp.sum(powers, axis=0, keepdims=True)
        probs = (powers * (1.0 / summed)).astype(BF)
        part = dot_tn(only(mask, v), probs)
        total = part if total is None else total + part
        rows.append(top + jnp.log(summed))
    return jnp.transpose(total).astype(BF), jnp.concatenate(rows, axis=0)


def attend_kernel(info, q_ref, k_ref, v_ref, c_ref, lse_ref):
    block = pl.program_id(0)
    short = info[4] == 1

    @pl.when(jnp.logical_not(short))
    def _():
        c, rows = attend_tile(q_ref[...], k_ref[...], v_ref[...], info[5 + block])
        c_ref[...] = c
        lse_ref[0, 0] = rows

    @pl.when(short)
    def _():
        for sub in range(LONG // SHORT):
            at = slice(sub * SHORT, (sub + 1) * SHORT)
            length = info[5 + block * (LONG // SHORT) + sub]
            c, rows = attend_tile(q_ref[at, :], k_ref[at, :], v_ref[at, :], length)
            c_ref[at, :] = c
            lse_ref[0, 0, :, at] = rows


def attend_back_tile(q, k, v, grad_c, lse, length):
    size = q.shape[0]
    hide = jnp.where(lax.broadcasted_iota(jnp.int32, (size, 1), 0) < length, 0.0, NEG)
    dq = dk = dv = None
    for index, mask in enumerate(head_masks()):
        q_own, c_own, k_own = only(mask, q), only(mask, grad_c), only(mask, k)
        scores = dot_nt(k, q_own) + hide
        probs = jnp.exp(scores - lse[index : index + 1, :])
        grad_probs = dot_nt(v, c_own)
        row_dot = jnp.sum(probs * grad_probs, axis=0, keepdims=True)
        grad_scores = (probs * (grad_probs - row_dot)).astype(BF)
        parts = (
            dot_tn(k_own, grad_scores),
            dot_nn(grad_scores, q_own),
            dot_nn(probs.astype(BF), c_own),
        )
        if dq is None:
            dq, dk, dv = parts
        else:
            dq, dk, dv = dq + parts[0], dk + parts[1], dv + parts[2]
    return (jnp.transpose(dq) * (1.0 / math.sqrt(HEAD))).astype(BF), dk.astype(BF), dv.astype(BF)


def attend_back_kernel(pairs, info, q_ref, k_ref, v_ref, gc_ref, lse_ref, out_ref, sum_ref):
    block, pair = pl.program_id(0), pl.program_id(1)
    short = info[4] == 1

    def put(rows, parts, add):
        for which, part in enumerate(parts):
            lanes = pl.ds(pl.multiple_of((which * pairs + pair) * PAIR, PAIR), PAIR)
            out_ref[rows, lanes] = part
            summed = jnp.sum(part.astype(F32), axis=0, keepdims=True)
            if add:
                sum_ref[0, :, lanes] += summed
            else:
                sum_ref[0, :, lanes] = summed

    @pl.when(jnp.logical_not(short))
    def _():
        put(
            slice(None),
            attend_back_tile(
                q_ref[...], k_ref[...], v_ref[...], gc_ref[...], lse_ref[0, 0], info[5 + block]
            ),
            False,
        )

    @pl.when(short)
    def _():
        for sub in range(LONG // SHORT):
            at = slice(sub * SHORT, (sub + 1) * SHORT)
            length = info[5 + block * (LONG // SHORT) + sub]
            put(
                at,
                attend_back_tile(
                    q_ref[at, :], k_ref[at, :], v_ref[at, :], gc_ref[at, :], lse_ref[0, 0, :, at], length
                ),
                sub > 0,
            )


def attend_specs(width):
    pairs = width // PAIR
    return [
        pl.BlockSpec((LONG, PAIR), lambda b, p, info, k=k: (b, p + k * pairs)) for k in range(3)
    ]


def attend(info, qkv, deps=()):
    rows, width = qkv.shape[0], qkv.shape[1] // 3
    blocks, pairs = rows // LONG, width // PAIR
    tile = pl.BlockSpec((LONG, PAIR), lambda b, p, info: (b, p))
    lse_tile = pl.BlockSpec((1, 1, 2, LONG), lambda b, p, info: (b, p, 0, 0))
    return call(
        attend_kernel,
        "attend",
        info,
        (blocks, pairs),
        (qkv, qkv, qkv),
        attend_specs(width),
        [shaped((rows, width), BF), shaped((blocks, pairs, 2, LONG), F32)],
        [tile, lse_tile],
        flops=4 * rows * LONG * width,
        moved=8 * rows * width,
        limit=14,
        exps=rows * LONG * width // HEAD,
        deps=deps,
    )


def attend_back(info, qkv, grad_c, lse, deps=()):
    rows, width = grad_c.shape
    blocks, pairs = rows // LONG, width // PAIR
    tile = pl.BlockSpec((LONG, PAIR), lambda b, p, info: (b, p))
    lse_tile = pl.BlockSpec((1, 1, 2, LONG), lambda b, p, info: (b, p, 0, 0))
    grads, sums = call(
        functools.partial(attend_back_kernel, pairs),
        "attend_back",
        info,
        (blocks, pairs),
        (qkv, qkv, qkv, grad_c, lse),
        attend_specs(width) + [tile, lse_tile],
        [shaped((rows, 3 * width), BF), shaped((blocks, 1, 3 * width), F32)],
        [
            pl.BlockSpec((LONG, 3 * width), lambda b, p, info: (b, 0)),
            pl.BlockSpec((1, 1, 3 * width), lambda b, p, info: (b, 0, 0)),
        ],
        flops=10 * rows * LONG * width,
        moved=14 * rows * width,
        limit=18,
        exps=rows * LONG * width // HEAD,
        deps=deps,
    )
    return grads, sums


def ffn_forward_kernel(
    chunk, place, h_ref, up_ref, bias_ref, down_ref, acc_in, act_ref, slope_ref, acc_ref
):
    @pl.when(pl.program_id(0) == 0)
    def _():
        acc_ref[...] = acc_in[...]

    size = up_ref.shape[1]
    first = bias_ref.shape[1] - pl.num_programs(0) * size
    bias = bias_ref[:, pl.ds(pl.multiple_of(first + pl.program_id(0) * size, PAIR), size)]
    for start in range(0, h_ref.shape[0], chunk):
        at = slice(start, start + chunk)
        pre = dot_nn(h_ref[at, :], up_ref[...]) + bias
        cumulative = 0.5 + 0.5 * lax.erf(pre * (1.0 / math.sqrt(2.0)))
        density = jnp.exp(-0.5 * pre * pre) * (1.0 / math.sqrt(2.0 * math.pi))
        act = (pre * cumulative).astype(BF)
        act_ref[at, :] = act
        slope_ref[at, :] = (cumulative + pre * density).astype(BF)
        acc_ref[at, :] += dot_nn(act, down_ref[...])


def ffn_forward(place, hidden_low, up, bias, down, acc):
    rows, width = hidden_low.shape
    local = up.shape[1]
    tiles = 3
    size = local // tiles
    piece = pl.BlockSpec((rows, size), lambda i, p: (0, i))
    return call(
        functools.partial(ffn_forward_kernel, min(rows, 512)),
        "ffn_forward",
        place,
        (tiles,),
        (hidden_low, up, bias, down, acc),
        [
            whole_block((rows, width)),
            pl.BlockSpec((width, size), lambda i, p: (0, i)),
            whole_block(bias.shape),
            pl.BlockSpec((size, width), lambda i, p: (i, 0)),
            whole_block((rows, width)),
        ],
        [shaped((rows, local), BF), shaped((rows, local), BF), shaped((rows, width), F32)],
        [piece, piece, whole_block((rows, width))],
        flops=4 * rows * width * local,
        moved=20 * rows * width,
        exps=rows * local,
        limit=19,
    )


def ffn_backward_kernel(chunk, place, g_ref, slope_ref, up_ref, down_ref, acc_in, pre_ref, acc_ref, sum_ref):
    @pl.when(pl.program_id(0) == 0)
    def _():
        acc_ref[...] = acc_in[...]

    total = None
    for start in range(0, g_ref.shape[0], chunk):
        at = slice(start, start + chunk)
        grad_act = dot_nt(g_ref[at, :], down_ref[...])
        low = (grad_act * slope_ref[at, :].astype(F32)).astype(BF)
        pre_ref[at, :] = low
        part = jnp.sum(low.astype(F32), axis=0, keepdims=True)
        total = part if total is None else total + part
        acc_ref[at, :] += dot_nt(low, up_ref[...])
    size = pre_ref.shape[1]
    sum_ref[:, pl.ds(pl.multiple_of(pl.program_id(0) * size, size), size)] = total


def ffn_backward(place, grad_low, slope, up, down, acc, deps=(), weight=WEIGHT):
    rows, width = grad_low.shape
    local = up.shape[1]
    tiles = 3
    size = local // tiles
    piece = pl.BlockSpec((rows, size), lambda i, p: (0, i))
    return call(
        functools.partial(ffn_backward_kernel, min(rows, 512)),
        "ffn_backward",
        place,
        (tiles,),
        (grad_low, slope, up, down, acc),
        [
            whole_block((rows, width)),
            piece,
            pl.BlockSpec((width, size), lambda i, p: (0, i)),
            pl.BlockSpec((size, width), lambda i, p: (i, 0)),
            whole_block((rows, width)),
        ],
        [shaped((rows, local), BF), shaped((rows, width), F32), shaped((1, local), F32)],
        [piece, whole_block((rows, width)), whole_block((1, local))],
        flops=4 * rows * width * local,
        limit=19,
        deps=deps,
        weight=weight,
    )


def spread(value, place, put):
    count = 8
    size = value.shape[0] // count
    step = 16 if size % 16 == 0 else 8
    for k in range(count):
        at = pl.ds(pl.multiple_of((k ^ place[2]) * size, step), size)
        put(at, value[k * size : (k + 1) * size].astype(BF))


def ffn_grad_kernel(paired, place, *refs):
    left, right = (refs[:2], refs[2:3]) if paired == "left" else (refs[:1], refs[1:3])
    step = pl.program_id(0)
    for half in range(2):
        for far in range(2):

            @pl.when(step == 2 * (1 - far) + half)
            def _():
                out = refs[3 if far else 4]

                def put(at, part):
                    out[0, at, :] = part

                spread(dot_tn(left[half % len(left)][...], right[half % len(right)][...]), place, put)


def ffn_grad(name, place, pair, shared, paired, deps=()):
    rows, size = pair[0].shape[0], pair[0].shape[1] // 2
    width = shared.shape[1]
    own = pl.BlockSpec((rows, size), lambda i, p: (0, jnp.where(i < 2, 1 - p[0], p[0])))
    oth = pl.BlockSpec((rows, size), lambda i, p: (0, jnp.where(i < 3, 1 - p[0], p[0])))
    whole = whole_block(shared.shape)
    ins, specs = ((*pair, shared), [own, oth, whole]) if paired == "left" else ((shared, *pair), [whole, own, oth])
    shape = (2, size, width) if paired == "left" else (2, width, size)
    return call(
        functools.partial(ffn_grad_kernel, paired),
        name,
        place,
        (4,),
        ins,
        specs,
        [shaped(shape, BF)] * 2,
        [
            pl.BlockSpec((1, *shape[1:]), lambda i, p: (jnp.minimum(i, 1), 0, 0)),
            pl.BlockSpec((1, *shape[1:]), lambda i, p: (jnp.maximum(i - 2, 0), 0, 0)),
        ],
        flops=8 * rows * size * width,
        limit=18,
        deps=deps,
    )


def attn_grad_kernel(place, x_ref, grads_ref, c_ref, a_ref, far_ref, near_ref):
    wide = grads_ref.shape[1]
    for far, out in ((True, far_ref), (False, near_ref)):

        @pl.when(pl.program_id(0) == (0 if far else 1))
        def _():
            values = (dot_tn(x_ref[...], grads_ref[...]), dot_tn(c_ref[...], a_ref[...]))
            for start, value in zip((0, wide), values):
                lanes = slice(start, start + value.shape[1])

                def put(at, part):
                    out[at, lanes] = part

                spread(value, place, put)


def attn_grad(place, tokens, grads, context, out_grad, deps=()):
    rows, width = out_grad.shape
    tall = width // 2
    tile = lambda i, p: jnp.where(i == 0, 1 - p[0], p[0])
    wide = grads.shape[1] + tall
    return call(
        attn_grad_kernel,
        "attn_grad",
        place,
        (2,),
        (tokens, grads, context, out_grad),
        [
            pl.BlockSpec((rows, tall), lambda i, p: (p[3], tile(i, p))),
            whole_block(grads.shape),
            whole_block(context.shape),
            pl.BlockSpec((rows, tall), lambda i, p: (0, tile(i, p))),
        ],
        [shaped((tall, wide), BF)] * 2,
        [whole_block((tall, wide))] * 2,
        flops=4 * rows * tall * wide,
        moved=2 * (rows * (wide + 3 * tall) + 2 * tall * wide),
        limit=18,
        deps=deps,
        weight=1,
    )


def pack_kernel(place, qkv_ref, proj_ref, up_ref, down_ref, attn_ref, *ffn_refs):
    wide = qkv_ref.shape[2]
    for k in range(3):
        attn_ref[:, k * wide : (k + 1) * wide] = qkv_ref[k]
    attn_ref[:, 3 * wide :] = proj_ref[...]
    tall = up_ref.shape[0] // 2
    for half, out in enumerate(ffn_refs):
        at = slice(half * tall, (half + 1) * tall)
        out[:tall, :] = up_ref[at, :]
        out[tall:, :] = down_ref[at, :]


def pack(place, qkv, proj, up, down):
    _, width, wide = qkv.shape
    heads, hidden = proj.shape[0], up.shape[1]
    quarter = lambda i, p: (2 * p[0] + p[1], 0)
    corner = lambda i, p: (p[1], p[0])
    rows = width // 4
    attn, ffn = (rows, 3 * wide + width // 2), (width // 4 + hidden // 8, width)
    qkv, proj, up, down = [pltpu.with_memory_space_constraint(a, pltpu.HBM) for a in (qkv, proj, up, down)]
    return call(
        pack_kernel,
        "pack",
        place,
        (1,),
        (qkv, proj, up, down),
        [
            pl.BlockSpec((3, rows, wide), lambda i, p: (0, 2 * p[0] + p[1], 0)),
            pl.BlockSpec((heads // 2, width // 2), corner),
            pl.BlockSpec((width // 2, hidden // 2), corner),
            pl.BlockSpec((hidden // 4, width), quarter),
        ],
        [shaped(attn, BF), shaped(ffn, BF), shaped(ffn, BF)],
        [whole_block(attn), whole_block(ffn), whole_block(ffn)],
        moved=8 * MIB,
    )


def join_attn_kernel(place, *refs):
    qkv_ref, proj_ref = refs[4:]
    wide = qkv_ref.shape[2]
    rows, side = refs[0].shape[0], refs[0].shape[1] - 3 * wide
    for r in range(4):
        c, y = (r >> 1) ^ place[0], (r & 1) ^ place[1]
        for k in range(3):
            qkv_ref[k, pl.ds(pl.multiple_of((2 * c + y) * rows, rows), rows), :] = refs[r][
                :, k * wide : (k + 1) * wide
            ]
        proj_ref[
            pl.ds(pl.multiple_of(y * rows, rows), rows), pl.ds(pl.multiple_of(c * side, side), side)
        ] = refs[r][:, 3 * wide :]


def join_attn(place, pieces, wide):
    rows, lanes = pieces[0].shape
    side = lanes - 3 * wide
    shapes = [(3, 4 * rows, wide), (2 * rows, 2 * side)]
    return call(
        join_attn_kernel,
        "join_attn",
        place,
        (1,),
        pieces,
        [whole_block(pieces[0].shape)] * 4,
        [shaped(s, BF) for s in shapes],
        [whole_block(s) for s in shapes],
    )


def join_ffn_kernel(place, *refs):
    up_ref, down_ref = refs[8:]
    rows, lanes = refs[0].shape
    tall = rows // 2
    for r in range(4):
        c, y = (r >> 1) ^ place[0], (r & 1) ^ place[1]
        for half in range(2):
            source = refs[4 * half + r]
            up_ref[
                pl.ds(pl.multiple_of((2 * y + half) * tall, tall), tall),
                pl.ds(pl.multiple_of(c * lanes, lanes), lanes),
            ] = source[:tall, :]
            down_ref[
                pl.ds(pl.multiple_of((4 * c + 2 * y + half) * tall, tall), tall), :
            ] = source[tall:, :]


def join_ffn(place, first, second):
    rows, lanes = first[0].shape
    shapes = [(2 * rows, 2 * lanes), (4 * rows, lanes)]
    return call(
        join_ffn_kernel,
        "join_ffn",
        place,
        (1,),
        [*first, *second],
        [whole_block(first[0].shape)] * 8,
        [shaped(s, BF) for s in shapes],
        [whole_block(s) for s in shapes],
    )


def rows_kernel(place, *refs):
    out_ref = refs[4]
    for step in range(4):

        @pl.when(pl.program_id(0) == step)
        def _():
            out_ref[...] = refs[step][...].astype(out_ref.dtype)


def both_rows(name, place, parts, dtype, deps=()):
    rows, width = parts[0].shape
    return call(
        rows_kernel,
        name,
        place,
        (4,),
        parts,
        [whole_block((rows, width))] * 4,
        [shaped((4 * rows, width), dtype)],
        [pl.BlockSpec((rows, width), lambda i, p: (i ^ (2 * p[3]), 0))],
        deps=deps,
        weight=1,
    )[0]


def small_kernel(place, one_ref, two_ref, *refs):
    for half in range(2):
        attn_ref, up_ref, out_ref = refs[half], refs[2 + half], refs[4 + half]
        local, width = attn_ref.shape[2] // 3, one_ref.shape[1]
        attn = jnp.sum(attn_ref[...], axis=0)
        rows = [one_ref[:3, :], two_ref[:3, :], jnp.concatenate([attn[:, :local], attn[:, 2 * local :]], axis=1)]
        rows += [up_ref[:, k * width : (k + 1) * width] for k in range(up_ref.shape[1] // width)]
        used = sum(r.shape[0] for r in rows)
        out_ref[:used, :] = jnp.concatenate(rows, axis=0)
        out_ref[used:, :] = jnp.zeros((out_ref.shape[0] - used, width), F32)


def small_sums(place, one, two, attn, up, deps=()):
    ins = (one, two, *attn, *up)
    shape = (16, one.shape[1])
    return call(
        small_kernel,
        "small_sums",
        place,
        (1,),
        ins,
        [whole_block(a.shape) for a in ins],
        [shaped(shape, F32)] * 2,
        [whole_block(shape)] * 2,
        deps=deps,
    )


def sums_kernel(outs, count, place, *refs):
    for out_ref, pieces in zip(refs[count:], outs):
        for out_at, parts in pieces:
            total = refs[parts[0][0]][parts[0][1]].astype(F32)
            for which, at in parts[1:]:
                total = total + refs[which][at].astype(F32)
            out_ref[out_at] = total.astype(out_ref.dtype)


def sums(name, place, outs, deps=()):
    arrays = []

    def number(array):
        for k, other in enumerate(arrays):
            if other is array:
                return k
        arrays.append(array)
        return len(arrays) - 1

    plan = [
        [(out_at, [(number(array), at) for array, at in parts]) for out_at, parts in pieces]
        for _, pieces in outs
    ]
    kinds = [pieces[0][1][0][0].dtype for _, pieces in outs]
    return call(
        functools.partial(sums_kernel, plan, len(arrays)),
        name,
        place,
        (1,),
        arrays,
        [whole_block(a.shape) for a in arrays],
        [shaped(shape, kind) for (shape, _), kind in zip(outs, kinds)],
        [whole_block(shape) for shape, _ in outs],
        deps=deps,
        weight=SUM_WEIGHT,
    )


def tile_out_kernel(place, *refs):
    out_ref = refs[4]
    step = pl.program_id(0)
    size = refs[0].shape[0] // 4

    def work(low, high):
        for k in range(8):
            for h in range(2):

                @pl.when((k >> 2) ^ (place[2] >> 2) == h)
                def _():
                    at = pl.ds(pl.multiple_of(((k ^ place[2]) & 3) * size, size), size)
                    out_ref[k * size : (k + 1) * size, :] = (low, high)[h][at, :].astype(F32)

    pl.when(step == 0)(lambda: work(refs[0], refs[1]))
    pl.when(step == 1)(lambda: work(refs[2], refs[3]))


def tile_out(name, place, parts, across, deps=()):
    rows, width = parts[0].shape
    tall = 2 * rows
    shape = (tall, 2 * width) if across else (2 * tall, width)
    turn = (lambda i, p: (0, i ^ p[0])) if across else (lambda i, p: (i ^ p[0], 0))
    return call(
        tile_out_kernel,
        name,
        place,
        (2,),
        parts,
        [whole_block(parts[0].shape)] * 4,
        [shaped(shape, F32)],
        [pl.BlockSpec((tall, width), turn)],
        deps=deps,
        weight=1,
    )[0]


def attn_out_kernel(place, *refs):
    qkv_ref, proj_ref = refs[4:]
    step = pl.program_id(0)
    size = refs[0].shape[0] // 4
    count, _, lanes = qkv_ref.shape

    def work(low, high):
        for k in range(8):
            for h in range(2):

                @pl.when((k >> 2) ^ (place[2] >> 2) == h)
                def _():
                    at = pl.ds(pl.multiple_of(((k ^ place[2]) & 3) * size, size), size)
                    source = (low, high)[h]
                    for n in range(count):
                        qkv_ref[n, k * size : (k + 1) * size, :] = source[
                            at, n * lanes : (n + 1) * lanes
                        ].astype(F32)
                    proj_ref[k * size : (k + 1) * size, :] = source[at, count * lanes :].astype(F32)

    pl.when(step == 0)(lambda: work(refs[0], refs[1]))
    pl.when(step == 1)(lambda: work(refs[2], refs[3]))


def attn_out(place, parts, count, lanes, deps=()):
    rows, wide = parts[0].shape
    tall = 2 * rows
    side = wide - count * lanes
    return call(
        attn_out_kernel,
        "attn_out",
        place,
        (2,),
        parts,
        [whole_block(parts[0].shape)] * 4,
        [shaped((count, 2 * tall, lanes), F32), shaped((tall, 2 * side), F32)],
        [
            pl.BlockSpec((count, tall, lanes), lambda i, p: (0, i ^ p[0], 0)),
            pl.BlockSpec((tall, side), lambda i, p: (0, i ^ p[0])),
        ],
        deps=deps,
    )


CORE, ROW, NEAR, FAR = range(4)


def swap_tensor(values):
    count = lax.axis_size("tensor")
    return lax.ppermute(values, "tensor", [(i, (i + 1) % count) for i in range(count)])


def swap(values, bit):
    count = lax.axis_size("dp")
    return lax.ppermute(values, "dp", [(i, i ^ (1 << bit)) for i in range(count)])


def dp_bits():
    return lax.axis_size("dp").bit_length() - 1


def after(values, *others):
    return lax.optimization_barrier((values, *others))[0]


def add(*parts):
    total = parts[0].astype(F32)
    for part in parts[1:]:
        total = total + part.astype(F32)
    return total.astype(BF)


def vector(ref):
    return ref[...].reshape(1, -1)


def average(values):
    return jnp.sum(values, axis=-1, keepdims=True) * (1.0 / values.shape[-1])


def normed(values):
    centered = values - average(values)
    inverse = lax.rsqrt(average(centered * centered) + 1e-05)
    return centered * inverse, inverse


def norm_back(upstream, scaled, inverse, gain):
    through = upstream * gain
    return inverse * (through - average(through) - scaled * average(through * scaled))


def column_sums(ref, parts):
    summed = [jnp.sum(part, axis=0, keepdims=True) for part in parts]
    summed.append(jnp.zeros((ref.shape[0] - len(parts), ref.shape[1]), F32))
    summed = jnp.concatenate(summed, axis=0)

    @pl.when(pl.program_id(0) == 0)
    def _():
        ref[...] = summed

    @pl.when(pl.program_id(0) > 0)
    def _():
        ref[...] += summed


def kept_column(place, groups):
    row = lax.broadcasted_iota(jnp.int32, (SHORT, 1), 0)
    first = 13 + pl.program_id(0) * groups
    return jnp.concatenate([(row < place[first + g]).astype(F32) for g in range(groups)], axis=0) > 0.5


def qkv_kernel(place, x_ref, weight_ref, bias_ref, out_ref):
    which, local = pl.program_id(0), weight_ref.shape[2]
    factor = jnp.where(which == 0, 1.0 / math.sqrt(HEAD), 1.0)
    value_bias = jnp.where(which == 2, bias_ref[:, local : 2 * local], 0.0)
    bias = jnp.where(which == 0, bias_ref[:, :local], value_bias)
    out_ref[...] = ((dot_nn(x_ref[...], weight_ref[0]) + bias) * factor).astype(BF)


def project_qkv(place, tokens, rows, weight, bias):
    count, width, local = weight.shape
    return call(
        qkv_kernel,
        "project_qkv",
        place,
        (count,),
        (tokens, weight, bias),
        [
            pl.BlockSpec((rows, width), lambda k, p: (p[3], 0)),
            pl.BlockSpec((1, width, local), lambda k, p: (k, 0, 0)),
            whole_block(bias.shape),
        ],
        [shaped((rows, count * local), BF)],
        [pl.BlockSpec((rows, local), lambda k, p: (0, k))],
        flops=2 * rows * width * count * local,
    )[0]


def first_norm_kernel(
    place, x_ref, c_own, c_oth, w_own, w_oth, bias, gain, shift, hidden_ref, low_ref, scaled_ref, inverse_ref
):
    attended = dot_nn(c_own[...], w_own[...]) + dot_nn(c_oth[...], w_oth[...])
    scaled, inverse = normed(x_ref[...].astype(F32) + attended + vector(bias))
    hidden = scaled * vector(gain) + vector(shift)
    hidden_ref[...] = hidden
    low_ref[...] = hidden.astype(BF)
    scaled_ref[...] = scaled
    inverse_ref[...] = inverse


def first_norm(place, tokens, context, proj, vectors):
    rows, local = context[0].shape
    width = tokens.shape[1]
    steps = 4
    size = rows // steps
    tile = pl.BlockSpec((size, width), lambda i, p: (i, 0))
    part = pl.BlockSpec((size, local), lambda i, p: (i, 0))
    return call(
        first_norm_kernel,
        "first_norm",
        place,
        (steps,),
        (tokens, *context, *proj, *vectors),
        [
            pl.BlockSpec((size, width), lambda i, p: (steps * p[3] + i, 0)),
            part,
            part,
            whole_block((local, width)),
            whole_block((local, width)),
            *[whole_block((width,))] * 3,
        ],
        [
            shaped((rows, width), F32),
            shaped((rows, width), BF),
            shaped((rows, width), F32),
            shaped((rows, 1), F32),
        ],
        [tile, tile, tile, pl.BlockSpec((size, 1), lambda i, p: (i, 0))],
        flops=4 * rows * width * local,
        moved=14 * rows * width,
    )


def put_rows(low_ref, high_ref, value):
    first = pl.program_id(0) < pl.num_programs(0) // 2

    @pl.when(first)
    def _():
        low_ref[...] = value

    @pl.when(jnp.logical_not(first))
    def _():
        high_ref[...] = value


def two_arrays(size, width, steps):
    half = steps // 2
    return [
        pl.BlockSpec((size, width), lambda i, p: (jnp.minimum(i, half - 1), 0)),
        pl.BlockSpec((size, width), lambda i, p: (jnp.maximum(i - half, 0), 0)),
    ]


def second_norm_kernel(
    place, acc_ref, x_ref, up_ref, bias, gain_ref, shift, result_low, result_high, grad_ref, low_ref, sum_ref
):
    keep = kept_column(place, acc_ref.shape[0] // SHORT)
    gain = vector(gain_ref)
    scaled, inverse = normed(acc_ref[...] + vector(bias))
    result = scaled * gain + vector(shift)
    put_rows(result_low, result_high, jnp.where(keep, result, x_ref[...].astype(F32)).astype(BF))
    upstream = jnp.where(keep, up_ref[...].astype(F32), 0.0)
    grad = norm_back(upstream, scaled, inverse, gain)
    grad_ref[...] = grad
    low_ref[...] = grad.astype(BF)
    column_sums(sum_ref, (grad, upstream * scaled, upstream))


def second_norm(place, acc, tokens, cotangent, vectors):
    rows, width = acc.shape
    steps = 4
    size = rows // steps
    tile = pl.BlockSpec((size, width), lambda i, p: (i, 0))
    far = pl.BlockSpec((size, width), lambda i, p: (steps * p[3] + i, 0))
    return call(
        second_norm_kernel,
        "second_norm",
        place,
        (steps,),
        (acc, tokens, cotangent, *vectors),
        [tile, far, far, *[whole_block((width,))] * 3],
        [shaped((rows // 2, width), BF)] * 2
        + [shaped((rows, width), F32), shaped((rows, width), BF), shaped((8, width), F32)],
        [*two_arrays(size, width, steps), tile, tile, whole_block((8, width))],
        moved=16 * rows * width,
    )


def first_back_kernel(
    place, grad_in, scaled_ref, inverse_ref, up_ref, w_own, w_oth, gain, base_ref, low_ref, c_own, c_oth, sum_ref
):
    keep = kept_column(place, grad_in.shape[0] // SHORT)
    upstream, scaled = grad_in[...], scaled_ref[...]
    grad = norm_back(upstream, scaled, inverse_ref[...], vector(gain))
    low = grad.astype(BF)
    base_ref[...] = grad + jnp.where(keep, 0.0, up_ref[...].astype(F32))
    low_ref[...] = low
    c_own[...] = dot_nt(low, w_own[...]).astype(BF)
    c_oth[...] = dot_nt(low, w_oth[...]).astype(BF)
    column_sums(sum_ref, (grad, upstream * scaled, upstream))


def first_back(place, grad, scaled, inverse, cotangent, proj, gain, deps=()):
    rows, width = grad.shape
    local = proj[0].shape[0]
    steps = 4
    size = rows // steps
    tile = pl.BlockSpec((size, width), lambda i, p: (i, 0))
    part = pl.BlockSpec((size, local), lambda i, p: (i, 0))
    return call(
        first_back_kernel,
        "first_back",
        place,
        (steps,),
        (grad, scaled, inverse, cotangent, *proj, gain),
        [
            tile,
            tile,
            pl.BlockSpec((size, 1), lambda i, p: (i, 0)),
            pl.BlockSpec((size, width), lambda i, p: (steps * p[3] + i, 0)),
            whole_block((local, width)),
            whole_block((local, width)),
            whole_block((width,)),
        ],
        [
            shaped((rows, width), F32),
            shaped((rows, width), BF),
            shaped((rows, local), BF),
            shaped((rows, local), BF),
            shaped((8, width), F32),
        ],
        [tile, tile, part, part, whole_block((8, width))],
        flops=4 * rows * width * local,
        moved=18 * rows * width,
        deps=deps,
    )


def input_grad_kernel(place, base_ref, g_own, g_oth, w_own, w_oth, low_ref, high_ref):
    count, _, local = w_own.shape
    total = base_ref[...]
    for grads, weight in ((g_own, w_own), (g_oth, w_oth)):
        for k in range(count):
            total = total + dot_nt(grads[:, k * local : (k + 1) * local], weight[k])
    put_rows(low_ref, high_ref, total.astype(BF))


def input_grad(place, base, grads, weights, deps=()):
    rows, width = base.shape
    wide = grads[0].shape[1]
    steps = 2
    size = rows // steps
    tile = pl.BlockSpec((size, width), lambda i, p: (i, 0))
    part = pl.BlockSpec((size, wide), lambda i, p: (i, 0))
    return call(
        input_grad_kernel,
        "input_grad",
        place,
        (steps,),
        (base, *grads, *weights),
        [tile, part, part, whole_block(weights[0].shape), whole_block(weights[0].shape)],
        [shaped((rows // 2, width), BF)] * 2,
        two_arrays(size, width, steps),
        flops=4 * rows * width * wide,
        deps=deps,
    )


def body(
    tokens,
    qkv_weight,
    qv_bias,
    proj_weight,
    proj_bias,
    first_gain,
    first_shift,
    up_weight,
    up_bias,
    down_weight,
    down_bias,
    second_gain,
    second_shift,
    cotangent,
    bucket,
    lengths,
    dropped,
):
    token_count, width = tokens.shape
    rows = token_count // lax.axis_size("tensor")
    side = lax.axis_index("tensor")
    index = lax.axis_index("dp")
    core, row, near, far = [(index >> bit) & 1 for bit in range(4)]
    local = qkv_weight.shape[2]
    hidden_count = up_weight.shape[1]

    groups = rows // SHORT
    is_short = bucket[0] == 1
    first_slot = jnp.where(is_short, side * groups, side * (rows // LONG))
    slot_lengths = lax.dynamic_slice_in_dim(lengths, first_slot, groups, 0)
    slot_drops = lax.dynamic_slice_in_dim(dropped, first_slot, groups, 0)
    limits = jnp.where(slot_drops == 0, slot_lengths, 0)
    per = LONG // SHORT
    long_limits = jnp.repeat(limits[: groups // per], per) - SHORT * (jnp.arange(groups) % per)
    limits = jnp.where(is_short, limits, long_limits)
    place = jnp.concatenate(
        [
            jnp.stack([core, row, 4 * row + 2 * near + far, side, bucket[0]]),
            slot_lengths,
            limits,
        ]
    ).astype(jnp.int32)
    qkv_own = jnp.transpose(qkv_weight, (1, 0, 2))
    attn_piece, ffn_one, ffn_two = pack(place, qkv_own, proj_weight, up_weight, down_weight)
    biases = jnp.concatenate([qv_bias.reshape(1, -1), up_bias.reshape(1, -1)], axis=1)
    attn_x = swap_tensor(attn_piece)
    qkv = [project_qkv(place, tokens, rows, qkv_own, biases)]
    c_own, lse_own = attend(place, qkv[0])
    attn_x = after(attn_x, c_own)
    attn_y = swap(attn_x, ROW)
    ffn_x = [swap_tensor(after(ffn_one, c_own))]
    biases_oth = swap_tensor(after(biases, c_own))
    ffn_x.append(swap_tensor(after(ffn_two, attn_x)))
    attn_core = swap(attn_x, CORE)
    ffn_x[0] = after(ffn_x[0], attn_y)
    ffn_y = [swap(ffn_x[0], ROW)]
    qkv_oth, proj_oth = join_attn(place, [attn_x, attn_y, attn_core, swap(attn_y, CORE)], local)
    qkv_w, proj_w = (qkv_own, qkv_oth), (proj_weight, proj_oth)
    qkv.append(project_qkv(place, tokens, rows, qkv_oth, biases_oth))
    c_oth, lse_oth = attend(place, qkv[1])
    ffn_x[1] = after(ffn_x[1], c_oth)
    context, lse = (c_own, c_oth), (lse_own, lse_oth)
    ffn_y[0] = after(ffn_y[0], c_oth)
    ffn_y.append(swap(ffn_x[1], ROW))
    ffn_core = [swap(after(v, c_oth), CORE) for v in ffn_x]
    hidden, hidden_low, scaled, inverse = first_norm(
        place, tokens, context, proj_w, (proj_bias, first_gain, first_shift)
    )
    act_own, slope_own, acc = ffn_forward(place, hidden_low, up_weight, biases, down_weight, hidden)
    ffn_y[1] = after(ffn_y[1], act_own)
    first, second = [
        [ffn_x[k], ffn_y[k], ffn_core[k], swap(ffn_y[k], CORE)] for k in range(2)
    ]
    up_oth, down_oth = join_ffn(place, first, second)
    act_oth, slope_oth, acc = ffn_forward(place, hidden_low, up_oth, biases_oth, down_oth, acc)
    *result_own, grad_second, branch_grad, sums_two = second_norm(
        place, acc, tokens, cotangent, (down_bias, second_gain, second_shift)
    )

    def part(pair, half, low, high, first, last):
        at = (slice(low, high), slice(first, last))
        return (pair[half], at) if isinstance(pair, tuple) else (pair, (half, *at))

    def first_left(near, got, size, wide):
        pieces = [part(p, 1, 0, size, 0, wide) for p in (near, got)]
        return ((size, wide), [((slice(None), slice(None)), pieces)])

    def first_right(near, got, size, wide):
        return (
            (size // 2, 2 * wide),
            [
                (
                    (slice(None), slice(h * wide, (h + 1) * wide)),
                    [part(p, h, size // 2, size, wide, 2 * wide) for p in (near, got)],
                )
                for h in range(2)
            ],
        )

    def second_left(near, got, left, size, wide):
        return [
            (
                (size // 2, wide),
                [
                    (
                        (slice(None), slice(None)),
                        [part(p, 0, low, low + size // 2, 0, wide) for p in (near, got)]
                        + [(left, (slice(low, low + size // 2), slice(None)))],
                    )
                ],
            )
            for low in (0, size // 2)
        ]

    def second_right(near, got, right, size, wide):
        return [
            (
                (size // 2, wide),
                [
                    (
                        (slice(None), slice(None)),
                        [part(p, h, 0, size // 2, wide, 2 * wide) for p in (near, got)]
                        + [(right, (slice(None), slice(h * wide, (h + 1) * wide)))],
                    )
                ],
            )
            for h in range(2)
        ]

    def third(keeps, received):
        size, wide = keeps[0].shape
        return [
            (
                (size // 2, 2 * wide),
                [
                    (
                        (slice(None), slice(k * wide, (k + 1) * wide)),
                        [(a, (slice(low, low + size // 2), slice(None))) for a in (keeps[k], received[k])],
                    )
                    for k in range(2)
                ],
            )
            for low in (0, size // 2)
        ]

    def fourth(keep, received):
        size, wide = keep.shape
        return [
            (
                (size // 2, wide),
                [((slice(None), slice(None)), [(a, (slice(low, low + size // 2), slice(None))) for a in (keep, received)])],
            )
            for low in (0, size // 2)
        ]

    everything = (slice(None), slice(None))

    def plain(*arrays):
        return (arrays[0].shape, [(everything, [(a, everything) for a in arrays])])

    def grown(piece, other):
        size, wide = piece.shape
        return (
            (2 * size, wide),
            [
                ((slice(k * size, (k + 1) * size), slice(None)), [(a, everything)])
                for k, a in enumerate((piece, other))
            ],
        )

    def last_bits(values):
        for bit in range(4, dp_bits()):
            values = add(values, swap(values, bit))
        return values

    size, half = width, width // 2
    down_far, down_near = ffn_grad("down_grad", place, (act_own, act_oth), branch_grad, "left")
    down_got = swap(down_far, CORE)
    pre_own, acc, up_sums_own = ffn_backward(
        place, branch_grad, slope_own, up_weight, down_weight, grad_second, deps=[down_near], weight=1
    )
    left, right = sums(
        "sums_1",
        place,
        [first_left(down_near, down_got, size, half), first_right(down_near, down_got, size, half)],
        deps=[pre_own],
    )
    down_left, down_right = swap_tensor(left), swap(right, ROW)
    pre_oth, grad_hidden, up_sums_oth = ffn_backward(
        place, branch_grad, slope_oth, up_oth, down_oth, acc, deps=[left]
    )
    up_far, up_near = ffn_grad("up_grad", place, (pre_own, pre_oth), hidden_low, "right")
    up_got = swap(up_far, CORE)
    down_keep = [None, None]
    down_keep[0], left, down_keep[1], right = sums(
        "sums_2",
        place,
        [
            *second_left(down_near, down_got, down_left, size, half),
            *second_right(down_near, down_got, down_right, size, half),
        ],
        deps=[up_near],
    )
    down_left, down_right = swap(left, ROW), swap_tensor(right)
    base, out_grad, gc_own, gc_oth, sums_one = first_back(
        place, grad_hidden, scaled, inverse, cotangent, proj_w, first_gain, deps=[left]
    )
    down_keep, down_send, left, right = sums(
        "sums_3",
        place,
        [
            *third(down_keep, (down_left, down_right)),
            first_left(up_near, up_got, size, half),
            first_right(up_near, up_got, size, half),
        ],
        deps=[out_grad],
    )
    down_z = swap(down_send, NEAR)
    up_left, up_right = swap_tensor(left), swap(right, ROW)
    grads_oth, attn_sums_oth = attend_back(place, qkv[1], gc_oth, lse[1], deps=[down_send])
    down_keep, down_send = sums("sums_4", place, fourth(down_keep, down_z), deps=[grads_oth])
    down_f = swap(down_send, FAR)
    far_oth, near_oth = attn_grad(place, tokens, grads_oth, context[1], out_grad, deps=[down_send])
    got_oth = swap(far_oth, CORE)
    up_keep = [None, None]
    up_keep[0], left, up_keep[1], right, down_sum = sums(
        "sums_5",
        place,
        [
            *second_left(up_near, up_got, up_left, size, half),
            *second_right(up_near, up_got, up_right, size, half),
            plain(down_keep, down_f),
        ],
        deps=[far_oth],
    )
    down_sum = last_bits(down_sum)
    up_left, up_right = swap(left, ROW), swap_tensor(right)
    down_a = swap(down_sum, FAR)
    grads_own, attn_sums_own = attend_back(place, qkv[0], gc_own, lse[0], deps=[down_sum])
    wide, tall = near_oth.shape[1] // 2, near_oth.shape[0]
    up_keep, up_send, down_sum, left = sums(
        "sums_6",
        place,
        [
            *third(up_keep, (up_left, up_right)),
            grown(down_sum, down_a),
            first_left((None, near_oth), (None, got_oth), tall, wide),
        ],
        deps=[grads_own],
    )
    up_z = swap(up_send, NEAR)
    down_b = swap(down_sum, NEAR)
    attn_left = swap_tensor(left)
    far_own, near_own = attn_grad(place, tokens, grads_own, context[0], out_grad, deps=[up_send])
    got_own = swap(far_own, CORE)
    small_own, small_oth = small_sums(
        place,
        sums_one,
        sums_two,
        (attn_sums_own, attn_sums_oth),
        (up_sums_own, up_sums_oth),
        deps=[far_own],
    )
    small_x = swap_tensor(small_oth)
    up_keep, up_send, down_sum = sums(
        "sums_7", place, [*fourth(up_keep, up_z), grown(down_sum, down_b)], deps=[small_own, attn_left]
    )
    up_f = swap(up_send, FAR)
    down_core = swap(down_sum, CORE)
    input_own = input_grad(place, base, (grads_own, grads_oth), qkv_w, deps=[up_send])
    input_x = [swap_tensor(input_own[0])]
    near, got = (near_own, near_oth), (got_own, got_oth)
    right, keep_left, left, up_sum, small = sums(
        "sums_8",
        place,
        [
            first_right(near, got, tall, wide),
            *second_left(near, got, attn_left, tall, wide),
            plain(up_keep, up_f),
            plain(small_own, small_x),
        ],
        deps=[input_own[0]],
    )
    up_sum = last_bits(up_sum)
    attn_right, attn_left = swap(right, ROW), swap(left, ROW)
    up_a, small_r = swap(up_sum, FAR), swap(small, CORE)
    up_sum, small = sums("sums_9", place, [grown(up_sum, up_a), plain(small, small_r)])
    up_b, small_r = swap(up_sum, NEAR), swap(small, ROW)
    keep_right, right, small = sums(
        "sums_10",
        place,
        [*second_right(near, got, attn_right, tall, wide), plain(small, small_r)],
        deps=[up_sum],
    )
    small_r = swap(small, NEAR)
    attn_right = swap_tensor(right)
    down_y = swap(after(down_sum, right), ROW)
    (up_sum,) = sums("sums_11", place, [grown(up_sum, up_b)], deps=[right, attn_left])
    up_core = swap(up_sum, CORE)
    attn_keep, attn_send, small = sums(
        "sums_12",
        place,
        [*third((keep_left, keep_right), (attn_left, attn_right)), plain(small, small_r)],
        deps=[up_sum, input_x[0]],
    )
    small_r = swap(small, FAR)
    attn_z = swap(attn_send, NEAR)
    input_x.append(swap_tensor(after(input_own[1], attn_send)))
    attn_keep, attn_send = sums("sums_13", place, fourth(attn_keep, attn_z), deps=[down_y])
    attn_f = swap(attn_send, FAR)
    result_x = [swap_tensor(after(result_own[0], attn_send))]
    up_y = swap(after(up_sum, attn_send), ROW)
    down_last = swap(after(down_y, attn_send), CORE)
    down_total = tile_out("down_out", place, [down_sum, down_y, down_core, down_last], False, deps=[attn_send])
    (attn_sum,) = sums("sums_14", place, [plain(attn_keep, attn_f)], deps=[down_total])
    attn_sum = last_bits(attn_sum)
    attn_a = swap(attn_sum, FAR)
    result_x.append(swap_tensor(after(result_own[1], attn_sum)))
    attn_sum, small = sums(
        "sums_15", place, [grown(attn_sum, attn_a), plain(small, small_r)], deps=[input_x[1], up_y]
    )
    for bit in range(4, dp_bits()):
        small = small + swap(small, bit)
    attn_b = swap(attn_sum, NEAR)
    up_last = swap(after(up_y, attn_sum), CORE)
    up_total = tile_out("up_out", place, [up_sum, up_y, up_core, up_last], True, deps=[attn_sum, result_x[0]])
    (attn_sum,) = sums("sums_16", place, [grown(attn_sum, attn_b)], deps=[up_total])
    attn_y, attn_core = swap(attn_sum, ROW), swap(attn_sum, CORE)
    tokens_grad = both_rows("grad_rows", place, [*input_own, *input_x], F32, deps=[attn_sum])
    result = both_rows("result_rows", place, [*result_own, *result_x], BF, deps=[tokens_grad])
    attn_last = swap(after(attn_y, result), CORE)
    qkv_total, proj_total = attn_out(place, [attn_sum, attn_y, attn_core, attn_last], 3, local)
    bias_total = small[6:9].reshape(-1)
    return (
        result,
        tokens_grad,
        jnp.transpose(qkv_total, (1, 0, 2)),
        bias_total[: 2 * local].reshape(2, local),
        proj_total,
        small[0],
        small[1],
        small[2],
        up_total,
        bias_total[2 * local :],
        down_total,
        small[3],
        small[4],
        small[5],
    )


def solution(mesh):
    rows, columns, whole = P("dp", None), P(None, "tensor"), P()
    return jax.shard_map(
        body,
        mesh=mesh,
        in_specs=(
            rows,
            P(None, None, "tensor"),
            columns,
            P("tensor", None),
            whole,
            whole,
            whole,
            columns,
            P("tensor"),
            P("tensor", None),
            whole,
            whole,
            whole,
            rows,
            P("dp"),
            P("dp"),
            P("dp"),
        ),
        out_specs=(
            rows,
            rows,
            P(None, None, "tensor"),
            columns,
            P("tensor", None),
            whole,
            whole,
            whole,
            columns,
            P("tensor"),
            P("tensor", None),
            whole,
            whole,
            whole,
        ),
        check_vma=False,
    )
```

```python
import functools
import math

import jax
import jax.numpy as jnp
from jax import lax
from jax.experimental import pallas as pl
from jax.experimental.pallas import tpu as pltpu
from jax.sharding import PartitionSpec as P

HEAD = 64
LONG = 512
SHORT = 128
PAIR = 128
NEG = -1e30
BF = jnp.bfloat16
F32 = jnp.float32
MIB = 1024 * 1024
WEIGHT = 40
SUM_WEIGHT = 1


def dot_nn(left, right):
    return lax.dot_general(left, right, (((1,), (0,)), ((), ())), preferred_element_type=F32)


def dot_nt(left, right):
    return lax.dot_general(left, right, (((1,), (1,)), ((), ())), preferred_element_type=F32)


def dot_tn(left, right):
    return lax.dot_general(left, right, (((0,), (0,)), ((), ())), preferred_element_type=F32)


def shaped(shape, dtype):
    return jax.ShapeDtypeStruct(shape, dtype)


def whole_block(shape):
    return pl.BlockSpec(shape, lambda *_: (0,) * len(shape), pipeline_mode=pl.Buffered(1))


def call(kernel, name, place, grid, ins, in_specs, outs, out_specs, flops=0, moved=0, limit=14, aliases=None, exps=0, deps=(), weight=WEIGHT):
    moved = moved or sum(math.prod(a.shape) * a.dtype.itemsize for a in (*ins, *outs))
    if deps:
        place = lax.optimization_barrier((place, *deps))[0]
    return pl.pallas_call(
        kernel,
        grid_spec=pltpu.PrefetchScalarGridSpec(
            num_scalar_prefetch=1, grid=grid, in_specs=in_specs, out_specs=out_specs
        ),
        out_shape=outs,
        compiler_params=pltpu.CompilerParams(vmem_limit_bytes=limit * MIB),
        cost_estimate=pl.CostEstimate(
            flops=weight * flops, bytes_accessed=weight * moved, transcendentals=weight * exps
        ),
        input_output_aliases=aliases or {},
        name=name,
    )(place, *ins)


def head_masks():
    lane = lax.broadcasted_iota(jnp.int32, (1, PAIR), 1)
    return (lane < HEAD, lane >= HEAD)


def only(mask, values):
    return jnp.where(mask, values, jnp.zeros_like(values))


def attend_tile(q, k, v, length):
    size = q.shape[0]
    hide = jnp.where(lax.broadcasted_iota(jnp.int32, (size, 1), 0) < length, 0.0, NEG)
    total = None
    rows = []
    for mask in head_masks():
        scores = dot_nt(k, only(mask, q)) + hide
        top = jnp.max(scores, axis=0, keepdims=True)
        powers = jnp.exp(scores - top)
        summed = jnp.sum(powers, axis=0, keepdims=True)
        probs = (powers * (1.0 / summed)).astype(BF)
        part = dot_tn(only(mask, v), probs)
        total = part if total is None else total + part
        rows.append(top + jnp.log(summed))
    return jnp.transpose(total).astype(BF), jnp.concatenate(rows, axis=0)


def attend_kernel(info, q_ref, k_ref, v_ref, c_ref, lse_ref):
    block = pl.program_id(0)
    short = info[4] == 1

    @pl.when(jnp.logical_not(short))
    def _():
        c, rows = attend_tile(q_ref[...], k_ref[...], v_ref[...], info[5 + block])
        c_ref[...] = c
        lse_ref[0, 0] = rows

    @pl.when(short)
    def _():
        for sub in range(LONG // SHORT):
            at = slice(sub * SHORT, (sub + 1) * SHORT)
            length = info[5 + block * (LONG // SHORT) + sub]
            c, rows = attend_tile(q_ref[at, :], k_ref[at, :], v_ref[at, :], length)
            c_ref[at, :] = c
            lse_ref[0, 0, :, at] = rows


def attend_back_tile(q, k, v, grad_c, lse, length):
    size = q.shape[0]
    hide = jnp.where(lax.broadcasted_iota(jnp.int32, (size, 1), 0) < length, 0.0, NEG)
    dq = dk = dv = None
    for index, mask in enumerate(head_masks()):
        q_own, c_own, k_own = only(mask, q), only(mask, grad_c), only(mask, k)
        scores = dot_nt(k, q_own) + hide
        probs = jnp.exp(scores - lse[index : index + 1, :])
        grad_probs = dot_nt(v, c_own)
        row_dot = jnp.sum(probs * grad_probs, axis=0, keepdims=True)
        grad_scores = (probs * (grad_probs - row_dot)).astype(BF)
        parts = (
            dot_tn(k_own, grad_scores),
            dot_nn(grad_scores, q_own),
            dot_nn(probs.astype(BF), c_own),
        )
        if dq is None:
            dq, dk, dv = parts
        else:
            dq, dk, dv = dq + parts[0], dk + parts[1], dv + parts[2]
    return (jnp.transpose(dq) * (1.0 / math.sqrt(HEAD))).astype(BF), dk.astype(BF), dv.astype(BF)


def attend_back_kernel(pairs, info, q_ref, k_ref, v_ref, gc_ref, lse_ref, out_ref, sum_ref):
    block, pair = pl.program_id(0), pl.program_id(1)
    short = info[4] == 1

    def put(rows, parts, add):
        for which, part in enumerate(parts):
            lanes = pl.ds(pl.multiple_of((which * pairs + pair) * PAIR, PAIR), PAIR)
            out_ref[rows, lanes] = part
            summed = jnp.sum(part.astype(F32), axis=0, keepdims=True)
            if add:
                sum_ref[0, :, lanes] += summed
            else:
                sum_ref[0, :, lanes] = summed

    @pl.when(jnp.logical_not(short))
    def _():
        put(
            slice(None),
            attend_back_tile(
                q_ref[...], k_ref[...], v_ref[...], gc_ref[...], lse_ref[0, 0], info[5 + block]
            ),
            False,
        )

    @pl.when(short)
    def _():
        for sub in range(LONG // SHORT):
            at = slice(sub * SHORT, (sub + 1) * SHORT)
            length = info[5 + block * (LONG // SHORT) + sub]
            put(
                at,
                attend_back_tile(
                    q_ref[at, :], k_ref[at, :], v_ref[at, :], gc_ref[at, :], lse_ref[0, 0, :, at], length
                ),
                sub > 0,
            )


def attend_specs(width):
    pairs = width // PAIR
    return [
        pl.BlockSpec((LONG, PAIR), lambda b, p, info, k=k: (b, p + k * pairs)) for k in range(3)
    ]


def attend(info, qkv, deps=()):
    rows, width = qkv.shape[0], qkv.shape[1] // 3
    blocks, pairs = rows // LONG, width // PAIR
    tile = pl.BlockSpec((LONG, PAIR), lambda b, p, info: (b, p))
    lse_tile = pl.BlockSpec((1, 1, 2, LONG), lambda b, p, info: (b, p, 0, 0))
    return call(
        attend_kernel,
        "attend",
        info,
        (blocks, pairs),
        (qkv, qkv, qkv),
        attend_specs(width),
        [shaped((rows, width), BF), shaped((blocks, pairs, 2, LONG), F32)],
        [tile, lse_tile],
        flops=4 * rows * LONG * width,
        moved=8 * rows * width,
        limit=14,
        exps=rows * LONG * width // HEAD,
        deps=deps,
    )


def attend_back(info, qkv, grad_c, lse, deps=()):
    rows, width = grad_c.shape
    blocks, pairs = rows // LONG, width // PAIR
    tile = pl.BlockSpec((LONG, PAIR), lambda b, p, info: (b, p))
    lse_tile = pl.BlockSpec((1, 1, 2, LONG), lambda b, p, info: (b, p, 0, 0))
    grads, sums = call(
        functools.partial(attend_back_kernel, pairs),
        "attend_back",
        info,
        (blocks, pairs),
        (qkv, qkv, qkv, grad_c, lse),
        attend_specs(width) + [tile, lse_tile],
        [shaped((rows, 3 * width), BF), shaped((blocks, 1, 3 * width), F32)],
        [
            pl.BlockSpec((LONG, 3 * width), lambda b, p, info: (b, 0)),
            pl.BlockSpec((1, 1, 3 * width), lambda b, p, info: (b, 0, 0)),
        ],
        flops=10 * rows * LONG * width,
        moved=14 * rows * width,
        limit=18,
        exps=rows * LONG * width // HEAD,
        deps=deps,
    )
    return grads, sums


def ffn_forward_kernel(
    chunk, place, h_ref, up_ref, bias_ref, down_ref, acc_in, act_ref, slope_ref, acc_ref
):
    @pl.when(pl.program_id(0) == 0)
    def _():
        acc_ref[...] = acc_in[...]

    size = up_ref.shape[1]
    first = bias_ref.shape[1] - pl.num_programs(0) * size
    bias = bias_ref[:, pl.ds(pl.multiple_of(first + pl.program_id(0) * size, PAIR), size)]
    for start in range(0, h_ref.shape[0], chunk):
        at = slice(start, start + chunk)
        pre = dot_nn(h_ref[at, :], up_ref[...]) + bias
        cumulative = 0.5 + 0.5 * lax.erf(pre * (1.0 / math.sqrt(2.0)))
        density = jnp.exp(-0.5 * pre * pre) * (1.0 / math.sqrt(2.0 * math.pi))
        act = (pre * cumulative).astype(BF)
        act_ref[at, :] = act
        slope_ref[at, :] = (cumulative + pre * density).astype(BF)
        acc_ref[at, :] += dot_nn(act, down_ref[...])


def ffn_forward(place, hidden_low, up, bias, down, acc):
    rows, width = hidden_low.shape
    local = up.shape[1]
    tiles = 3
    size = local // tiles
    piece = pl.BlockSpec((rows, size), lambda i, p: (0, i))
    return call(
        functools.partial(ffn_forward_kernel, min(rows, 512)),
        "ffn_forward",
        place,
        (tiles,),
        (hidden_low, up, bias, down, acc),
        [
            whole_block((rows, width)),
            pl.BlockSpec((width, size), lambda i, p: (0, i)),
            whole_block(bias.shape),
            pl.BlockSpec((size, width), lambda i, p: (i, 0)),
            whole_block((rows, width)),
        ],
        [shaped((rows, local), BF), shaped((rows, local), BF), shaped((rows, width), F32)],
        [piece, piece, whole_block((rows, width))],
        flops=4 * rows * width * local,
        moved=20 * rows * width,
        exps=rows * local,
        limit=19,
    )


def ffn_backward_kernel(chunk, place, g_ref, slope_ref, up_ref, down_ref, acc_in, pre_ref, acc_ref, sum_ref):
    @pl.when(pl.program_id(0) == 0)
    def _():
        acc_ref[...] = acc_in[...]

    total = None
    for start in range(0, g_ref.shape[0], chunk):
        at = slice(start, start + chunk)
        grad_act = dot_nt(g_ref[at, :], down_ref[...])
        low = (grad_act * slope_ref[at, :].astype(F32)).astype(BF)
        pre_ref[at, :] = low
        part = jnp.sum(low.astype(F32), axis=0, keepdims=True)
        total = part if total is None else total + part
        acc_ref[at, :] += dot_nt(low, up_ref[...])
    size = pre_ref.shape[1]
    sum_ref[:, pl.ds(pl.multiple_of(pl.program_id(0) * size, size), size)] = total


def ffn_backward(place, grad_low, slope, up, down, acc, deps=(), weight=WEIGHT):
    rows, width = grad_low.shape
    local = up.shape[1]
    tiles = 3
    size = local // tiles
    piece = pl.BlockSpec((rows, size), lambda i, p: (0, i))
    return call(
        functools.partial(ffn_backward_kernel, min(rows, 512)),
        "ffn_backward",
        place,
        (tiles,),
        (grad_low, slope, up, down, acc),
        [
            whole_block((rows, width)),
            piece,
            pl.BlockSpec((width, size), lambda i, p: (0, i)),
            pl.BlockSpec((size, width), lambda i, p: (i, 0)),
            whole_block((rows, width)),
        ],
        [shaped((rows, local), BF), shaped((rows, width), F32), shaped((1, local), F32)],
        [piece, whole_block((rows, width)), whole_block((1, local))],
        flops=4 * rows * width * local,
        limit=19,
        deps=deps,
        weight=weight,
    )


def spread(value, place, put):
    count = 8
    size = value.shape[0] // count
    step = 16 if size % 16 == 0 else 8
    for k in range(count):
        at = pl.ds(pl.multiple_of((k ^ place[2]) * size, step), size)
        put(at, value[k * size : (k + 1) * size].astype(BF))


def ffn_grad_kernel(paired, place, *refs):
    left, right = (refs[:2], refs[2:3]) if paired == "left" else (refs[:1], refs[1:3])
    step = pl.program_id(0)
    for half in range(2):
        for far in range(2):

            @pl.when(step == 2 * (1 - far) + half)
            def _():
                out = refs[3 if far else 4]

                def put(at, part):
                    out[0, at, :] = part

                spread(dot_tn(left[half % len(left)][...], right[half % len(right)][...]), place, put)


def ffn_grad(name, place, pair, shared, paired, deps=()):
    rows, size = pair[0].shape[0], pair[0].shape[1] // 2
    width = shared.shape[1]
    own = pl.BlockSpec((rows, size), lambda i, p: (0, jnp.where(i < 2, 1 - p[0], p[0])))
    oth = pl.BlockSpec((rows, size), lambda i, p: (0, jnp.where(i < 3, 1 - p[0], p[0])))
    whole = whole_block(shared.shape)
    ins, specs = ((*pair, shared), [own, oth, whole]) if paired == "left" else ((shared, *pair), [whole, own, oth])
    shape = (2, size, width) if paired == "left" else (2, width, size)
    return call(
        functools.partial(ffn_grad_kernel, paired),
        name,
        place,
        (4,),
        ins,
        specs,
        [shaped(shape, BF)] * 2,
        [
            pl.BlockSpec((1, *shape[1:]), lambda i, p: (jnp.minimum(i, 1), 0, 0)),
            pl.BlockSpec((1, *shape[1:]), lambda i, p: (jnp.maximum(i - 2, 0), 0, 0)),
        ],
        flops=8 * rows * size * width,
        limit=18,
        deps=deps,
    )


def attn_grad_kernel(place, x_ref, grads_ref, c_ref, a_ref, far_ref, near_ref):
    wide = grads_ref.shape[1]
    for far, out in ((True, far_ref), (False, near_ref)):

        @pl.when(pl.program_id(0) == (0 if far else 1))
        def _():
            values = (dot_tn(x_ref[...], grads_ref[...]), dot_tn(c_ref[...], a_ref[...]))
            for start, value in zip((0, wide), values):
                lanes = slice(start, start + value.shape[1])

                def put(at, part):
                    out[at, lanes] = part

                spread(value, place, put)


def attn_grad(place, tokens, grads, context, out_grad, deps=(), weight=WEIGHT):
    rows, width = out_grad.shape
    tall = width // 2
    tile = lambda i, p: jnp.where(i == 0, 1 - p[0], p[0])
    wide = grads.shape[1] + tall
    return call(
        attn_grad_kernel,
        "attn_grad",
        place,
        (2,),
        (tokens, grads, context, out_grad),
        [
            pl.BlockSpec((rows, tall), lambda i, p: (p[3], tile(i, p))),
            whole_block(grads.shape),
            whole_block(context.shape),
            pl.BlockSpec((rows, tall), lambda i, p: (0, tile(i, p))),
        ],
        [shaped((tall, wide), BF)] * 2,
        [whole_block((tall, wide))] * 2,
        flops=4 * rows * tall * wide,
        moved=2 * (rows * (wide + 3 * tall) + 2 * tall * wide),
        limit=18,
        deps=deps,
        weight=weight,
    )


def pack_kernel(place, qkv_ref, proj_ref, up_ref, down_ref, attn_ref, *ffn_refs):
    wide = qkv_ref.shape[2]
    for k in range(3):
        attn_ref[:, k * wide : (k + 1) * wide] = qkv_ref[k]
    attn_ref[:, 3 * wide :] = proj_ref[...]
    tall = up_ref.shape[0] // 2
    for half, out in enumerate(ffn_refs):
        at = slice(half * tall, (half + 1) * tall)
        out[:tall, :] = up_ref[at, :]
        out[tall:, :] = down_ref[at, :]


def pack(place, qkv, proj, up, down):
    _, width, wide = qkv.shape
    heads, hidden = proj.shape[0], up.shape[1]
    quarter = lambda i, p: (2 * p[0] + p[1], 0)
    corner = lambda i, p: (p[1], p[0])
    rows = width // 4
    attn, ffn = (rows, 3 * wide + width // 2), (width // 4 + hidden // 8, width)
    qkv, proj, up, down = [pltpu.with_memory_space_constraint(a, pltpu.HBM) for a in (qkv, proj, up, down)]
    return call(
        pack_kernel,
        "pack",
        place,
        (1,),
        (qkv, proj, up, down),
        [
            pl.BlockSpec((3, rows, wide), lambda i, p: (0, 2 * p[0] + p[1], 0)),
            pl.BlockSpec((heads // 2, width // 2), corner),
            pl.BlockSpec((width // 2, hidden // 2), corner),
            pl.BlockSpec((hidden // 4, width), quarter),
        ],
        [shaped(attn, BF), shaped(ffn, BF), shaped(ffn, BF)],
        [whole_block(attn), whole_block(ffn), whole_block(ffn)],
        moved=8 * MIB,
    )


def join_attn_kernel(place, *refs):
    qkv_ref, proj_ref = refs[4:]
    wide = qkv_ref.shape[2]
    rows, side = refs[0].shape[0], refs[0].shape[1] - 3 * wide
    for r in range(4):
        c, y = (r >> 1) ^ place[0], (r & 1) ^ place[1]
        for k in range(3):
            qkv_ref[k, pl.ds(pl.multiple_of((2 * c + y) * rows, rows), rows), :] = refs[r][
                :, k * wide : (k + 1) * wide
            ]
        proj_ref[
            pl.ds(pl.multiple_of(y * rows, rows), rows), pl.ds(pl.multiple_of(c * side, side), side)
        ] = refs[r][:, 3 * wide :]


def join_attn(place, pieces, wide):
    rows, lanes = pieces[0].shape
    side = lanes - 3 * wide
    shapes = [(3, 4 * rows, wide), (2 * rows, 2 * side)]
    return call(
        join_attn_kernel,
        "join_attn",
        place,
        (1,),
        pieces,
        [whole_block(pieces[0].shape)] * 4,
        [shaped(s, BF) for s in shapes],
        [whole_block(s) for s in shapes],
    )


def join_ffn_kernel(place, *refs):
    up_ref, down_ref = refs[8:]
    rows, lanes = refs[0].shape
    tall = rows // 2
    for r in range(4):
        c, y = (r >> 1) ^ place[0], (r & 1) ^ place[1]
        for half in range(2):
            source = refs[4 * half + r]
            up_ref[
                pl.ds(pl.multiple_of((2 * y + half) * tall, tall), tall),
                pl.ds(pl.multiple_of(c * lanes, lanes), lanes),
            ] = source[:tall, :]
            down_ref[
                pl.ds(pl.multiple_of((4 * c + 2 * y + half) * tall, tall), tall), :
            ] = source[tall:, :]


def join_ffn(place, first, second):
    rows, lanes = first[0].shape
    shapes = [(2 * rows, 2 * lanes), (4 * rows, lanes)]
    return call(
        join_ffn_kernel,
        "join_ffn",
        place,
        (1,),
        [*first, *second],
        [whole_block(first[0].shape)] * 8,
        [shaped(s, BF) for s in shapes],
        [whole_block(s) for s in shapes],
    )


def rows_kernel(place, mine_ref, other_ref, out_ref):
    half = pl.num_programs(0) // 2

    @pl.when(pl.program_id(0) < half)
    def _():
        out_ref[...] = mine_ref[...].astype(out_ref.dtype)

    @pl.when(pl.program_id(0) >= half)
    def _():
        out_ref[...] = other_ref[...].astype(out_ref.dtype)


def both_rows(name, place, mine, other, dtype, deps=()):
    rows, width = mine.shape
    size = rows // 2
    return call(
        rows_kernel,
        name,
        place,
        (4,),
        (mine, other),
        [
            pl.BlockSpec((size, width), lambda i, p: (jnp.minimum(i, 1), 0)),
            pl.BlockSpec((size, width), lambda i, p: (jnp.maximum(i - 2, 0), 0)),
        ],
        [shaped((2 * rows, width), dtype)],
        [pl.BlockSpec((size, width), lambda i, p: (i ^ (2 * p[3]), 0))],
        deps=deps,
        weight=1,
    )[0]


def small_kernel(place, one_ref, two_ref, *refs):
    for half in range(2):
        attn_ref, up_ref, out_ref = refs[half], refs[2 + half], refs[4 + half]
        local, width = attn_ref.shape[2] // 3, one_ref.shape[1]
        attn = jnp.sum(attn_ref[...], axis=0)
        rows = [one_ref[:3, :], two_ref[:3, :], jnp.concatenate([attn[:, :local], attn[:, 2 * local :]], axis=1)]
        rows += [up_ref[:, k * width : (k + 1) * width] for k in range(up_ref.shape[1] // width)]
        used = sum(r.shape[0] for r in rows)
        out_ref[:used, :] = jnp.concatenate(rows, axis=0)
        out_ref[used:, :] = jnp.zeros((out_ref.shape[0] - used, width), F32)


def small_sums(place, one, two, attn, up, deps=()):
    ins = (one, two, *attn, *up)
    shape = (16, one.shape[1])
    return call(
        small_kernel,
        "small_sums",
        place,
        (1,),
        ins,
        [whole_block(a.shape) for a in ins],
        [shaped(shape, F32)] * 2,
        [whole_block(shape)] * 2,
        deps=deps,
        weight=1,
    )


def sums_kernel(outs, count, place, *refs):
    for out_ref, pieces in zip(refs[count:], outs):
        for out_at, parts in pieces:
            total = refs[parts[0][0]][parts[0][1]].astype(F32)
            for which, at in parts[1:]:
                total = total + refs[which][at].astype(F32)
            out_ref[out_at] = total.astype(out_ref.dtype)


def sums(name, place, outs, deps=()):
    arrays = []

    def number(array):
        for k, other in enumerate(arrays):
            if other is array:
                return k
        arrays.append(array)
        return len(arrays) - 1

    plan = [
        [(out_at, [(number(array), at) for array, at in parts]) for out_at, parts in pieces]
        for _, pieces in outs
    ]
    kinds = [pieces[0][1][0][0].dtype for _, pieces in outs]
    return call(
        functools.partial(sums_kernel, plan, len(arrays)),
        name,
        place,
        (1,),
        arrays,
        [whole_block(a.shape) for a in arrays],
        [shaped(shape, kind) for (shape, _), kind in zip(outs, kinds)],
        [whole_block(shape) for shape, _ in outs],
        deps=deps,
        weight=SUM_WEIGHT,
    )


def tile_out_kernel(place, *refs):
    out_ref = refs[4]
    step = pl.program_id(0)
    size = refs[0].shape[0] // 4

    def work(low, high):
        for k in range(8):
            for h in range(2):

                @pl.when((k >> 2) ^ (place[2] >> 2) == h)
                def _():
                    at = pl.ds(pl.multiple_of(((k ^ place[2]) & 3) * size, size), size)
                    out_ref[k * size : (k + 1) * size, :] = (low, high)[h][at, :].astype(F32)

    pl.when(step == 0)(lambda: work(refs[0], refs[1]))
    pl.when(step == 1)(lambda: work(refs[2], refs[3]))


def tile_out(name, place, parts, across, deps=()):
    rows, width = parts[0].shape
    tall = 2 * rows
    shape = (tall, 2 * width) if across else (2 * tall, width)
    turn = (lambda i, p: (0, i ^ p[0])) if across else (lambda i, p: (i ^ p[0], 0))
    return call(
        tile_out_kernel,
        name,
        place,
        (2,),
        parts,
        [whole_block(parts[0].shape)] * 4,
        [shaped(shape, F32)],
        [pl.BlockSpec((tall, width), turn)],
        deps=deps,
        weight=1,
    )[0]


def attn_out_kernel(place, *refs):
    qkv_ref, proj_ref = refs[4:]
    step = pl.program_id(0)
    size = refs[0].shape[0] // 4
    count, _, lanes = qkv_ref.shape

    def work(low, high):
        for k in range(8):
            for h in range(2):

                @pl.when((k >> 2) ^ (place[2] >> 2) == h)
                def _():
                    at = pl.ds(pl.multiple_of(((k ^ place[2]) & 3) * size, size), size)
                    source = (low, high)[h]
                    for n in range(count):
                        qkv_ref[n, k * size : (k + 1) * size, :] = source[
                            at, n * lanes : (n + 1) * lanes
                        ].astype(F32)
                    proj_ref[k * size : (k + 1) * size, :] = source[at, count * lanes :].astype(F32)

    pl.when(step == 0)(lambda: work(refs[0], refs[1]))
    pl.when(step == 1)(lambda: work(refs[2], refs[3]))


def attn_out(place, parts, count, lanes, deps=()):
    rows, wide = parts[0].shape
    tall = 2 * rows
    side = wide - count * lanes
    return call(
        attn_out_kernel,
        "attn_out",
        place,
        (2,),
        parts,
        [whole_block(parts[0].shape)] * 4,
        [shaped((count, 2 * tall, lanes), F32), shaped((tall, 2 * side), F32)],
        [
            pl.BlockSpec((count, tall, lanes), lambda i, p: (0, i ^ p[0], 0)),
            pl.BlockSpec((tall, side), lambda i, p: (0, i ^ p[0])),
        ],
        deps=deps,
    )


CORE, ROW, NEAR, FAR = range(4)


def swap_tensor(values):
    count = lax.axis_size("tensor")
    return lax.ppermute(values, "tensor", [(i, (i + 1) % count) for i in range(count)])


def swap(values, bit):
    count = lax.axis_size("dp")
    return lax.ppermute(values, "dp", [(i, i ^ (1 << bit)) for i in range(count)])


def dp_bits():
    return lax.axis_size("dp").bit_length() - 1


def after(values, *others):
    return lax.optimization_barrier((values, *others))[0]


def add(*parts):
    total = parts[0].astype(F32)
    for part in parts[1:]:
        total = total + part.astype(F32)
    return total.astype(BF)


def vector(ref):
    return ref[...].reshape(1, -1)


def average(values):
    return jnp.sum(values, axis=-1, keepdims=True) * (1.0 / values.shape[-1])


def normed(values):
    centered = values - average(values)
    inverse = lax.rsqrt(average(centered * centered) + 1e-05)
    return centered * inverse, inverse


def norm_back(upstream, scaled, inverse, gain):
    through = upstream * gain
    return inverse * (through - average(through) - scaled * average(through * scaled))


def column_sums(ref, parts):
    summed = [jnp.sum(part, axis=0, keepdims=True) for part in parts]
    summed.append(jnp.zeros((ref.shape[0] - len(parts), ref.shape[1]), F32))
    summed = jnp.concatenate(summed, axis=0)

    @pl.when(pl.program_id(0) == 0)
    def _():
        ref[...] = summed

    @pl.when(pl.program_id(0) > 0)
    def _():
        ref[...] += summed


def kept_column(place, groups):
    row = lax.broadcasted_iota(jnp.int32, (SHORT, 1), 0)
    first = 13 + pl.program_id(0) * groups
    return jnp.concatenate([(row < place[first + g]).astype(F32) for g in range(groups)], axis=0) > 0.5


def qkv_kernel(place, x_ref, weight_ref, bias_ref, out_ref):
    which, local = pl.program_id(0), weight_ref.shape[2]
    factor = jnp.where(which == 0, 1.0 / math.sqrt(HEAD), 1.0)
    value_bias = jnp.where(which == 2, bias_ref[:, local : 2 * local], 0.0)
    bias = jnp.where(which == 0, bias_ref[:, :local], value_bias)
    out_ref[...] = ((dot_nn(x_ref[...], weight_ref[0]) + bias) * factor).astype(BF)


def project_qkv(place, tokens, rows, weight, bias):
    count, width, local = weight.shape
    return call(
        qkv_kernel,
        "project_qkv",
        place,
        (count,),
        (tokens, weight, bias),
        [
            pl.BlockSpec((rows, width), lambda k, p: (p[3], 0)),
            pl.BlockSpec((1, width, local), lambda k, p: (k, 0, 0)),
            whole_block(bias.shape),
        ],
        [shaped((rows, count * local), BF)],
        [pl.BlockSpec((rows, local), lambda k, p: (0, k))],
        flops=2 * rows * width * count * local,
    )[0]


def first_norm_kernel(
    place, x_ref, c_own, c_oth, w_own, w_oth, bias, gain, shift, hidden_ref, low_ref, scaled_ref, inverse_ref
):
    attended = dot_nn(c_own[...], w_own[...]) + dot_nn(c_oth[...], w_oth[...])
    scaled, inverse = normed(x_ref[...].astype(F32) + attended + vector(bias))
    hidden = scaled * vector(gain) + vector(shift)
    hidden_ref[...] = hidden
    low_ref[...] = hidden.astype(BF)
    scaled_ref[...] = scaled.astype(BF)
    inverse_ref[...] = inverse


def first_norm(place, tokens, context, proj, vectors):
    rows, local = context[0].shape
    width = tokens.shape[1]
    steps = 4
    size = rows // steps
    tile = pl.BlockSpec((size, width), lambda i, p: (i, 0))
    part = pl.BlockSpec((size, local), lambda i, p: (i, 0))
    return call(
        first_norm_kernel,
        "first_norm",
        place,
        (steps,),
        (tokens, *context, *proj, *vectors),
        [
            pl.BlockSpec((size, width), lambda i, p: (steps * p[3] + i, 0)),
            part,
            part,
            whole_block((local, width)),
            whole_block((local, width)),
            *[whole_block((width,))] * 3,
        ],
        [
            shaped((rows, width), F32),
            shaped((rows, width), BF),
            shaped((rows, width), BF),
            shaped((rows, 1), F32),
        ],
        [tile, tile, tile, pl.BlockSpec((size, 1), lambda i, p: (i, 0))],
        flops=4 * rows * width * local,
        moved=14 * rows * width,
    )


def second_norm_kernel(
    place, acc_ref, x_ref, up_ref, bias, gain_ref, shift, result_ref, grad_ref, low_ref, sum_ref
):
    keep = kept_column(place, acc_ref.shape[0] // SHORT)
    gain = vector(gain_ref)
    scaled, inverse = normed(acc_ref[...] + vector(bias))
    result = scaled * gain + vector(shift)
    result_ref[...] = jnp.where(keep, result, x_ref[...].astype(F32)).astype(BF)
    upstream = jnp.where(keep, up_ref[...].astype(F32), 0.0)
    grad = norm_back(upstream, scaled, inverse, gain)
    grad_ref[...] = grad
    low_ref[...] = grad.astype(BF)
    column_sums(sum_ref, (grad, upstream * scaled, upstream))


def second_norm(place, acc, tokens, cotangent, vectors):
    rows, width = acc.shape
    steps = 4
    size = rows // steps
    tile = pl.BlockSpec((size, width), lambda i, p: (i, 0))
    far = pl.BlockSpec((size, width), lambda i, p: (steps * p[3] + i, 0))
    return call(
        second_norm_kernel,
        "second_norm",
        place,
        (steps,),
        (acc, tokens, cotangent, *vectors),
        [tile, far, far, *[whole_block((width,))] * 3],
        [shaped((rows, width), BF), shaped((rows, width), F32), shaped((rows, width), BF), shaped((8, width), F32)],
        [tile, tile, tile, whole_block((8, width))],
        moved=16 * rows * width,
    )


def first_back_kernel(
    place, grad_in, scaled_ref, inverse_ref, up_ref, w_own, w_oth, gain, base_ref, low_ref, c_own, c_oth, sum_ref
):
    keep = kept_column(place, grad_in.shape[0] // SHORT)
    upstream, scaled = grad_in[...], scaled_ref[...].astype(F32)
    grad = norm_back(upstream, scaled, inverse_ref[...], vector(gain))
    low = grad.astype(BF)
    base_ref[...] = grad + jnp.where(keep, 0.0, up_ref[...].astype(F32))
    low_ref[...] = low
    c_own[...] = dot_nt(low, w_own[...]).astype(BF)
    c_oth[...] = dot_nt(low, w_oth[...]).astype(BF)
    column_sums(sum_ref, (grad, upstream * scaled, upstream))


def first_back(place, grad, scaled, inverse, cotangent, proj, gain, deps=()):
    rows, width = grad.shape
    local = proj[0].shape[0]
    steps = 4
    size = rows // steps
    tile = pl.BlockSpec((size, width), lambda i, p: (i, 0))
    part = pl.BlockSpec((size, local), lambda i, p: (i, 0))
    return call(
        first_back_kernel,
        "first_back",
        place,
        (steps,),
        (grad, scaled, inverse, cotangent, *proj, gain),
        [
            tile,
            tile,
            pl.BlockSpec((size, 1), lambda i, p: (i, 0)),
            pl.BlockSpec((size, width), lambda i, p: (steps * p[3] + i, 0)),
            whole_block((local, width)),
            whole_block((local, width)),
            whole_block((width,)),
        ],
        [
            shaped((rows, width), F32),
            shaped((rows, width), BF),
            shaped((rows, local), BF),
            shaped((rows, local), BF),
            shaped((8, width), F32),
        ],
        [tile, tile, part, part, whole_block((8, width))],
        flops=4 * rows * width * local,
        moved=18 * rows * width,
        deps=deps,
    )


def input_grad_kernel(place, base_ref, g_own, g_oth, w_own, w_oth, out_ref):
    count, _, local = w_own.shape
    total = base_ref[...]
    for grads, weight in ((g_own, w_own), (g_oth, w_oth)):
        for k in range(count):
            total = total + dot_nt(grads[:, k * local : (k + 1) * local], weight[k])
    out_ref[...] = total.astype(BF)


def input_grad(place, base, grads, weights, deps=()):
    rows, width = base.shape
    wide = grads[0].shape[1]
    steps = 2
    size = rows // steps
    tile = pl.BlockSpec((size, width), lambda i, p: (i, 0))
    part = pl.BlockSpec((size, wide), lambda i, p: (i, 0))
    return call(
        input_grad_kernel,
        "input_grad",
        place,
        (steps,),
        (base, *grads, *weights),
        [tile, part, part, whole_block(weights[0].shape), whole_block(weights[0].shape)],
        [shaped((rows, width), BF)],
        [tile],
        flops=4 * rows * width * wide,
        deps=deps,
    )[0]


def body(
    tokens,
    qkv_weight,
    qv_bias,
    proj_weight,
    proj_bias,
    first_gain,
    first_shift,
    up_weight,
    up_bias,
    down_weight,
    down_bias,
    second_gain,
    second_shift,
    cotangent,
    bucket,
    lengths,
    dropped,
):
    token_count, width = tokens.shape
    rows = token_count // lax.axis_size("tensor")
    side = lax.axis_index("tensor")
    index = lax.axis_index("dp")
    core, row, near, far = [(index >> bit) & 1 for bit in range(4)]
    local = qkv_weight.shape[2]
    hidden_count = up_weight.shape[1]

    groups = rows // SHORT
    is_short = bucket[0] == 1
    first_slot = jnp.where(is_short, side * groups, side * (rows // LONG))
    slot_lengths = lax.dynamic_slice_in_dim(lengths, first_slot, groups, 0)
    slot_drops = lax.dynamic_slice_in_dim(dropped, first_slot, groups, 0)
    limits = jnp.where(slot_drops == 0, slot_lengths, 0)
    per = LONG // SHORT
    long_limits = jnp.repeat(limits[: groups // per], per) - SHORT * (jnp.arange(groups) % per)
    limits = jnp.where(is_short, limits, long_limits)
    place = jnp.concatenate(
        [
            jnp.stack([core, row, 4 * row + 2 * near + far, side, bucket[0]]),
            slot_lengths,
            limits,
        ]
    ).astype(jnp.int32)
    qkv_own = jnp.transpose(qkv_weight, (1, 0, 2))
    attn_piece, ffn_one, ffn_two = pack(place, qkv_own, proj_weight, up_weight, down_weight)
    biases = jnp.concatenate([qv_bias.reshape(1, -1), up_bias.reshape(1, -1)], axis=1)
    attn_x = swap_tensor(attn_piece)
    qkv = [project_qkv(place, tokens, rows, qkv_own, biases)]
    c_own, lse_own = attend(place, qkv[0])
    attn_x = after(attn_x, c_own)
    attn_y = swap(attn_x, ROW)
    ffn_x = [swap_tensor(after(ffn_one, c_own))]
    biases_oth = swap_tensor(after(biases, c_own))
    ffn_x.append(swap_tensor(after(ffn_two, attn_x)))
    attn_core = swap(attn_x, CORE)
    ffn_x[0] = after(ffn_x[0], attn_y)
    ffn_y = [swap(ffn_x[0], ROW)]
    qkv_oth, proj_oth = join_attn(place, [attn_x, attn_y, attn_core, swap(attn_y, CORE)], local)
    qkv_w, proj_w = (qkv_own, qkv_oth), (proj_weight, proj_oth)
    qkv.append(project_qkv(place, tokens, rows, qkv_oth, biases_oth))
    c_oth, lse_oth = attend(place, qkv[1])
    ffn_x[1] = after(ffn_x[1], c_oth)
    context, lse = (c_own, c_oth), (lse_own, lse_oth)
    ffn_y[0] = after(ffn_y[0], c_oth)
    ffn_y.append(swap(ffn_x[1], ROW))
    ffn_core = [swap(after(v, c_oth), CORE) for v in ffn_x]
    hidden, hidden_low, scaled, inverse = first_norm(
        place, tokens, context, proj_w, (proj_bias, first_gain, first_shift)
    )
    act_own, slope_own, acc = ffn_forward(place, hidden_low, up_weight, biases, down_weight, hidden)
    ffn_y[1] = after(ffn_y[1], act_own)
    first, second = [
        [ffn_x[k], ffn_y[k], ffn_core[k], swap(ffn_y[k], CORE)] for k in range(2)
    ]
    up_oth, down_oth = join_ffn(place, first, second)
    act_oth, slope_oth, acc = ffn_forward(place, hidden_low, up_oth, biases_oth, down_oth, acc)
    result_own, grad_second, branch_grad, sums_two = second_norm(
        place, acc, tokens, cotangent, (down_bias, second_gain, second_shift)
    )

    def part(pair, half, low, high, first, last):
        at = (slice(low, high), slice(first, last))
        return (pair[half], at) if isinstance(pair, tuple) else (pair, (half, *at))

    def first_left(near, got, size, wide):
        pieces = [part(p, 1, 0, size, 0, wide) for p in (near, got)]
        return ((size, wide), [((slice(None), slice(None)), pieces)])

    def first_right(near, got, size, wide):
        return (
            (size // 2, 2 * wide),
            [
                (
                    (slice(None), slice(h * wide, (h + 1) * wide)),
                    [part(p, h, size // 2, size, wide, 2 * wide) for p in (near, got)],
                )
                for h in range(2)
            ],
        )

    def second_left(near, got, left, size, wide):
        return [
            (
                (size // 2, wide),
                [
                    (
                        (slice(None), slice(None)),
                        [part(p, 0, low, low + size // 2, 0, wide) for p in (near, got)]
                        + [(left, (slice(low, low + size // 2), slice(None)))],
                    )
                ],
            )
            for low in (0, size // 2)
        ]

    def second_right(near, got, right, size, wide):
        return [
            (
                (size // 2, wide),
                [
                    (
                        (slice(None), slice(None)),
                        [part(p, h, 0, size // 2, wide, 2 * wide) for p in (near, got)]
                        + [(right, (slice(None), slice(h * wide, (h + 1) * wide)))],
                    )
                ],
            )
            for h in range(2)
        ]

    def third(keeps, received):
        size, wide = keeps[0].shape
        return [
            (
                (size // 2, 2 * wide),
                [
                    (
                        (slice(None), slice(k * wide, (k + 1) * wide)),
                        [(a, (slice(low, low + size // 2), slice(None))) for a in (keeps[k], received[k])],
                    )
                    for k in range(2)
                ],
            )
            for low in (0, size // 2)
        ]

    def fourth(keep, received):
        size, wide = keep.shape
        return [
            (
                (size // 2, wide),
                [((slice(None), slice(None)), [(a, (slice(low, low + size // 2), slice(None))) for a in (keep, received)])],
            )
            for low in (0, size // 2)
        ]

    everything = (slice(None), slice(None))

    def plain(*arrays):
        return (arrays[0].shape, [(everything, [(a, everything) for a in arrays])])

    def grown(piece, other):
        size, wide = piece.shape
        return (
            (2 * size, wide),
            [
                ((slice(k * size, (k + 1) * size), slice(None)), [(a, everything)])
                for k, a in enumerate((piece, other))
            ],
        )

    def last_bits(values):
        for bit in range(4, dp_bits()):
            values = add(values, swap(values, bit))
        return values

    size, half = width, width // 2
    down_far, down_near = ffn_grad("down_grad", place, (act_own, act_oth), branch_grad, "left")
    down_got = swap(down_far, CORE)
    pre_own, acc, up_sums_own = ffn_backward(
        place, branch_grad, slope_own, up_weight, down_weight, grad_second, deps=[down_near], weight=1
    )
    left, right = sums(
        "sums_1",
        place,
        [first_left(down_near, down_got, size, half), first_right(down_near, down_got, size, half)],
        deps=[pre_own],
    )
    down_left, down_right = swap_tensor(left), swap(right, ROW)
    pre_oth, grad_hidden, up_sums_oth = ffn_backward(
        place, branch_grad, slope_oth, up_oth, down_oth, acc, deps=[left]
    )
    up_far, up_near = ffn_grad("up_grad", place, (pre_own, pre_oth), hidden_low, "right")
    up_got = swap(up_far, CORE)
    down_keep = [None, None]
    down_keep[0], left, down_keep[1], right = sums(
        "sums_2",
        place,
        [
            *second_left(down_near, down_got, down_left, size, half),
            *second_right(down_near, down_got, down_right, size, half),
        ],
        deps=[up_near],
    )
    down_left, down_right = swap(left, ROW), swap_tensor(right)
    base, out_grad, gc_own, gc_oth, sums_one = first_back(
        place, grad_hidden, scaled, inverse, cotangent, proj_w, first_gain, deps=[left]
    )
    down_keep, down_send, left, right = sums(
        "sums_3",
        place,
        [
            *third(down_keep, (down_left, down_right)),
            first_left(up_near, up_got, size, half),
            first_right(up_near, up_got, size, half),
        ],
        deps=[out_grad],
    )
    down_z = swap(down_send, NEAR)
    up_left, up_right = swap_tensor(left), swap(right, ROW)
    grads_oth, attn_sums_oth = attend_back(place, qkv[1], gc_oth, lse[1], deps=[down_send])
    down_keep, down_send = sums("sums_4", place, fourth(down_keep, down_z), deps=[grads_oth])
    down_f = swap(down_send, FAR)
    far_oth, near_oth = attn_grad(
        place, tokens, grads_oth, context[1], out_grad, deps=[down_send], weight=1
    )
    got_oth = swap(far_oth, CORE)
    up_keep = [None, None]
    up_keep[0], left, up_keep[1], right, down_sum = sums(
        "sums_5",
        place,
        [
            *second_left(up_near, up_got, up_left, size, half),
            *second_right(up_near, up_got, up_right, size, half),
            plain(down_keep, down_f),
        ],
        deps=[far_oth],
    )
    down_sum = last_bits(down_sum)
    up_left, up_right = swap(left, ROW), swap_tensor(right)
    down_a = swap(down_sum, FAR)
    grads_own, attn_sums_own = attend_back(place, qkv[0], gc_own, lse[0], deps=[down_sum])
    tall, wide = near_oth.shape
    up_keep, up_send, down_sum, left, right = sums(
        "sums_6",
        place,
        [
            *third(up_keep, (up_left, up_right)),
            grown(down_sum, down_a),
            *[
                (
                    (tall, wide // 2),
                    [(everything, [(a, (slice(None), lanes)) for a in (near_oth, got_oth)])],
                )
                for lanes in (slice(0, wide // 2), slice(wide // 2, wide))
            ],
        ],
        deps=[grads_own],
    )
    up_z = swap(up_send, NEAR)
    down_b = swap(down_sum, NEAR)
    attn_x = [swap_tensor(left), swap_tensor(right)]
    far_own, near_own = attn_grad(place, tokens, grads_own, context[0], out_grad, deps=[up_send])
    got_own = swap(far_own, CORE)
    small_own, small_oth = small_sums(
        place,
        sums_one,
        sums_two,
        (attn_sums_own, attn_sums_oth),
        (up_sums_own, up_sums_oth),
        deps=[far_own],
    )
    small_x = swap_tensor(small_oth)
    up_keep, up_send, down_sum = sums(
        "sums_7", place, [*fourth(up_keep, up_z), grown(down_sum, down_b)], deps=[small_own, attn_x[0]]
    )
    up_f = swap(up_send, FAR)
    input_own = input_grad(place, base, (grads_own, grads_oth), qkv_w, deps=[up_send])
    attn_keep, attn_send, up_sum, small = sums(
        "sums_8",
        place,
        [
            *[
                (
                    (tall // 2, wide),
                    [
                        (
                            (slice(None), lanes),
                            [(near_own, (at, lanes)), (got_own, (at, lanes)), (attn_x[k], (at, slice(None)))],
                        )
                        for k, lanes in enumerate((slice(0, wide // 2), slice(wide // 2, wide)))
                    ],
                )
                for at in (slice(0, tall // 2), slice(tall // 2, tall))
            ],
            plain(up_keep, up_f),
            plain(small_own, small_x),
        ],
        deps=[input_own],
    )
    up_sum = last_bits(up_sum)
    attn_y = swap(attn_send, ROW)
    input_x = swap_tensor(after(input_own, small))
    up_a, small_r = swap(up_sum, FAR), swap(small, CORE)
    up_sum, small = sums("sums_9", place, [grown(up_sum, up_a), plain(small, small_r)])
    up_b, small_r = swap(up_sum, NEAR), swap(small, ROW)
    attn_keep, attn_send, small, up_sum = sums(
        "sums_10",
        place,
        [*fourth(attn_keep, attn_y), plain(small, small_r), grown(up_sum, up_b)],
    )
    attn_z, small_r = swap(attn_send, NEAR), swap(small, NEAR)
    down_y = swap(after(down_sum, attn_send), ROW)
    attn_keep, attn_send, small = sums(
        "sums_11", place, [*fourth(attn_keep, attn_z), plain(small, small_r)]
    )
    attn_f, small_r = swap(attn_send, FAR), swap(small, FAR)
    up_y = swap(after(up_sum, attn_send), ROW)
    (attn_sum,) = sums("sums_12", place, [plain(attn_keep, attn_f)], deps=[down_y])
    attn_sum = last_bits(attn_sum)
    attn_a = swap(attn_sum, FAR)
    result_x = swap_tensor(after(result_own, attn_sum, input_x))
    (attn_sum,) = sums("sums_13", place, [grown(attn_sum, attn_a)], deps=[input_x])
    attn_b = swap(attn_sum, NEAR)
    tokens_grad = both_rows("grad_rows", place, input_own, input_x, F32, deps=[attn_sum])
    attn_sum, small = sums(
        "sums_14", place, [grown(attn_sum, attn_b), plain(small, small_r)], deps=[tokens_grad, up_y]
    )
    for bit in range(4, dp_bits()):
        small = small + swap(small, bit)
    attn_y, attn_core = swap(attn_sum, ROW), swap(attn_sum, CORE)
    down_core, down_last, up_core, up_last = [
        swap(after(v, attn_sum), CORE) for v in (down_sum, down_y, up_sum, up_y)
    ]
    down_total = tile_out("down_out", place, [down_sum, down_y, down_core, down_last], False, deps=[attn_sum])
    up_total = tile_out("up_out", place, [up_sum, up_y, up_core, up_last], True, deps=[down_total])
    result = both_rows("result_rows", place, result_own, result_x, BF, deps=[up_total])
    attn_last = swap(after(attn_y, result), CORE)
    qkv_total, proj_total = attn_out(place, [attn_sum, attn_y, attn_core, attn_last], 3, local, deps=[result])
    bias_total = small[6:9].reshape(-1)
    return (
        result,
        tokens_grad,
        jnp.transpose(qkv_total, (1, 0, 2)),
        bias_total[: 2 * local].reshape(2, local),
        proj_total,
        small[0],
        small[1],
        small[2],
        up_total,
        bias_total[2 * local :],
        down_total,
        small[3],
        small[4],
        small[5],
    )


def solution(mesh):
    rows, columns, whole = P("dp", None), P(None, "tensor"), P()
    return jax.shard_map(
        body,
        mesh=mesh,
        in_specs=(
            rows,
            P(None, None, "tensor"),
            columns,
            P("tensor", None),
            whole,
            whole,
            whole,
            columns,
            P("tensor"),
            P("tensor", None),
            whole,
            whole,
            whole,
            rows,
            P("dp"),
            P("dp"),
            P("dp"),
        ),
        out_specs=(
            rows,
            rows,
            P(None, None, "tensor"),
            columns,
            P("tensor", None),
            whole,
            whole,
            whole,
            columns,
            P("tensor"),
            P("tensor", None),
            whole,
            whole,
            whole,
        ),
        check_vma=False,
    )
```

```python
import functools
import math

import jax
import jax.numpy as jnp
from jax import lax
from jax.experimental import pallas as pl
from jax.experimental.pallas import tpu as pltpu
from jax.sharding import PartitionSpec as P

HEAD = 64
LONG = 512
SHORT = 128
PAIR = 128
NEG = -1e30
BF = jnp.bfloat16
F32 = jnp.float32
MIB = 1024 * 1024
WEIGHT = 40
SUM_WEIGHT = 1


def dot_nn(left, right):
    return lax.dot_general(left, right, (((1,), (0,)), ((), ())), preferred_element_type=F32)


def dot_nt(left, right):
    return lax.dot_general(left, right, (((1,), (1,)), ((), ())), preferred_element_type=F32)


def dot_tn(left, right):
    return lax.dot_general(left, right, (((0,), (0,)), ((), ())), preferred_element_type=F32)


def shaped(shape, dtype):
    return jax.ShapeDtypeStruct(shape, dtype)


def whole_block(shape):
    return pl.BlockSpec(shape, lambda *_: (0,) * len(shape), pipeline_mode=pl.Buffered(1))


def call(kernel, name, place, grid, ins, in_specs, outs, out_specs, flops=0, moved=0, limit=14, aliases=None, exps=0, deps=(), weight=WEIGHT):
    moved = moved or sum(math.prod(a.shape) * a.dtype.itemsize for a in (*ins, *outs))
    if deps:
        place = lax.optimization_barrier((place, *deps))[0]
    return pl.pallas_call(
        kernel,
        grid_spec=pltpu.PrefetchScalarGridSpec(
            num_scalar_prefetch=1, grid=grid, in_specs=in_specs, out_specs=out_specs
        ),
        out_shape=outs,
        compiler_params=pltpu.CompilerParams(vmem_limit_bytes=limit * MIB),
        cost_estimate=pl.CostEstimate(
            flops=weight * flops, bytes_accessed=weight * moved, transcendentals=weight * exps
        ),
        input_output_aliases=aliases or {},
        name=name,
    )(place, *ins)


def head_masks():
    lane = lax.broadcasted_iota(jnp.int32, (1, PAIR), 1)
    return (lane < HEAD, lane >= HEAD)


def only(mask, values):
    return jnp.where(mask, values, jnp.zeros_like(values))


def attend_tile(q, k, v, length):
    size = q.shape[0]
    hide = jnp.where(lax.broadcasted_iota(jnp.int32, (size, 1), 0) < length, 0.0, NEG)
    total = None
    rows = []
    for mask in head_masks():
        scores = dot_nt(k, only(mask, q)) + hide
        top = jnp.max(scores, axis=0, keepdims=True)
        powers = jnp.exp(scores - top)
        summed = jnp.sum(powers, axis=0, keepdims=True)
        probs = (powers * (1.0 / summed)).astype(BF)
        part = dot_tn(only(mask, v), probs)
        total = part if total is None else total + part
        rows.append(top + jnp.log(summed))
    return jnp.transpose(total).astype(BF), jnp.concatenate(rows, axis=0)


def attend_kernel(info, q_ref, k_ref, v_ref, c_ref, lse_ref):
    block = pl.program_id(0)
    short = info[4] == 1

    @pl.when(jnp.logical_not(short))
    def _():
        c, rows = attend_tile(q_ref[...], k_ref[...], v_ref[...], info[5 + block])
        c_ref[...] = c
        lse_ref[0, 0] = rows

    @pl.when(short)
    def _():
        for sub in range(LONG // SHORT):
            at = slice(sub * SHORT, (sub + 1) * SHORT)
            length = info[5 + block * (LONG // SHORT) + sub]
            c, rows = attend_tile(q_ref[at, :], k_ref[at, :], v_ref[at, :], length)
            c_ref[at, :] = c
            lse_ref[0, 0, :, at] = rows


def attend_back_tile(q, k, v, grad_c, lse, length):
    size = q.shape[0]
    hide = jnp.where(lax.broadcasted_iota(jnp.int32, (size, 1), 0) < length, 0.0, NEG)
    dq = dk = dv = None
    for index, mask in enumerate(head_masks()):
        q_own, c_own, k_own = only(mask, q), only(mask, grad_c), only(mask, k)
        scores = dot_nt(k, q_own) + hide
        probs = jnp.exp(scores - lse[index : index + 1, :])
        grad_probs = dot_nt(v, c_own)
        row_dot = jnp.sum(probs * grad_probs, axis=0, keepdims=True)
        grad_scores = (probs * (grad_probs - row_dot)).astype(BF)
        parts = (
            dot_tn(k_own, grad_scores),
            dot_nn(grad_scores, q_own),
            dot_nn(probs.astype(BF), c_own),
        )
        if dq is None:
            dq, dk, dv = parts
        else:
            dq, dk, dv = dq + parts[0], dk + parts[1], dv + parts[2]
    return (jnp.transpose(dq) * (1.0 / math.sqrt(HEAD))).astype(BF), dk.astype(BF), dv.astype(BF)


def attend_back_kernel(pairs, info, q_ref, k_ref, v_ref, gc_ref, lse_ref, out_ref, sum_ref):
    block, pair = pl.program_id(0), pl.program_id(1)
    short = info[4] == 1

    def put(rows, parts, add):
        for which, part in enumerate(parts):
            lanes = pl.ds(pl.multiple_of((which * pairs + pair) * PAIR, PAIR), PAIR)
            out_ref[rows, lanes] = part
            summed = jnp.sum(part.astype(F32), axis=0, keepdims=True)
            if add:
                sum_ref[0, :, lanes] += summed
            else:
                sum_ref[0, :, lanes] = summed

    @pl.when(jnp.logical_not(short))
    def _():
        put(
            slice(None),
            attend_back_tile(
                q_ref[...], k_ref[...], v_ref[...], gc_ref[...], lse_ref[0, 0], info[5 + block]
            ),
            False,
        )

    @pl.when(short)
    def _():
        for sub in range(LONG // SHORT):
            at = slice(sub * SHORT, (sub + 1) * SHORT)
            length = info[5 + block * (LONG // SHORT) + sub]
            put(
                at,
                attend_back_tile(
                    q_ref[at, :], k_ref[at, :], v_ref[at, :], gc_ref[at, :], lse_ref[0, 0, :, at], length
                ),
                sub > 0,
            )


def attend_specs(width):
    pairs = width // PAIR
    return [
        pl.BlockSpec((LONG, PAIR), lambda b, p, info, k=k: (b, p + k * pairs)) for k in range(3)
    ]


def attend(info, qkv, deps=()):
    rows, width = qkv.shape[0], qkv.shape[1] // 3
    blocks, pairs = rows // LONG, width // PAIR
    tile = pl.BlockSpec((LONG, PAIR), lambda b, p, info: (b, p))
    lse_tile = pl.BlockSpec((1, 1, 2, LONG), lambda b, p, info: (b, p, 0, 0))
    return call(
        attend_kernel,
        "attend",
        info,
        (blocks, pairs),
        (qkv, qkv, qkv),
        attend_specs(width),
        [shaped((rows, width), BF), shaped((blocks, pairs, 2, LONG), F32)],
        [tile, lse_tile],
        flops=4 * rows * LONG * width,
        moved=8 * rows * width,
        limit=14,
        exps=rows * LONG * width // HEAD,
        deps=deps,
    )


def attend_back(info, qkv, grad_c, lse, deps=()):
    rows, width = grad_c.shape
    blocks, pairs = rows // LONG, width // PAIR
    tile = pl.BlockSpec((LONG, PAIR), lambda b, p, info: (b, p))
    lse_tile = pl.BlockSpec((1, 1, 2, LONG), lambda b, p, info: (b, p, 0, 0))
    grads, sums = call(
        functools.partial(attend_back_kernel, pairs),
        "attend_back",
        info,
        (blocks, pairs),
        (qkv, qkv, qkv, grad_c, lse),
        attend_specs(width) + [tile, lse_tile],
        [shaped((rows, 3 * width), BF), shaped((blocks, 1, 3 * width), F32)],
        [
            pl.BlockSpec((LONG, 3 * width), lambda b, p, info: (b, 0)),
            pl.BlockSpec((1, 1, 3 * width), lambda b, p, info: (b, 0, 0)),
        ],
        flops=10 * rows * LONG * width,
        moved=14 * rows * width,
        limit=18,
        exps=rows * LONG * width // HEAD,
        deps=deps,
    )
    return grads, sums


def ffn_forward_kernel(
    chunk, place, h_ref, up_ref, bias_ref, down_ref, acc_in, act_ref, slope_ref, acc_ref
):
    @pl.when(pl.program_id(0) == 0)
    def _():
        acc_ref[...] = acc_in[...]

    size = up_ref.shape[1]
    first = bias_ref.shape[1] - pl.num_programs(0) * size
    bias = bias_ref[:, pl.ds(pl.multiple_of(first + pl.program_id(0) * size, PAIR), size)]
    for start in range(0, h_ref.shape[0], chunk):
        at = slice(start, start + chunk)
        pre = dot_nn(h_ref[at, :], up_ref[...]) + bias
        cumulative = 0.5 + 0.5 * lax.erf(pre * (1.0 / math.sqrt(2.0)))
        density = jnp.exp(-0.5 * pre * pre) * (1.0 / math.sqrt(2.0 * math.pi))
        act = (pre * cumulative).astype(BF)
        act_ref[at, :] = act
        slope_ref[at, :] = (cumulative + pre * density).astype(BF)
        acc_ref[at, :] += dot_nn(act, down_ref[...])


def ffn_forward(place, hidden_low, up, bias, down, acc):
    rows, width = hidden_low.shape
    local = up.shape[1]
    tiles = 3
    size = local // tiles
    piece = pl.BlockSpec((rows, size), lambda i, p: (0, i))
    return call(
        functools.partial(ffn_forward_kernel, min(rows, 512)),
        "ffn_forward",
        place,
        (tiles,),
        (hidden_low, up, bias, down, acc),
        [
            whole_block((rows, width)),
            pl.BlockSpec((width, size), lambda i, p: (0, i)),
            whole_block(bias.shape),
            pl.BlockSpec((size, width), lambda i, p: (i, 0)),
            whole_block((rows, width)),
        ],
        [shaped((rows, local), BF), shaped((rows, local), BF), shaped((rows, width), F32)],
        [piece, piece, whole_block((rows, width))],
        flops=4 * rows * width * local,
        moved=20 * rows * width,
        exps=rows * local,
        limit=19,
    )


def ffn_backward_kernel(chunk, place, g_ref, slope_ref, up_ref, down_ref, acc_in, pre_ref, acc_ref, sum_ref):
    @pl.when(pl.program_id(0) == 0)
    def _():
        acc_ref[...] = acc_in[...]

    total = None
    for start in range(0, g_ref.shape[0], chunk):
        at = slice(start, start + chunk)
        grad_act = dot_nt(g_ref[at, :], down_ref[...])
        low = (grad_act * slope_ref[at, :].astype(F32)).astype(BF)
        pre_ref[at, :] = low
        part = jnp.sum(low.astype(F32), axis=0, keepdims=True)
        total = part if total is None else total + part
        acc_ref[at, :] += dot_nt(low, up_ref[...])
    size = pre_ref.shape[1]
    sum_ref[:, pl.ds(pl.multiple_of(pl.program_id(0) * size, size), size)] = total


def ffn_backward(place, grad_low, slope, up, down, acc, deps=(), weight=WEIGHT):
    rows, width = grad_low.shape
    local = up.shape[1]
    tiles = 3
    size = local // tiles
    piece = pl.BlockSpec((rows, size), lambda i, p: (0, i))
    return call(
        functools.partial(ffn_backward_kernel, min(rows, 512)),
        "ffn_backward",
        place,
        (tiles,),
        (grad_low, slope, up, down, acc),
        [
            whole_block((rows, width)),
            piece,
            pl.BlockSpec((width, size), lambda i, p: (0, i)),
            pl.BlockSpec((size, width), lambda i, p: (i, 0)),
            whole_block((rows, width)),
        ],
        [shaped((rows, local), BF), shaped((rows, width), F32), shaped((1, local), F32)],
        [piece, whole_block((rows, width)), whole_block((1, local))],
        flops=4 * rows * width * local,
        limit=19,
        deps=deps,
        weight=weight,
    )


def spread(value, place, put):
    count = 8
    size = value.shape[0] // count
    step = 16 if size % 16 == 0 else 8
    for k in range(count):
        at = pl.ds(pl.multiple_of((k ^ place[2]) * size, step), size)
        put(at, value[k * size : (k + 1) * size].astype(BF))


def ffn_grad_kernel(paired, place, *refs):
    left, right = (refs[:2], refs[2:3]) if paired == "left" else (refs[:1], refs[1:3])
    step = pl.program_id(0)
    for half in range(2):
        for far in range(2):

            @pl.when(step == 2 * (1 - far) + half)
            def _():
                out = refs[3 if far else 4]

                def put(at, part):
                    out[0, at, :] = part

                spread(dot_tn(left[half % len(left)][...], right[half % len(right)][...]), place, put)


def ffn_grad(name, place, pair, shared, paired, deps=()):
    rows, size = pair[0].shape[0], pair[0].shape[1] // 2
    width = shared.shape[1]
    own = pl.BlockSpec((rows, size), lambda i, p: (0, jnp.where(i < 2, 1 - p[0], p[0])))
    oth = pl.BlockSpec((rows, size), lambda i, p: (0, jnp.where(i < 3, 1 - p[0], p[0])))
    whole = whole_block(shared.shape)
    ins, specs = ((*pair, shared), [own, oth, whole]) if paired == "left" else ((shared, *pair), [whole, own, oth])
    shape = (2, size, width) if paired == "left" else (2, width, size)
    return call(
        functools.partial(ffn_grad_kernel, paired),
        name,
        place,
        (4,),
        ins,
        specs,
        [shaped(shape, BF)] * 2,
        [
            pl.BlockSpec((1, *shape[1:]), lambda i, p: (jnp.minimum(i, 1), 0, 0)),
            pl.BlockSpec((1, *shape[1:]), lambda i, p: (jnp.maximum(i - 2, 0), 0, 0)),
        ],
        flops=8 * rows * size * width,
        limit=18,
        deps=deps,
    )


def attn_grad_kernel(place, x_ref, grads_ref, c_ref, a_ref, far_ref, near_ref):
    wide = grads_ref.shape[1]
    for far, out in ((True, far_ref), (False, near_ref)):

        @pl.when(pl.program_id(0) == (0 if far else 1))
        def _():
            values = (dot_tn(x_ref[...], grads_ref[...]), dot_tn(c_ref[...], a_ref[...]))
            for start, value in zip((0, wide), values):
                lanes = slice(start, start + value.shape[1])

                def put(at, part):
                    out[at, lanes] = part

                spread(value, place, put)


def attn_grad(place, tokens, grads, context, out_grad, deps=(), weight=WEIGHT):
    rows, width = out_grad.shape
    tall = width // 2
    tile = lambda i, p: jnp.where(i == 0, 1 - p[0], p[0])
    wide = grads.shape[1] + tall
    return call(
        attn_grad_kernel,
        "attn_grad",
        place,
        (2,),
        (tokens, grads, context, out_grad),
        [
            pl.BlockSpec((rows, tall), lambda i, p: (p[3], tile(i, p))),
            whole_block(grads.shape),
            whole_block(context.shape),
            pl.BlockSpec((rows, tall), lambda i, p: (0, tile(i, p))),
        ],
        [shaped((tall, wide), BF)] * 2,
        [whole_block((tall, wide))] * 2,
        flops=4 * rows * tall * wide,
        moved=2 * (rows * (wide + 3 * tall) + 2 * tall * wide),
        limit=18,
        deps=deps,
        weight=weight,
    )


def pack_kernel(place, qkv_ref, proj_ref, up_ref, down_ref, attn_ref, *ffn_refs):
    wide = qkv_ref.shape[2]
    for k in range(3):
        attn_ref[:, k * wide : (k + 1) * wide] = qkv_ref[k]
    attn_ref[:, 3 * wide :] = proj_ref[...]
    tall = up_ref.shape[0] // 2
    for half, out in enumerate(ffn_refs):
        at = slice(half * tall, (half + 1) * tall)
        out[:tall, :] = up_ref[at, :]
        out[tall:, :] = down_ref[at, :]


def pack(place, qkv, proj, up, down):
    _, width, wide = qkv.shape
    heads, hidden = proj.shape[0], up.shape[1]
    quarter = lambda i, p: (2 * p[0] + p[1], 0)
    corner = lambda i, p: (p[1], p[0])
    rows = width // 4
    attn, ffn = (rows, 3 * wide + width // 2), (width // 4 + hidden // 8, width)
    qkv, proj, up, down = [pltpu.with_memory_space_constraint(a, pltpu.HBM) for a in (qkv, proj, up, down)]
    return call(
        pack_kernel,
        "pack",
        place,
        (1,),
        (qkv, proj, up, down),
        [
            pl.BlockSpec((3, rows, wide), lambda i, p: (0, 2 * p[0] + p[1], 0)),
            pl.BlockSpec((heads // 2, width // 2), corner),
            pl.BlockSpec((width // 2, hidden // 2), corner),
            pl.BlockSpec((hidden // 4, width), quarter),
        ],
        [shaped(attn, BF), shaped(ffn, BF), shaped(ffn, BF)],
        [whole_block(attn), whole_block(ffn), whole_block(ffn)],
        moved=8 * MIB,
    )


def join_attn_kernel(place, *refs):
    qkv_ref, proj_ref = refs[4:]
    wide = qkv_ref.shape[2]
    rows, side = refs[0].shape[0], refs[0].shape[1] - 3 * wide
    for r in range(4):
        c, y = (r >> 1) ^ place[0], (r & 1) ^ place[1]
        for k in range(3):
            qkv_ref[k, pl.ds(pl.multiple_of((2 * c + y) * rows, rows), rows), :] = refs[r][
                :, k * wide : (k + 1) * wide
            ]
        proj_ref[
            pl.ds(pl.multiple_of(y * rows, rows), rows), pl.ds(pl.multiple_of(c * side, side), side)
        ] = refs[r][:, 3 * wide :]


def join_attn(place, pieces, wide):
    rows, lanes = pieces[0].shape
    side = lanes - 3 * wide
    shapes = [(3, 4 * rows, wide), (2 * rows, 2 * side)]
    return call(
        join_attn_kernel,
        "join_attn",
        place,
        (1,),
        pieces,
        [whole_block(pieces[0].shape)] * 4,
        [shaped(s, BF) for s in shapes],
        [whole_block(s) for s in shapes],
    )


def join_ffn_kernel(place, *refs):
    up_ref, down_ref = refs[8:]
    rows, lanes = refs[0].shape
    tall = rows // 2
    for r in range(4):
        c, y = (r >> 1) ^ place[0], (r & 1) ^ place[1]
        for half in range(2):
            source = refs[4 * half + r]
            up_ref[
                pl.ds(pl.multiple_of((2 * y + half) * tall, tall), tall),
                pl.ds(pl.multiple_of(c * lanes, lanes), lanes),
            ] = source[:tall, :]
            down_ref[
                pl.ds(pl.multiple_of((4 * c + 2 * y + half) * tall, tall), tall), :
            ] = source[tall:, :]


def join_ffn(place, first, second):
    rows, lanes = first[0].shape
    shapes = [(2 * rows, 2 * lanes), (4 * rows, lanes)]
    return call(
        join_ffn_kernel,
        "join_ffn",
        place,
        (1,),
        [*first, *second],
        [whole_block(first[0].shape)] * 8,
        [shaped(s, BF) for s in shapes],
        [whole_block(s) for s in shapes],
    )


def rows_kernel(place, mine_ref, other_ref, out_ref):
    half = pl.num_programs(0) // 2

    @pl.when(pl.program_id(0) < half)
    def _():
        out_ref[...] = mine_ref[...].astype(out_ref.dtype)

    @pl.when(pl.program_id(0) >= half)
    def _():
        out_ref[...] = other_ref[...].astype(out_ref.dtype)


def both_rows(name, place, mine, other, dtype, deps=()):
    rows, width = mine.shape
    size = rows // 2
    return call(
        rows_kernel,
        name,
        place,
        (4,),
        (mine, other),
        [
            pl.BlockSpec((size, width), lambda i, p: (jnp.minimum(i, 1), 0)),
            pl.BlockSpec((size, width), lambda i, p: (jnp.maximum(i - 2, 0), 0)),
        ],
        [shaped((2 * rows, width), dtype)],
        [pl.BlockSpec((size, width), lambda i, p: (i ^ (2 * p[3]), 0))],
        deps=deps,
        weight=1,
    )[0]


def small_kernel(place, one_ref, two_ref, *refs):
    for half in range(2):
        attn_ref, up_ref, out_ref = refs[half], refs[2 + half], refs[4 + half]
        local, width = attn_ref.shape[2] // 3, one_ref.shape[1]
        attn = jnp.sum(attn_ref[...], axis=0)
        rows = [one_ref[:3, :], two_ref[:3, :], jnp.concatenate([attn[:, :local], attn[:, 2 * local :]], axis=1)]
        rows += [up_ref[:, k * width : (k + 1) * width] for k in range(up_ref.shape[1] // width)]
        used = sum(r.shape[0] for r in rows)
        out_ref[:used, :] = jnp.concatenate(rows, axis=0)
        out_ref[used:, :] = jnp.zeros((out_ref.shape[0] - used, width), F32)


def small_sums(place, one, two, attn, up, deps=()):
    ins = (one, two, *attn, *up)
    shape = (16, one.shape[1])
    return call(
        small_kernel,
        "small_sums",
        place,
        (1,),
        ins,
        [whole_block(a.shape) for a in ins],
        [shaped(shape, F32)] * 2,
        [whole_block(shape)] * 2,
        deps=deps,
        weight=1,
    )


def sums_kernel(outs, count, place, *refs):
    for out_ref, pieces in zip(refs[count:], outs):
        for out_at, parts in pieces:
            total = refs[parts[0][0]][parts[0][1]].astype(F32)
            for which, at in parts[1:]:
                total = total + refs[which][at].astype(F32)
            out_ref[out_at] = total.astype(out_ref.dtype)


def sums(name, place, outs, deps=()):
    arrays = []

    def number(array):
        for k, other in enumerate(arrays):
            if other is array:
                return k
        arrays.append(array)
        return len(arrays) - 1

    plan = [
        [(out_at, [(number(array), at) for array, at in parts]) for out_at, parts in pieces]
        for _, pieces in outs
    ]
    kinds = [pieces[0][1][0][0].dtype for _, pieces in outs]
    return call(
        functools.partial(sums_kernel, plan, len(arrays)),
        name,
        place,
        (1,),
        arrays,
        [whole_block(a.shape) for a in arrays],
        [shaped(shape, kind) for (shape, _), kind in zip(outs, kinds)],
        [whole_block(shape) for shape, _ in outs],
        deps=deps,
        weight=SUM_WEIGHT,
    )


def tile_out_kernel(place, *refs):
    out_ref = refs[4]
    step = pl.program_id(0)
    size = refs[0].shape[0] // 4

    def work(low, high):
        for k in range(8):
            for h in range(2):

                @pl.when((k >> 2) ^ (place[2] >> 2) == h)
                def _():
                    at = pl.ds(pl.multiple_of(((k ^ place[2]) & 3) * size, size), size)
                    out_ref[k * size : (k + 1) * size, :] = (low, high)[h][at, :].astype(F32)

    pl.when(step == 0)(lambda: work(refs[0], refs[1]))
    pl.when(step == 1)(lambda: work(refs[2], refs[3]))


def tile_out(name, place, parts, across, deps=()):
    rows, width = parts[0].shape
    tall = 2 * rows
    shape = (tall, 2 * width) if across else (2 * tall, width)
    turn = (lambda i, p: (0, i ^ p[0])) if across else (lambda i, p: (i ^ p[0], 0))
    return call(
        tile_out_kernel,
        name,
        place,
        (2,),
        parts,
        [whole_block(parts[0].shape)] * 4,
        [shaped(shape, F32)],
        [pl.BlockSpec((tall, width), turn)],
        deps=deps,
        weight=1,
    )[0]


def attn_out_kernel(place, *refs):
    qkv_ref, proj_ref = refs[8:]
    size = refs[0].shape[0] // 4
    count, _, lanes = qkv_ref.shape
    wide = refs[0].shape[1]

    def put(rows, first, values):
        for n in range(count + 1):
            low, high = max(first, n * lanes), min(first + values.shape[1], (n + 1) * lanes)
            if low < high:
                piece = values[:, low - first : high - first].astype(F32)
                if n < count:
                    qkv_ref[n, rows, low - n * lanes : high - n * lanes] = piece
                else:
                    proj_ref[rows, low - n * lanes : high - n * lanes] = piece

    def work(left_low, left_high, right_low, right_high):
        for k in range(8):
            rows = slice(k * size, (k + 1) * size)
            where = k ^ place[2]
            left_at = pl.ds(pl.multiple_of((where & 3) * size, size), size)
            right_at = pl.ds(pl.multiple_of((2 * (where >> 2) + (where & 1)) * size, size), size)
            for h, (left, right) in enumerate(((left_low, right_low), (left_high, right_high))):

                @pl.when((where >> 2) == h)
                def _():
                    put(rows, 0, left[left_at, :])

                @pl.when(((where >> 1) & 1) == h)
                def _():
                    put(rows, wide, right[right_at, :])

    pl.when(pl.program_id(0) == 0)(lambda: work(*refs[:4]))
    pl.when(pl.program_id(0) == 1)(lambda: work(*refs[4:8]))


def attn_out(place, parts, count, lanes, deps=()):
    rows, wide = parts[0].shape
    tall = 2 * rows
    side = 2 * wide - count * lanes
    return call(
        attn_out_kernel,
        "attn_out",
        place,
        (2,),
        parts,
        [whole_block(parts[0].shape)] * 8,
        [shaped((count, 2 * tall, lanes), F32), shaped((tall, 2 * side), F32)],
        [
            pl.BlockSpec((count, tall, lanes), lambda i, p: (0, i ^ p[0], 0)),
            pl.BlockSpec((tall, side), lambda i, p: (0, i ^ p[0])),
        ],
        deps=deps,
    )


CORE, ROW, NEAR, FAR = range(4)


def swap_tensor(values):
    count = lax.axis_size("tensor")
    return lax.ppermute(values, "tensor", [(i, (i + 1) % count) for i in range(count)])


def swap(values, bit):
    count = lax.axis_size("dp")
    return lax.ppermute(values, "dp", [(i, i ^ (1 << bit)) for i in range(count)])


def dp_bits():
    return lax.axis_size("dp").bit_length() - 1


def after(values, *others):
    return lax.optimization_barrier((values, *others))[0]


def add(*parts):
    total = parts[0].astype(F32)
    for part in parts[1:]:
        total = total + part.astype(F32)
    return total.astype(BF)


def vector(ref):
    return ref[...].reshape(1, -1)


def average(values):
    return jnp.sum(values, axis=-1, keepdims=True) * (1.0 / values.shape[-1])


def normed(values):
    centered = values - average(values)
    inverse = lax.rsqrt(average(centered * centered) + 1e-05)
    return centered * inverse, inverse


def norm_back(upstream, scaled, inverse, gain):
    through = upstream * gain
    return inverse * (through - average(through) - scaled * average(through * scaled))


def column_sums(ref, parts):
    summed = [jnp.sum(part, axis=0, keepdims=True) for part in parts]
    summed.append(jnp.zeros((ref.shape[0] - len(parts), ref.shape[1]), F32))
    summed = jnp.concatenate(summed, axis=0)

    @pl.when(pl.program_id(0) == 0)
    def _():
        ref[...] = summed

    @pl.when(pl.program_id(0) > 0)
    def _():
        ref[...] += summed


def kept_column(place, groups):
    row = lax.broadcasted_iota(jnp.int32, (SHORT, 1), 0)
    first = 13 + pl.program_id(0) * groups
    return jnp.concatenate([(row < place[first + g]).astype(F32) for g in range(groups)], axis=0) > 0.5


def qkv_kernel(place, x_ref, weight_ref, bias_ref, out_ref):
    which, local = pl.program_id(0), weight_ref.shape[2]
    factor = jnp.where(which == 0, 1.0 / math.sqrt(HEAD), 1.0)
    value_bias = jnp.where(which == 2, bias_ref[:, local : 2 * local], 0.0)
    bias = jnp.where(which == 0, bias_ref[:, :local], value_bias)
    out_ref[...] = ((dot_nn(x_ref[...], weight_ref[0]) + bias) * factor).astype(BF)


def project_qkv(place, tokens, rows, weight, bias):
    count, width, local = weight.shape
    return call(
        qkv_kernel,
        "project_qkv",
        place,
        (count,),
        (tokens, weight, bias),
        [
            pl.BlockSpec((rows, width), lambda k, p: (p[3], 0)),
            pl.BlockSpec((1, width, local), lambda k, p: (k, 0, 0)),
            whole_block(bias.shape),
        ],
        [shaped((rows, count * local), BF)],
        [pl.BlockSpec((rows, local), lambda k, p: (0, k))],
        flops=2 * rows * width * count * local,
    )[0]


def first_norm_kernel(
    place, x_ref, c_own, c_oth, w_own, w_oth, bias, gain, shift, hidden_ref, low_ref, scaled_ref, inverse_ref
):
    attended = dot_nn(c_own[...], w_own[...]) + dot_nn(c_oth[...], w_oth[...])
    scaled, inverse = normed(x_ref[...].astype(F32) + attended + vector(bias))
    hidden = scaled * vector(gain) + vector(shift)
    hidden_ref[...] = hidden
    low_ref[...] = hidden.astype(BF)
    scaled_ref[...] = scaled.astype(BF)
    inverse_ref[...] = inverse


def first_norm(place, tokens, context, proj, vectors):
    rows, local = context[0].shape
    width = tokens.shape[1]
    steps = 4
    size = rows // steps
    tile = pl.BlockSpec((size, width), lambda i, p: (i, 0))
    part = pl.BlockSpec((size, local), lambda i, p: (i, 0))
    return call(
        first_norm_kernel,
        "first_norm",
        place,
        (steps,),
        (tokens, *context, *proj, *vectors),
        [
            pl.BlockSpec((size, width), lambda i, p: (steps * p[3] + i, 0)),
            part,
            part,
            whole_block((local, width)),
            whole_block((local, width)),
            *[whole_block((width,))] * 3,
        ],
        [
            shaped((rows, width), F32),
            shaped((rows, width), BF),
            shaped((rows, width), BF),
            shaped((rows, 1), F32),
        ],
        [tile, tile, tile, pl.BlockSpec((size, 1), lambda i, p: (i, 0))],
        flops=4 * rows * width * local,
        moved=14 * rows * width,
    )


def second_norm_kernel(
    place, acc_ref, x_ref, up_ref, bias, gain_ref, shift, result_ref, grad_ref, low_ref, sum_ref
):
    keep = kept_column(place, acc_ref.shape[0] // SHORT)
    gain = vector(gain_ref)
    scaled, inverse = normed(acc_ref[...] + vector(bias))
    result = scaled * gain + vector(shift)
    result_ref[...] = jnp.where(keep, result, x_ref[...].astype(F32)).astype(BF)
    upstream = jnp.where(keep, up_ref[...].astype(F32), 0.0)
    grad = norm_back(upstream, scaled, inverse, gain)
    grad_ref[...] = grad
    low_ref[...] = grad.astype(BF)
    column_sums(sum_ref, (grad, upstream * scaled, upstream))


def second_norm(place, acc, tokens, cotangent, vectors):
    rows, width = acc.shape
    steps = 4
    size = rows // steps
    tile = pl.BlockSpec((size, width), lambda i, p: (i, 0))
    far = pl.BlockSpec((size, width), lambda i, p: (steps * p[3] + i, 0))
    return call(
        second_norm_kernel,
        "second_norm",
        place,
        (steps,),
        (acc, tokens, cotangent, *vectors),
        [tile, far, far, *[whole_block((width,))] * 3],
        [shaped((rows, width), BF), shaped((rows, width), F32), shaped((rows, width), BF), shaped((8, width), F32)],
        [tile, tile, tile, whole_block((8, width))],
        moved=16 * rows * width,
    )


def first_back_kernel(
    place, grad_in, scaled_ref, inverse_ref, up_ref, w_own, w_oth, gain, base_ref, low_ref, c_own, c_oth, sum_ref
):
    keep = kept_column(place, grad_in.shape[0] // SHORT)
    upstream, scaled = grad_in[...], scaled_ref[...].astype(F32)
    grad = norm_back(upstream, scaled, inverse_ref[...], vector(gain))
    low = grad.astype(BF)
    base_ref[...] = grad + jnp.where(keep, 0.0, up_ref[...].astype(F32))
    low_ref[...] = low
    c_own[...] = dot_nt(low, w_own[...]).astype(BF)
    c_oth[...] = dot_nt(low, w_oth[...]).astype(BF)
    column_sums(sum_ref, (grad, upstream * scaled, upstream))


def first_back(place, grad, scaled, inverse, cotangent, proj, gain, deps=()):
    rows, width = grad.shape
    local = proj[0].shape[0]
    steps = 4
    size = rows // steps
    tile = pl.BlockSpec((size, width), lambda i, p: (i, 0))
    part = pl.BlockSpec((size, local), lambda i, p: (i, 0))
    return call(
        first_back_kernel,
        "first_back",
        place,
        (steps,),
        (grad, scaled, inverse, cotangent, *proj, gain),
        [
            tile,
            tile,
            pl.BlockSpec((size, 1), lambda i, p: (i, 0)),
            pl.BlockSpec((size, width), lambda i, p: (steps * p[3] + i, 0)),
            whole_block((local, width)),
            whole_block((local, width)),
            whole_block((width,)),
        ],
        [
            shaped((rows, width), F32),
            shaped((rows, width), BF),
            shaped((rows, local), BF),
            shaped((rows, local), BF),
            shaped((8, width), F32),
        ],
        [tile, tile, part, part, whole_block((8, width))],
        flops=4 * rows * width * local,
        moved=18 * rows * width,
        deps=deps,
    )


def input_grad_kernel(place, base_ref, g_own, g_oth, w_own, w_oth, out_ref):
    count, _, local = w_own.shape
    total = base_ref[...]
    for grads, weight in ((g_own, w_own), (g_oth, w_oth)):
        for k in range(count):
            total = total + dot_nt(grads[:, k * local : (k + 1) * local], weight[k])
    out_ref[...] = total.astype(BF)


def input_grad(place, base, grads, weights, deps=()):
    rows, width = base.shape
    wide = grads[0].shape[1]
    steps = 2
    size = rows // steps
    tile = pl.BlockSpec((size, width), lambda i, p: (i, 0))
    part = pl.BlockSpec((size, wide), lambda i, p: (i, 0))
    return call(
        input_grad_kernel,
        "input_grad",
        place,
        (steps,),
        (base, *grads, *weights),
        [tile, part, part, whole_block(weights[0].shape), whole_block(weights[0].shape)],
        [shaped((rows, width), BF)],
        [tile],
        flops=4 * rows * width * wide,
        deps=deps,
    )[0]


def body(
    tokens,
    qkv_weight,
    qv_bias,
    proj_weight,
    proj_bias,
    first_gain,
    first_shift,
    up_weight,
    up_bias,
    down_weight,
    down_bias,
    second_gain,
    second_shift,
    cotangent,
    bucket,
    lengths,
    dropped,
):
    token_count, width = tokens.shape
    rows = token_count // lax.axis_size("tensor")
    side = lax.axis_index("tensor")
    index = lax.axis_index("dp")
    core, row, near, far = [(index >> bit) & 1 for bit in range(4)]
    local = qkv_weight.shape[2]
    hidden_count = up_weight.shape[1]

    groups = rows // SHORT
    is_short = bucket[0] == 1
    first_slot = jnp.where(is_short, side * groups, side * (rows // LONG))
    slot_lengths = lax.dynamic_slice_in_dim(lengths, first_slot, groups, 0)
    slot_drops = lax.dynamic_slice_in_dim(dropped, first_slot, groups, 0)
    limits = jnp.where(slot_drops == 0, slot_lengths, 0)
    per = LONG // SHORT
    long_limits = jnp.repeat(limits[: groups // per], per) - SHORT * (jnp.arange(groups) % per)
    limits = jnp.where(is_short, limits, long_limits)
    place = jnp.concatenate(
        [
            jnp.stack([core, row, 4 * row + 2 * near + far, side, bucket[0]]),
            slot_lengths,
            limits,
        ]
    ).astype(jnp.int32)
    qkv_own = jnp.transpose(qkv_weight, (1, 0, 2))
    attn_piece, ffn_one, ffn_two = pack(place, qkv_own, proj_weight, up_weight, down_weight)
    biases = jnp.concatenate([qv_bias.reshape(1, -1), up_bias.reshape(1, -1)], axis=1)
    attn_x = swap_tensor(attn_piece)
    qkv = [project_qkv(place, tokens, rows, qkv_own, biases)]
    c_own, lse_own = attend(place, qkv[0])
    attn_x = after(attn_x, c_own)
    attn_y = swap(attn_x, ROW)
    ffn_x = [swap_tensor(after(ffn_one, c_own))]
    biases_oth = swap_tensor(after(biases, c_own))
    ffn_x.append(swap_tensor(after(ffn_two, attn_x)))
    attn_core = swap(attn_x, CORE)
    ffn_x[0] = after(ffn_x[0], attn_y)
    ffn_y = [swap(ffn_x[0], ROW)]
    qkv_oth, proj_oth = join_attn(place, [attn_x, attn_y, attn_core, swap(attn_y, CORE)], local)
    qkv_w, proj_w = (qkv_own, qkv_oth), (proj_weight, proj_oth)
    qkv.append(project_qkv(place, tokens, rows, qkv_oth, biases_oth))
    c_oth, lse_oth = attend(place, qkv[1])
    ffn_x[1] = after(ffn_x[1], c_oth)
    context, lse = (c_own, c_oth), (lse_own, lse_oth)
    ffn_y[0] = after(ffn_y[0], c_oth)
    ffn_y.append(swap(ffn_x[1], ROW))
    ffn_core = [swap(after(v, c_oth), CORE) for v in ffn_x]
    hidden, hidden_low, scaled, inverse = first_norm(
        place, tokens, context, proj_w, (proj_bias, first_gain, first_shift)
    )
    act_own, slope_own, acc = ffn_forward(place, hidden_low, up_weight, biases, down_weight, hidden)
    ffn_y[1] = after(ffn_y[1], act_own)
    first, second = [
        [ffn_x[k], ffn_y[k], ffn_core[k], swap(ffn_y[k], CORE)] for k in range(2)
    ]
    up_oth, down_oth = join_ffn(place, first, second)
    act_oth, slope_oth, acc = ffn_forward(place, hidden_low, up_oth, biases_oth, down_oth, acc)
    result_own, grad_second, branch_grad, sums_two = second_norm(
        place, acc, tokens, cotangent, (down_bias, second_gain, second_shift)
    )

    def part(pair, half, low, high, first, last):
        at = (slice(low, high), slice(first, last))
        return (pair[half], at) if isinstance(pair, tuple) else (pair, (half, *at))

    def first_left(near, got, size, wide):
        pieces = [part(p, 1, 0, size, 0, wide) for p in (near, got)]
        return ((size, wide), [((slice(None), slice(None)), pieces)])

    def first_right(near, got, size, wide):
        return (
            (size // 2, 2 * wide),
            [
                (
                    (slice(None), slice(h * wide, (h + 1) * wide)),
                    [part(p, h, size // 2, size, wide, 2 * wide) for p in (near, got)],
                )
                for h in range(2)
            ],
        )

    def second_left(near, got, left, size, wide):
        return [
            (
                (size // 2, wide),
                [
                    (
                        (slice(None), slice(None)),
                        [part(p, 0, low, low + size // 2, 0, wide) for p in (near, got)]
                        + [(left, (slice(low, low + size // 2), slice(None)))],
                    )
                ],
            )
            for low in (0, size // 2)
        ]

    def second_right(near, got, right, size, wide):
        return [
            (
                (size // 2, wide),
                [
                    (
                        (slice(None), slice(None)),
                        [part(p, h, 0, size // 2, wide, 2 * wide) for p in (near, got)]
                        + [(right, (slice(None), slice(h * wide, (h + 1) * wide)))],
                    )
                ],
            )
            for h in range(2)
        ]

    def third(keeps, received):
        size, wide = keeps[0].shape
        return [
            (
                (size // 2, 2 * wide),
                [
                    (
                        (slice(None), slice(k * wide, (k + 1) * wide)),
                        [(a, (slice(low, low + size // 2), slice(None))) for a in (keeps[k], received[k])],
                    )
                    for k in range(2)
                ],
            )
            for low in (0, size // 2)
        ]

    def fourth(keep, received):
        size, wide = keep.shape
        return [
            (
                (size // 2, wide),
                [((slice(None), slice(None)), [(a, (slice(low, low + size // 2), slice(None))) for a in (keep, received)])],
            )
            for low in (0, size // 2)
        ]

    everything = (slice(None), slice(None))

    def plain(*arrays):
        return (arrays[0].shape, [(everything, [(a, everything) for a in arrays])])

    def grown(piece, other):
        size, wide = piece.shape
        return (
            (2 * size, wide),
            [
                ((slice(k * size, (k + 1) * size), slice(None)), [(a, everything)])
                for k, a in enumerate((piece, other))
            ],
        )

    def last_bits(values):
        for bit in range(4, dp_bits()):
            values = add(values, swap(values, bit))
        return values

    size, half = width, width // 2
    down_far, down_near = ffn_grad("down_grad", place, (act_own, act_oth), branch_grad, "left")
    down_got = swap(down_far, CORE)
    pre_own, acc, up_sums_own = ffn_backward(
        place, branch_grad, slope_own, up_weight, down_weight, grad_second, deps=[down_near], weight=1
    )
    left, right = sums(
        "sums_1",
        place,
        [first_left(down_near, down_got, size, half), first_right(down_near, down_got, size, half)],
        deps=[pre_own],
    )
    down_left, down_right = swap_tensor(left), swap(right, ROW)
    pre_oth, grad_hidden, up_sums_oth = ffn_backward(
        place, branch_grad, slope_oth, up_oth, down_oth, acc, deps=[left]
    )
    up_far, up_near = ffn_grad("up_grad", place, (pre_own, pre_oth), hidden_low, "right")
    up_got = swap(up_far, CORE)
    down_keep = [None, None]
    down_keep[0], left, down_keep[1], right = sums(
        "sums_2",
        place,
        [
            *second_left(down_near, down_got, down_left, size, half),
            *second_right(down_near, down_got, down_right, size, half),
        ],
        deps=[up_near],
    )
    down_left, down_right = swap(left, ROW), swap_tensor(right)
    base, out_grad, gc_own, gc_oth, sums_one = first_back(
        place, grad_hidden, scaled, inverse, cotangent, proj_w, first_gain, deps=[left]
    )
    down_keep, down_send, left, right = sums(
        "sums_3",
        place,
        [
            *third(down_keep, (down_left, down_right)),
            first_left(up_near, up_got, size, half),
            first_right(up_near, up_got, size, half),
        ],
        deps=[out_grad],
    )
    down_z = swap(down_send, NEAR)
    up_left, up_right = swap_tensor(left), swap(right, ROW)
    grads_oth, attn_sums_oth = attend_back(place, qkv[1], gc_oth, lse[1], deps=[down_send])
    down_keep, down_send = sums("sums_4", place, fourth(down_keep, down_z), deps=[grads_oth])
    down_f = swap(down_send, FAR)
    far_oth, near_oth = attn_grad(
        place, tokens, grads_oth, context[1], out_grad, deps=[down_send], weight=1
    )
    got_oth = swap(far_oth, CORE)
    up_keep = [None, None]
    up_keep[0], left, up_keep[1], right, down_sum = sums(
        "sums_5",
        place,
        [
            *second_left(up_near, up_got, up_left, size, half),
            *second_right(up_near, up_got, up_right, size, half),
            plain(down_keep, down_f),
        ],
        deps=[far_oth],
    )
    down_sum = last_bits(down_sum)
    up_left, up_right = swap(left, ROW), swap_tensor(right)
    down_a = swap(down_sum, FAR)
    grads_own, attn_sums_own = attend_back(place, qkv[0], gc_own, lse[0], deps=[down_sum])
    tall, wide = near_oth.shape
    up_keep, up_send, down_sum, left, right = sums(
        "sums_6",
        place,
        [
            *third(up_keep, (up_left, up_right)),
            grown(down_sum, down_a),
            *[
                (
                    (tall, wide // 2),
                    [(everything, [(a, (slice(None), lanes)) for a in (near_oth, got_oth)])],
                )
                for lanes in (slice(0, wide // 2), slice(wide // 2, wide))
            ],
        ],
        deps=[grads_own],
    )
    up_z = swap(up_send, NEAR)
    down_b = swap(down_sum, NEAR)
    attn_x = [swap_tensor(left), swap_tensor(right)]
    far_own, near_own = attn_grad(place, tokens, grads_own, context[0], out_grad, deps=[up_send])
    got_own = swap(far_own, CORE)
    small_own, small_oth = small_sums(
        place,
        sums_one,
        sums_two,
        (attn_sums_own, attn_sums_oth),
        (up_sums_own, up_sums_oth),
        deps=[far_own],
    )
    small_x = swap_tensor(small_oth)
    up_keep, up_send, down_sum = sums(
        "sums_7", place, [*fourth(up_keep, up_z), grown(down_sum, down_b)], deps=[small_own, attn_x[0]]
    )
    up_f = swap(up_send, FAR)
    down_y = swap(down_sum, ROW)
    input_own = input_grad(place, base, (grads_own, grads_oth), qkv_w, deps=[up_send])
    part_rows, half_wide = tall // 4, wide // 2

    def lane_sums(k, *blocks):
        lanes = slice(k * half_wide, (k + 1) * half_wide)
        return (
            (len(blocks) * part_rows, half_wide),
            [
                (
                    (slice(n * part_rows, (n + 1) * part_rows), slice(None)),
                    [
                        (near_own, (slice(b * part_rows, (b + 1) * part_rows), lanes)),
                        (got_own, (slice(b * part_rows, (b + 1) * part_rows), lanes)),
                        (attn_x[k], (slice(b * part_rows, (b + 1) * part_rows), slice(None))),
                    ],
                )
                for n, b in enumerate(blocks)
            ],
        )

    left_keep, left_send, right_keep, right_send, up_sum, small = sums(
        "sums_8",
        place,
        [
            lane_sums(0, 0, 1),
            lane_sums(0, 2, 3),
            lane_sums(1, 0, 2),
            lane_sums(1, 1, 3),
            plain(up_keep, up_f),
            plain(small_own, small_x),
        ],
        deps=[input_own, down_y],
    )
    up_sum = last_bits(up_sum)
    left_got, right_got = swap(left_send, ROW), swap(right_send, NEAR)
    input_x = swap_tensor(after(input_own, small))
    up_a, small_r = swap(up_sum, FAR), swap(small, CORE)
    left_keep, left_send, right_keep, right_send, small, up_sum = sums(
        "sums_10",
        place,
        [
            *fourth(left_keep, left_got),
            *fourth(right_keep, right_got),
            plain(small, small_r),
            grown(up_sum, up_a),
        ],
    )
    left_got, right_got = swap(left_send, NEAR), swap(right_send, ROW)
    small_r, up_b = swap(small, ROW), swap(up_sum, NEAR)
    attn_keep, attn_send, small, up_sum = sums(
        "sums_11",
        place,
        [
            *third((left_keep, right_keep), (left_got, right_got)),
            plain(small, small_r),
            grown(up_sum, up_b),
        ],
    )
    attn_f, small_r, up_y = swap(attn_send, FAR), swap(small, NEAR), swap(up_sum, ROW)
    attn_sum, small = sums("sums_12", place, [plain(attn_keep, attn_f), plain(small, small_r)])
    small_r = swap(small, FAR)
    attn_sum = last_bits(attn_sum)
    attn_a = swap(attn_sum, FAR)
    result_x = swap_tensor(after(result_own, attn_sum, input_x))
    tokens_grad = both_rows("grad_rows", place, input_own, input_x, F32, deps=[attn_sum])

    def lane_rows(k):
        size = attn_sum.shape[0]
        lanes = slice(k * half_wide, (k + 1) * half_wide)
        return (
            (2 * size, half_wide),
            [
                ((slice(n * size, (n + 1) * size), slice(None)), [(a, (slice(None), lanes))])
                for n, a in enumerate((attn_sum, attn_a))
            ],
        )

    left, right = sums("sums_13", place, [lane_rows(0), lane_rows(1)], deps=[tokens_grad, up_y])
    left_got, right_got = swap(left, NEAR), swap(right, ROW)
    down_core, down_last = [swap(after(v, attn_sum), CORE) for v in (down_sum, down_y)]
    down_total = tile_out("down_out", place, [down_sum, down_y, down_core, down_last], False, deps=[left])
    left, right, small = sums(
        "sums_14",
        place,
        [grown(left, left_got), grown(right, right_got), plain(small, small_r)],
        deps=[down_total],
    )
    for bit in range(4, dp_bits()):
        small = small + swap(small, bit)
    left_high, right_high = swap(left, ROW), swap(right, NEAR)
    attn_core = [swap(left, CORE), swap(right, CORE)]
    up_core, up_last = [swap(after(v, left), CORE) for v in (up_sum, up_y)]
    up_total = tile_out("up_out", place, [up_sum, up_y, up_core, up_last], True, deps=[left])
    left_high, right_high = after((left_high, right_high), up_total)
    attn_last = [swap(left_high, CORE), swap(right_high, CORE)]
    qkv_total, proj_total = attn_out(
        place,
        [left, left_high, right, right_high, attn_core[0], attn_last[0], attn_core[1], attn_last[1]],
        3,
        local,
        deps=[up_total],
    )
    result = both_rows("result_rows", place, result_own, result_x, BF, deps=[proj_total])
    bias_total = small[6:9].reshape(-1)
    return (
        result,
        tokens_grad,
        jnp.transpose(qkv_total, (1, 0, 2)),
        bias_total[: 2 * local].reshape(2, local),
        proj_total,
        small[0],
        small[1],
        small[2],
        up_total,
        bias_total[2 * local :],
        down_total,
        small[3],
        small[4],
        small[5],
    )


def solution(mesh):
    rows, columns, whole = P("dp", None), P(None, "tensor"), P()
    return jax.shard_map(
        body,
        mesh=mesh,
        in_specs=(
            rows,
            P(None, None, "tensor"),
            columns,
            P("tensor", None),
            whole,
            whole,
            whole,
            columns,
            P("tensor"),
            P("tensor", None),
            whole,
            whole,
            whole,
            rows,
            P("dp"),
            P("dp"),
            P("dp"),
        ),
        out_specs=(
            rows,
            rows,
            P(None, None, "tensor"),
            columns,
            P("tensor", None),
            whole,
            whole,
            whole,
            columns,
            P("tensor"),
            P("tensor", None),
            whole,
            whole,
            whole,
        ),
        check_vma=False,
    )
```
